32 devices in a mesh: dp: 8 (over y, x, core), group: 4 (over z).
Axes of the slice: x: 2, y: 2, z: 4, core: 2. Of those that a mesh axis runs over, the one named last changes fastest.
Arguments:
- inputs: float32 [4096, 768], P(('dp', 'group')), may hold values from -6 to 6
- cotangent: float32 [4096, 768], P(('dp', 'group')), may hold values from -6 to 6
- lengths: int32 [32, 4], P(('dp', 'group')), may hold values from 1 to 64, 128 in all within a row
- attn_weights: float32 [4, 768, 768], P('group', 'dp'), may hold values from -1 to 1
- attn_momenta: float32 [4, 768, 768], P('group', 'dp'), may hold values from -1 to 1
- ffn_weights: float32 [2, 768, 3072], P(None, 'dp', 'group'), may hold values from -1 to 1
- ffn_momenta: float32 [2, 768, 3072], P(None, 'dp', 'group'), may hold values from -1 to 1
- vectors: float32 [12, 768], replicated, may hold values from -2 to 2
- vector_momenta: float32 [12, 768], replicated, may hold values from -1 to 1
Outputs:
- outputs: float32 [4096, 768], P(('dp', 'group'))
- input_grad: float32 [4096, 768], P(('dp', 'group'))
- attn_grads: float32 [4, 768, 768], P('group', 'dp')
- ffn_grads: float32 [2, 768, 3072], P(None, 'dp', 'group')
- vector_grads: float32 [12, 768], replicated
- new_attn_weights: float32 [4, 768, 768], P('group', 'dp')
- new_attn_momenta: float32 [4, 768, 768], P('group', 'dp')
- new_ffn_weights: float32 [2, 768, 3072], P(None, 'dp', 'group')
- new_ffn_momenta: float32 [2, 768, 3072], P(None, 'dp', 'group')
- new_vectors: float32 [12, 768], replicated
- new_vector_momenta: float32 [12, 768], replicated
The draws below stay inside these ranges and needn't reach their ends.
Inputs may be any that keep to these rules, and one draw needn't show every extreme that they name: Each device's 4 lengths sum to 128.
All inputs are finite; a program needn't handle non-finite values.
Results may differ from the reference program's by a relative error of at most 0.025.
The reference program's roundings to bfloat16 on the way count: a program that leaves them out, or rounds other values in their place, can miss the bound.
Values may be sent and summed in bfloat16 or wider, within the bound.
A program may use at most 128 MiB of HBM per device.

```python
import math
import jax
import jax.numpy as jnp
import numpy as np
from jax import lax

D = 768
HEADS = 12
FF = 3072
TOK_DEV = 128
SEQ_DEV = 4
MOST = 64
NS_ITERS = 3
TOKENS = 4096
N_DP = 8
N_GROUP = 4


def rising_scale(key, count):
    place = jnp.arange(count, dtype=jnp.float32) / float(max(count - 1, 1))
    ramp = jnp.exp(math.log(3.0) * (place - 0.5))
    jitter = jnp.exp(jax.random.uniform(key, (count,), jnp.float32, -0.6, 0.6))
    return ramp * jitter


def draw_attn_weights(key, part):
    scales = jnp.array([1.0, 1.0, 1.0, 4.0], jnp.float32) * D ** (-0.5)
    first = jax.random.normal(jax.random.fold_in(key, 11), (4, D, D), jnp.float32)
    values = first * scales[:, None, None]
    return jnp.clip(values, -1.0, 1.0)


def draw_attn_momenta(key, part):
    scales = jnp.array([0.5, 0.5, 1.0, 0.5], jnp.float32) / math.sqrt(TOKENS)
    rows = rising_scale(jax.random.fold_in(key, 23), D)
    values = jax.random.normal(jax.random.fold_in(key, 21), (4, D, D), jnp.float32)
    return jnp.clip(values * scales[:, None, None] * rows[None, :, None], -1.0, 1.0)


def draw_ffn_weights(key, part):
    scales = jnp.array([D ** (-0.5), 1.5 * FF ** (-0.5)], jnp.float32)
    values = jax.random.normal(jax.random.fold_in(key, 51), (2, D, FF), jnp.float32)
    return jnp.clip(values * scales[:, None, None], -1.0, 1.0)


def draw_ffn_momenta(key, part):
    scales = jnp.array([0.4, 0.8], jnp.float32) / math.sqrt(TOKENS)
    rows = rising_scale(jax.random.fold_in(key, 63), D)
    columns = rising_scale(jax.random.fold_in(key, 64), FF)
    values = jax.random.normal(jax.random.fold_in(key, 61), (2, D, FF), jnp.float32)
    values = values * scales[:, None, None] * rows[None, :, None] * columns[None, None, :]
    return jnp.clip(values, -1.0, 1.0)


def draw_vectors(key, part):
    count = 8 + FF // D
    row_index = jnp.arange(count, dtype=jnp.int32)
    is_gain = (row_index == 0) | (row_index == 5)
    offset = jnp.where(is_gain, 1.0, 0.0).astype(jnp.float32)
    spread = jnp.where(is_gain, 0.3, 0.5).astype(jnp.float32)
    base = jax.random.normal(jax.random.fold_in(key, 31), (count, D), jnp.float32)
    return jnp.clip(offset[:, None] + spread[:, None] * base, -2.0, 2.0)


def draw_vector_momenta(key, part):
    count = 8 + FF // D
    scale = 1.0 / math.sqrt(TOKENS)
    values = jax.random.normal(jax.random.fold_in(key, 41), (count, D), jnp.float32) * scale
    return jnp.clip(values, -1.0, 1.0)


def block_scale(rng, shape, split, low, largest):
    def one(dim, shards_of):
        steps = jax.random.uniform(jax.random.fold_in(jax.random.fold_in(rng, 6), dim), (shards_of,), jnp.float32, low / len(split), largest / len(split))
        return jnp.repeat(jnp.exp(steps), shape[dim] // shards_of).reshape((-1,) + (1,) * (len(shape) - dim - 1))

    loudness = one(*split[0])
    for cut in split[1:]:
        loudness = loudness * one(*cut)
    return loudness


def split_up(amount, total, limit, skew):
    portions = [(1 << 20) // math.isqrt(rank ** skew) + 1 for rank in range(2, amount + 1)]
    spare, counts = total - limit - (amount - 1), [1] * (amount - 1)
    while spare > 0:
        candidates = [i for i in range(amount - 1) if counts[i] < limit]
        whole, left = sum([portions[i] for i in candidates]), spare
        for i in candidates:
            extra = min(limit - counts[i], max(1, left * portions[i] // whole), spare)
            counts[i] = counts[i] + extra
            spare = spare - extra
    return np.array([limit] + counts)


def uneven(rng, count, total, limit, skew):
    if count == 2:
        one = jax.random.randint(rng, (), max(1, total - limit), min(limit, total - 1) + 1)
        return jnp.stack([one, total - one])
    tallies = jnp.asarray(split_up(count, total, limit, skew), jnp.int32)
    couples = (count - 1) // 2
    giver, receiver = tallies[1:1 + 2 * couples:2], tallies[2:2 + 2 * couples:2]
    margin = jnp.minimum(giver - 1, limit - receiver)
    passed = jax.random.randint(jax.random.fold_in(rng, 1), (couples,), 0, 1 << 20) % (margin + 1)
    tallies = tallies.at[1:1 + 2 * couples:2].set(giver - passed).at[2:2 + 2 * couples:2].set(receiver + passed)
    return tallies[jax.random.permutation(jax.random.fold_in(rng, 2), count)]


def gaussian(own_key, shape, scale, reach, shards=(), held_as=jnp.bfloat16):
    gain = block_scale(own_key, shape, shards, -0.22, 0.18) if shards else 1.0
    values = jax.random.normal(own_key, shape, jnp.float32) * scale * gain
    return jnp.minimum(jnp.maximum(values, -reach), reach).astype(held_as)


def setup_inputs(seed: int = 0) -> dict:
    key_list = jax.random.split(jax.random.key(seed), 10)
    inputs = gaussian(key_list[0], (TOKENS, D), 1.0, 6.0, ((0, 32),), jnp.float32)
    cotangent = gaussian(key_list[1], (TOKENS, D), 1.0, 6.0, ((0, 32),), jnp.float32)
    lengths = jax.vmap(lambda own: uneven(own, SEQ_DEV, TOK_DEV, MOST, 2))(jax.random.split(key_list[2], (N_DP * N_GROUP))).reshape((N_DP * N_GROUP, SEQ_DEV)).astype(jnp.int32)
    attn_weights = draw_attn_weights(jax.random.fold_in(key_list[9], 71), 0)
    attn_momenta = draw_attn_momenta(jax.random.fold_in(key_list[9], 71), 0)
    ffn_weights = draw_ffn_weights(jax.random.fold_in(key_list[9], 71), 0)
    ffn_momenta = draw_ffn_momenta(jax.random.fold_in(key_list[9], 71), 0)
    vectors = draw_vectors(jax.random.fold_in(key_list[9], 71), 0)
    vector_momenta = draw_vector_momenta(jax.random.fold_in(key_list[9], 71), 0)
    return {"inputs": inputs, "cotangent": cotangent, "lengths": lengths, "attn_weights": attn_weights, "attn_momenta": attn_momenta, "ffn_weights": ffn_weights, "ffn_momenta": ffn_momenta, "vectors": vectors, "vector_momenta": vector_momenta}


coef_first = 3.4445
coef_second = -4.775
coef_third = 2.0315
momentum_rate = 0.9
muon_rate = 0.8
vector_rate = 0.1

def norm_forward(rows):
    centre = lax.optimization_barrier(jnp.mean(rows, axis=1, keepdims=True))
    centred = rows - centre
    variance = lax.optimization_barrier(jnp.mean(centred * centred, axis=1, keepdims=True))
    inverse = lax.rsqrt(variance + 1e-05)
    return (centred * inverse, inverse)

def norm_backward(grad_normed, normed, inverse):
    return inverse * (grad_normed - lax.optimization_barrier(jnp.mean(grad_normed, axis=1, keepdims=True)) - normed * lax.optimization_barrier(jnp.mean(grad_normed * normed, axis=1, keepdims=True)))

def masked_scores(query_heads, key_heads, allowed):
    scores = jnp.einsum('qhd,khd->hqk', query_heads.astype(jnp.float32), key_heads.astype(jnp.float32))
    return jnp.where(allowed[None], scores, -jnp.inf)

def layer_block(block_rows, block_cotan, seq_lengths, attn_w, ffn_w, vectors):
    token_count = block_rows.shape[0]
    width = block_rows.shape[1]
    head_size = width // HEADS
    scale = 1.0 / math.sqrt(head_size)
    w_query, w_key, w_value, w_output = (attn_w[0], attn_w[1], attn_w[2], attn_w[3])
    w_expand, w_reduce = (ffn_w[0], ffn_w[1])
    expand_bias = vectors[8:].reshape(-1)
    positions = jnp.arange(token_count, dtype=jnp.int32)
    seq_ends = jnp.cumsum(seq_lengths.astype(jnp.int32)).astype(jnp.int32)
    segment = lax.optimization_barrier(jnp.sum((positions[:, None] >= seq_ends[None, :]).astype(jnp.int32), axis=1))
    allowed = (segment[:, None] == segment[None, :]) & (positions[None, :] <= positions[:, None])
    normed_first, inverse_first = norm_forward(block_rows)
    hidden_first = (normed_first * vectors[0] + vectors[1]).astype(jnp.bfloat16)
    query = ((jnp.dot(hidden_first, w_query, preferred_element_type=jnp.float32) + vectors[2]) * scale).astype(jnp.bfloat16)
    keyed = jnp.dot(hidden_first, w_key, preferred_element_type=jnp.float32).astype(jnp.bfloat16)
    valued = (jnp.dot(hidden_first, w_value, preferred_element_type=jnp.float32) + vectors[3]).astype(jnp.bfloat16)
    query_heads = query.reshape(token_count, HEADS, head_size)
    key_heads = keyed.reshape(token_count, HEADS, head_size)
    value_heads = valued.reshape(token_count, HEADS, head_size)
    scores = masked_scores(query_heads, key_heads, allowed)
    highest = lax.optimization_barrier(jnp.max(scores, axis=2, keepdims=True))
    log_total = highest + jnp.log(lax.optimization_barrier(jnp.sum(jnp.exp(scores - highest), axis=2, keepdims=True)))
    probs_first = jnp.exp(scores - log_total).astype(jnp.bfloat16)
    attended = jnp.einsum('hqk,khd->qhd', probs_first.astype(jnp.float32), value_heads.astype(jnp.float32))
    attended = attended.reshape(token_count, width).astype(jnp.bfloat16)
    middle = block_rows + jnp.dot(attended, w_output, preferred_element_type=jnp.float32) + vectors[4]
    normed_second, inverse_second = norm_forward(middle)
    hidden_second = (normed_second * vectors[5] + vectors[6]).astype(jnp.bfloat16)
    before = jnp.dot(hidden_second, w_expand, preferred_element_type=jnp.float32) + expand_bias
    active = jnp.maximum(before, 0.0).astype(jnp.bfloat16)
    outputs = middle + jnp.dot(active, w_reduce.T, preferred_element_type=jnp.float32) + vectors[7]
    cotan_b = block_cotan.astype(jnp.bfloat16)
    grad_reduce = jnp.dot(cotan_b.T, active, preferred_element_type=jnp.float32)
    grad_active = jnp.dot(cotan_b, w_reduce, preferred_element_type=jnp.float32)
    grad_before = jnp.where(before > 0.0, grad_active, 0.0)
    before_grad_b = grad_before.astype(jnp.bfloat16)
    grad_expand = jnp.dot(hidden_second.T, before_grad_b, preferred_element_type=jnp.float32)
    grad_second = jnp.dot(before_grad_b, w_expand.T, preferred_element_type=jnp.float32)
    grad_middle = block_cotan + norm_backward(grad_second * vectors[5], normed_second, inverse_second)
    middle_b = grad_middle.astype(jnp.bfloat16)
    grad_output_w = jnp.dot(attended.T, middle_b, preferred_element_type=jnp.float32)
    grad_attended = jnp.dot(middle_b, w_output.T, preferred_element_type=jnp.float32).astype(jnp.bfloat16)
    attended_heads = grad_attended.reshape(token_count, HEADS, head_size).astype(jnp.float32)
    probs = jnp.exp(masked_scores(query_heads, key_heads, allowed) - log_total)
    probs_b = probs.astype(jnp.bfloat16)
    grad_probs = jnp.einsum('qhd,khd->hqk', attended_heads, value_heads.astype(jnp.float32))
    grad_value = jnp.einsum('hqk,qhd->khd', probs_b.astype(jnp.float32), attended_heads)
    delta = lax.optimization_barrier(jnp.sum(probs * grad_probs, axis=2, keepdims=True))
    grad_scores = (probs * (grad_probs - delta)).astype(jnp.bfloat16).astype(jnp.float32)
    grad_query = jnp.einsum('hqk,khd->qhd', grad_scores, key_heads.astype(jnp.float32)) * scale
    grad_key = jnp.einsum('hqk,qhd->khd', grad_scores, query_heads.astype(jnp.float32))
    query_grad = grad_query.reshape(token_count, width)
    key_grad = grad_key.reshape(token_count, width)
    value_grad = grad_value.reshape(token_count, width)
    query_grad_b = query_grad.astype(jnp.bfloat16)
    key_grad_b = key_grad.astype(jnp.bfloat16)
    value_grad_b = value_grad.astype(jnp.bfloat16)
    grad_wq = jnp.dot(hidden_first.T, query_grad_b, preferred_element_type=jnp.float32)
    grad_wk = jnp.dot(hidden_first.T, key_grad_b, preferred_element_type=jnp.float32)
    grad_wv = jnp.dot(hidden_first.T, value_grad_b, preferred_element_type=jnp.float32)
    grad_first = jnp.dot(query_grad_b, w_query.T, preferred_element_type=jnp.float32)
    grad_first = grad_first + jnp.dot(key_grad_b, w_key.T, preferred_element_type=jnp.float32)
    grad_first = grad_first + jnp.dot(value_grad_b, w_value.T, preferred_element_type=jnp.float32)
    input_grad = grad_middle + norm_backward(grad_first * vectors[0], normed_first, inverse_first)
    attn_terms = jnp.stack([grad_wq, grad_wk, grad_wv, grad_output_w])
    ffn_terms = jnp.stack([grad_expand, grad_reduce])
    small_terms = jnp.stack([lax.optimization_barrier(jnp.sum(grad_first * normed_first, axis=0)), lax.optimization_barrier(jnp.sum(grad_first, axis=0)), lax.optimization_barrier(jnp.sum(query_grad, axis=0)), lax.optimization_barrier(jnp.sum(value_grad, axis=0)), lax.optimization_barrier(jnp.sum(grad_middle, axis=0)), lax.optimization_barrier(jnp.sum(grad_second * normed_second, axis=0)), lax.optimization_barrier(jnp.sum(grad_second, axis=0)), lax.optimization_barrier(jnp.sum(block_cotan, axis=0))])
    bias_terms = lax.optimization_barrier(jnp.sum(grad_before, axis=0)).reshape(-1, width)
    vector_terms = jnp.concatenate([small_terms, bias_terms], axis=0)
    return (outputs, input_grad, attn_terms, ffn_terms, vector_terms)

def orthogonalize(matrix):
    norm_value = jnp.sqrt(jnp.sum(matrix * matrix))
    iterate = matrix / (norm_value + 1e-07)
    for iteration in range(NS_ITERS):
        iterate_b = iterate.astype(jnp.bfloat16)
        gram = jnp.dot(iterate_b, iterate_b.T, preferred_element_type=jnp.float32)
        gram_b = gram.astype(jnp.bfloat16)
        mixed = coef_second * gram + coef_third * jnp.dot(gram_b, gram_b, preferred_element_type=jnp.float32)
        iterate = coef_first * iterate + jnp.dot(mixed.astype(jnp.bfloat16), iterate_b, preferred_element_type=jnp.float32)
    return iterate

def reference(inputs, cotangent, lengths, attn_weights, attn_momenta, ffn_weights, ffn_momenta, vectors, vector_momenta):
    width = inputs.shape[1]
    device_count = lengths.shape[0]
    attn_b = attn_weights.astype(jnp.bfloat16)
    ffn_b = ffn_weights.astype(jnp.bfloat16)

    def visit(carry, pieces):
        attn_sum, ffn_sum, vector_sum = carry
        block_rows, block_cotan, seq_lengths = pieces
        outputs, input_grad, attn_terms, ffn_terms, vector_terms = layer_block(block_rows, block_cotan, seq_lengths, attn_b, ffn_b, vectors)
        return ((attn_sum + attn_terms, ffn_sum + ffn_terms, vector_sum + vector_terms), (outputs, input_grad))
    start_carry = (jnp.zeros(attn_weights.shape, jnp.float32), jnp.zeros(ffn_weights.shape, jnp.float32), jnp.zeros(vectors.shape, jnp.float32))
    pieces = (inputs.reshape(device_count, TOK_DEV, width), cotangent.reshape(device_count, TOK_DEV, width), lengths)
    (attn_sum, ffn_sum, vector_sum), (outputs, input_grad) = lax.scan(visit, start_carry, pieces)
    outputs = outputs.reshape(device_count * TOK_DEV, width)
    input_grad = input_grad.reshape(device_count * TOK_DEV, width)
    attn_grads = attn_sum / float(TOKENS)
    ffn_grads = ffn_sum / float(TOKENS)
    vector_grads = vector_sum / float(TOKENS)
    new_attn_momenta = momentum_rate * attn_momenta + attn_grads
    new_ffn_momenta = momentum_rate * ffn_momenta + ffn_grads
    new_attn_weights = attn_weights - muon_rate * lax.map(orthogonalize, new_attn_momenta)
    new_ffn_weights = ffn_weights - muon_rate * lax.map(orthogonalize, new_ffn_momenta)
    new_vector_momenta = momentum_rate * vector_momenta + vector_grads
    spread = lax.rsqrt(lax.optimization_barrier(jnp.mean(new_vector_momenta * new_vector_momenta, axis=1, keepdims=True)) + 1e-06)
    new_vectors = vectors - vector_rate * new_vector_momenta * spread
    return (outputs, input_grad, attn_grads, ffn_grads, vector_grads, new_attn_weights, new_attn_momenta, new_ffn_weights, new_ffn_momenta, new_vectors, new_vector_momenta)
```

```python
import math

import jax
import jax.numpy as jnp
from jax import lax
from jax.experimental import pallas as pl
from jax.experimental.pallas import tpu as pltpu
from jax.sharding import PartitionSpec as P

HEADS = 12
NS_ITERS = 3


coef_first = 3.4445
coef_second = -4.775
coef_third = 2.0315
momentum_rate = 0.9
muon_rate = 0.8
vector_rate = 0.1


def norm_forward(rows):
    centre = jnp.mean(rows, axis=1, keepdims=True)
    centred = rows - centre
    variance = jnp.mean(centred * centred, axis=1, keepdims=True)
    inverse = lax.rsqrt(variance + 1e-05)
    return (centred * inverse, inverse)


def norm_backward(grad_normed, normed, inverse):
    return inverse * (
        grad_normed
        - jnp.mean(grad_normed, axis=1, keepdims=True)
        - normed * jnp.mean(grad_normed * normed, axis=1, keepdims=True)
    )


def masked_scores(query_heads, key_heads, allowed):
    scores = jnp.einsum("qhd,khd->hqk", query_heads, key_heads, preferred_element_type=jnp.float32)
    return jnp.where(allowed[None], scores, -jnp.inf)


MESH = pl.DeviceIdType.MESH


def flip(index, bits):
    result = index
    for bit in (1, 2, 4):
        if bits & bit:
            result = result + bit - 2 * bit * ((index // bit) % 2)
    return result


def out_struct(kind, x, n_group):
    dtype = x.dtype
    if kind == "zag":
        shape = (n_group,) + x.shape
    elif kind == "za2a":
        shape = x.shape
    elif kind == "dpag":
        shape = (8,) + x.shape
    elif kind == "dprow":
        shape = (x.shape[0], 8 * x.shape[1], x.shape[2])
    elif kind == "dpscatter":
        shape = (x.shape[0], x.shape[1] // 8, x.shape[2])
        dtype = jnp.float32
    else:
        count = kind[1]
        shape = (count, 8 * (n_group // count) * x.shape[0], x.shape[1])
    return jax.ShapeDtypeStruct(shape, dtype)


def scratch_of(kind, x, n_group):
    if kind[0] == "chain":
        return [pltpu.VMEM((n_group,) + x.shape, x.dtype)]
    if kind == "dpscatter":
        count, rows, width = x.shape
        rows = rows // 8
        return [
            pltpu.VMEM((count, 4, rows, width), x.dtype),
            pltpu.VMEM((count, 4, rows, width), x.dtype),
            pltpu.VMEM((count, 4, rows // 2, width), x.dtype),
            pltpu.VMEM((count, 2, rows // 2, width), x.dtype),
            pltpu.VMEM((count, 2, rows // 2, width), x.dtype),
        ]
    return []


def copies_of(kind, x, n_group):
    if kind[0] == "chain":
        return n_group - 1 + 8 * n_group
    if kind == "dprow":
        return 8 * x.shape[0]
    if kind == "dpscatter":
        return 10 * x.shape[0]
    return 7 if kind == "dpag" else n_group - 1


def exchange_kernel(kinds, n_group, scratch_counts, *refs):
    count = len(kinds)
    ins, outs = refs[:count], refs[count : 2 * count]
    send_sem, recv_sem = refs[-2:]
    spare = list(refs[2 * count : -2])
    scratch = []
    for number in scratch_counts:
        scratch.append(spare[:number])
        spare = spare[number:]
    z = lax.axis_index("group")
    d = lax.axis_index("dp")
    z_used = any(kind[0] in ("z", "chain") for kind in kinds)
    dp_used = any(kind[0] in ("d", "chain") for kind in kinds)

    def z_peer(k):
        return lax.rem(z + k, n_group)

    barrier = pltpu.get_barrier_semaphore()
    greeted = 0
    if z_used:
        for k in range(1, n_group):
            pl.semaphore_signal(
                barrier, inc=1, device_id={"group": z_peer(k)}, device_id_type=MESH
            )
            greeted += 1
    if dp_used:
        for k in range(1, 8):
            pl.semaphore_signal(barrier, inc=1, device_id={"dp": flip(d, k)}, device_id_type=MESH)
            greeted += 1
    pl.semaphore_wait(barrier, greeted)

    slot = [0]

    def send(src, dst, device):
        copy = pltpu.make_async_remote_copy(
            src_ref=src,
            dst_ref=dst,
            send_sem=send_sem.at[slot[0]],
            recv_sem=recv_sem.at[slot[0]],
            device_id=device,
            device_id_type=MESH,
        )
        slot[0] += 1
        copy.start()
        return copy

    pending = []
    staged = []

    def spread(src, o, matrix, block, offset, rows):
        first = rows // 32 * 16

        def place(index, part=None):
            start = index * block + offset
            size = rows
            if part is not None:
                start = start + part * first
                size = (first, rows - first)[part]
            return o.at[matrix, pl.ds(pl.multiple_of(start, 16), size), :]

        along_x = send(src, place(d), {"dp": flip(d, 2)})
        along_y = send(src, place(d), {"dp": flip(d, 4)})
        sibling = send(src, place(d), {"dp": flip(d, 1)})
        staged.append((place, along_x, along_y, sibling))

    chained = []
    for kind, x, o, spare in zip(kinds, ins, outs, scratch):
        if kind[0] == "chain":
            copies = [
                send(x, spare[0].at[z], {"group": z_peer(k)}) for k in range(1, n_group)
            ]
            per = n_group // kind[1]
            chained.append((copies, x, o, spare[0], per))
            rows = x.shape[0]
            spread(x, o, z // per, per * rows, lax.rem(z, per) * rows, rows)
    scatters = []
    for kind, x, o, spare in zip(kinds, ins, outs, scratch):
        if kind == "dprow":
            rows = x.shape[1]
            for i in range(x.shape[0]):
                spread(x.at[i], o, i, rows, 0, rows)
        elif kind == "dpscatter":
            rows = x.shape[1] // 8
            for i in range(x.shape[0]):
                copies = []
                for r in (3, 1, 2, 0):
                    start = pl.multiple_of(flip(d, 2 * r + 1) * rows, rows)
                    copies.append(
                        send(
                            x.at[i, pl.ds(start, rows), :],
                            spare[0].at[i, r],
                            {"dp": flip(d, 1)},
                        )
                    )
                scatters.append((i, x, o, rows, spare, copies))
        elif kind == "dpag":
            for k in range(1, 8):
                pending.append(send(x, o.at[d], {"dp": flip(d, k)}))
    if not chained:
        start_z(kinds, ins, outs, z, z_peer, n_group, send, pending)

    for kind, x, o in zip(kinds, ins, outs):
        if kind[0] == "chain":
            per = n_group // kind[1]
            rows = x.shape[0]
            start = pl.multiple_of(d * per * rows + lax.rem(z, per) * rows, 16)
            o[z // per, pl.ds(start, rows), :] = x[...]
        elif kind == "dprow":
            rows = x.shape[1]
            o[:, pl.ds(pl.multiple_of(d * rows, rows), rows), :] = x[...]
        elif kind == "dpag":
            o[d] = x[...]
        elif kind == "zag":
            o[z] = x[...]
        elif kind == "za2a":
            o[z] = x[z]

    for copies, x, o, held, per in chained:
        rows = x.shape[0]
        for k in range(1, n_group):
            copies[k - 1].wait_recv()
            origin = lax.rem(z + n_group - k, n_group)
            offset = lax.rem(origin, per) * rows
            spread(held.at[origin], o, origin // per, per * rows, offset, rows)
            start = pl.multiple_of(d * per * rows + offset, 16)
            o[origin // per, pl.ds(start, rows), :] = held[origin]
    if chained:
        start_z(kinds, ins, outs, z, z_peer, n_group, send, pending)

    second = []
    for place, along_x, along_y, sibling in staged:
        along_x.wait_recv()
        from_x = flip(d, 2)
        to_y = send(place(from_x, 0), place(from_x, 0), {"dp": flip(d, 4)})
        share_x = send(place(from_x), place(from_x), {"dp": flip(d, 1)})
        along_y.wait_recv()
        from_y = flip(d, 4)
        to_x = send(place(from_y, 1), place(from_y, 1), {"dp": flip(d, 2)})
        share_y = send(place(from_y), place(from_y), {"dp": flip(d, 1)})
        second.append((place, (along_x, along_y, to_y, to_x), (sibling, share_x, share_y)))
    third = []
    for place, links, shares in second:
        links[2].wait_recv()
        links[3].wait_recv()
        far = flip(d, 6)
        third.append(send(place(far), place(far), {"dp": flip(d, 1)}))

    wide = jnp.float32
    level = []
    for i, x, o, rows, spare, copies in scatters:
        near, total, recv_b, recv_c, part = spare
        half = rows // 2
        low, high = pl.ds(0, half), pl.ds(half, half)
        for r, copy in zip((3, 1, 2, 0), copies):
            copy.wait_recv()
            start = pl.multiple_of(flip(d, 2 * r) * rows, rows)
            own = x[i, pl.ds(start, rows), :].astype(wide)
            total[i, r] = (own + near[i, r].astype(wide)).astype(total.dtype)
        to_x = {"dp": flip(d, 2)}
        to_y = {"dp": flip(d, 4)}
        moved = [
            send(total.at[i, 3, low], recv_b.at[i, 1], to_x),
            send(total.at[i, 3, high], recv_b.at[i, 3], to_y),
            send(total.at[i, 1, low], recv_b.at[i, 0], to_x),
            send(total.at[i, 2, high], recv_b.at[i, 2], to_y),
        ]
        level.append(moved)
    last = []
    for (i, x, o, rows, spare, copies), moved in zip(scatters, level):
        near, total, recv_b, recv_c, part = spare
        half = rows // 2
        low, high = pl.ds(0, half), pl.ds(half, half)
        moved[0].wait_recv()
        part[i, 0] = (
            total[i, 2, low].astype(wide) + recv_b[i, 1].astype(wide)
        ).astype(part.dtype)
        moved[1].wait_recv()
        part[i, 1] = (
            total[i, 1, high].astype(wide) + recv_b[i, 3].astype(wide)
        ).astype(part.dtype)
        last.append(
            (
                send(part.at[i, 0], recv_c.at[i, 0], {"dp": flip(d, 4)}),
                send(part.at[i, 1], recv_c.at[i, 1], {"dp": flip(d, 2)}),
            )
        )
    for (i, x, o, rows, spare, copies), moved, ends in zip(scatters, level, last):
        near, total, recv_b, recv_c, part = spare
        half = rows // 2
        low, high = pl.ds(0, half), pl.ds(half, half)
        moved[2].wait_recv()
        moved[3].wait_recv()
        ends[0].wait_recv()
        o[i, low, :] = (
            total[i, 0, low].astype(wide) + recv_b[i, 0].astype(wide) + recv_c[i, 0].astype(wide)
        )
        ends[1].wait_recv()
        o[i, high, :] = (
            total[i, 0, high].astype(wide) + recv_b[i, 2].astype(wide) + recv_c[i, 1].astype(wide)
        )
        for copy in (*copies, *moved, *ends):
            copy.wait_send()

    for copies, *_ in chained:
        for copy in copies:
            copy.wait_send()
    for place, links, shares in second:
        for copy in shares:
            copy.wait()
        for copy in links:
            copy.wait_send()
    for copy in third:
        copy.wait()
    for copy in pending:
        copy.wait()


def start_z(kinds, ins, outs, z, z_peer, n_group, send, pending):
    for kind, x, o in zip(kinds, ins, outs):
        for k in range(1, n_group):
            if kind == "zag":
                pending.append(send(x, o.at[z], {"group": z_peer(k)}))
            elif kind == "za2a":
                pending.append(send(x.at[z_peer(k)], o.at[z], {"group": z_peer(k)}))


def exchange(collective_id, *pairs):
    n_group = lax.axis_size("group")
    kinds = tuple(kind for kind, _ in pairs)
    arrays = [x for _, x in pairs]
    if lax.axis_size("dp") != 8:
        results = []
        for kind, x in pairs:
            if kind == "zag":
                results.append(lax.all_gather(x, "group", axis=0))
            elif kind == "za2a":
                results.append(lax.all_to_all(x, "group", 0, 0))
            elif kind == "dpag":
                results.append(lax.all_gather(x, "dp", axis=0))
            elif kind == "dprow":
                results.append(lax.all_gather(x, "dp", axis=1, tiled=True))
            elif kind == "dpscatter":
                wide = x.astype(jnp.float32)
                results.append(lax.psum_scatter(wide, "dp", scatter_dimension=1, tiled=True))
            else:
                held = lax.all_gather(x, "group", axis=0).reshape(kind[1], -1, x.shape[1])
                results.append(lax.all_gather(held, "dp", axis=1, tiled=True))
        return results
    copies = sum(copies_of(kind, x, n_group) for kind, x in pairs)
    scratch = [scratch_of(kind, x, n_group) for kind, x in pairs]
    scratch_counts = tuple(len(shapes) for shapes in scratch)
    return pl.pallas_call(
        lambda *refs: exchange_kernel(kinds, n_group, scratch_counts, *refs),
        out_shape=[out_struct(kind, x, n_group) for kind, x in pairs],
        in_specs=[pl.BlockSpec(memory_space=pltpu.VMEM)] * len(kinds),
        out_specs=[pl.BlockSpec(memory_space=pltpu.VMEM)] * len(kinds),
        scratch_shapes=[
            *[shape for shapes in scratch for shape in shapes],
            pltpu.SemaphoreType.DMA((copies,)),
            pltpu.SemaphoreType.DMA((copies,)),
        ],
        compiler_params=pltpu.CompilerParams(collective_id=collective_id, has_side_effects=True),
        name=f"exchange_{collective_id}",
    )(*arrays)


def mm(left, right, dims):
    return lax.dot_general(left, right, (dims, ((), ())), preferred_element_type=jnp.float32)


NN = ((1,), (0,))
NT = ((1,), (1,))
TN = ((0,), (0,))


def newton_schulz_kernel(
    scale_ref,
    start_ref,
    attn_ref,
    ffn_ref,
    gram_ref,
    own_ref,
    weight_ref,
    out_ref,
    gram,
    gram_b,
    mixed,
    mixed_b,
    half,
    half_b,
):
    rows = own_ref.shape[1]
    mine = pl.ds(pl.multiple_of(start_ref[0], 8), rows)
    bf16 = jnp.bfloat16

    def one(index, whole_b):
        scale = scale_ref[index]
        lead = 1.0
        spread = None
        for iteration in range(NS_ITERS - 1):
            gram_b[...] = gram[...].astype(bf16)
            mixed[...] = coef_second * gram[...] + coef_third * mm(gram_b[...], gram_b[...], NN)
            mixed_b[...] = mixed[...].astype(bf16)
            half[...] = coef_first * gram[...] + mm(mixed_b[...], gram_b[...], NN)
            half_b[...] = half[...].astype(bf16)
            gram[...] = coef_first * half[...] + mm(half_b[...], mixed_b[...], NN)
            if spread is None:
                spread = mixed[mine, :]
            else:
                product = mm(spread.astype(bf16), mixed_b[...], NN)
                spread = coef_first * spread + lead * mixed[mine, :] + product
            lead = lead * coef_first
        gram_b[...] = gram[...].astype(bf16)
        once = lead * gram[mine, :] + mm(spread.astype(bf16), gram_b[...], NN)
        twice = mm(once.astype(bf16), gram_b[...], NN)
        spread = coef_first * spread + coef_second * once + coef_third * twice
        lead = lead * coef_first
        moved = lead * own_ref[index] + mm(spread.astype(bf16), whole_b, NN)
        out_ref[index] = weight_ref[index] - (muon_rate * scale) * moved

    gram[...] = mm(attn_ref[...], attn_ref[...], NT) * (scale_ref[0] * scale_ref[0])
    one(0, attn_ref[...])

    @pl.loop(0, gram_ref.shape[0])
    def _(i):
        gram[...] = gram_ref[i].astype(jnp.float32) * (scale_ref[i + 1] * scale_ref[i + 1])
        one(i + 1, ffn_ref[i])


def newton_schulz(scales, row_start, attn_b, ffn_b, grams, own, weights):
    side = attn_b.shape[0]
    vmem = pl.BlockSpec(memory_space=pltpu.VMEM)
    smem = pl.BlockSpec(memory_space=pltpu.SMEM)
    wide, narrow = pltpu.VMEM((side, side), jnp.float32), pltpu.VMEM((side, side), jnp.bfloat16)
    return pl.pallas_call(
        newton_schulz_kernel,
        out_shape=jax.ShapeDtypeStruct(own.shape, jnp.float32),
        in_specs=[smem, smem, vmem, vmem, vmem, vmem, vmem],
        out_specs=vmem,
        scratch_shapes=[wide, narrow] * 3,
        compiler_params=pltpu.CompilerParams(vmem_limit_bytes=48 * 2**20),
        name="newton_schulz",
    )(scales, jnp.reshape(row_start, (1,)), attn_b, ffn_b, grams, own, weights)


def on_device(
    inputs,
    cotangent,
    lengths,
    attn_weights,
    attn_momenta,
    ffn_weights,
    ffn_momenta,
    vectors,
    vector_momenta,
):
    group_count = lax.axis_size("group")
    dp_count = lax.axis_size("dp")
    own_index = lax.axis_index("group")
    dp_index = lax.axis_index("dp")
    token_count, width = inputs.shape
    own_count = attn_weights.shape[1]
    quarter = ffn_weights.shape[2]
    head_size = width // HEADS
    scale = 1.0 / math.sqrt(head_size)
    bf16 = jnp.bfloat16

    own_attn = attn_weights.astype(bf16)
    own_ffn = ffn_weights.astype(bf16)
    cotan_b = cotangent.astype(bf16)
    attn_full, ffn_full, all_cotan = exchange(
        0, (("chain", 4), own_attn[0]), ("dprow", own_ffn), ("zag", cotan_b)
    )
    w_query, w_key, w_value, w_output = [attn_full[i] for i in range(4)]
    w_expand, w_reduce = [ffn_full[i] for i in range(2)]
    all_cotan = all_cotan.reshape(-1, width)

    positions = jnp.arange(token_count, dtype=jnp.int32)
    order = jnp.arange(lengths.shape[1], dtype=jnp.int32)
    seq_ends = jnp.sum(jnp.where(order[:, None] <= order[None, :], lengths[0][:, None], 0), axis=0)
    segment = jnp.sum((positions[:, None] >= seq_ends[None, :]).astype(jnp.int32), axis=1)
    allowed = (segment[:, None] == segment[None, :]) & (positions[None, :] <= positions[:, None])
    normed_first, inverse_first = norm_forward(inputs)
    hidden_first = (normed_first * vectors[0] + vectors[1]).astype(bf16)
    query = ((mm(hidden_first, w_query, NN) + vectors[2]) * scale).astype(bf16)
    keyed = mm(hidden_first, w_key, NN).astype(bf16)
    valued = (mm(hidden_first, w_value, NN) + vectors[3]).astype(bf16)
    query_heads = query.reshape(token_count, HEADS, head_size)
    key_heads = keyed.reshape(token_count, HEADS, head_size)
    value_heads = valued.reshape(token_count, HEADS, head_size)
    scores = masked_scores(query_heads, key_heads, allowed)
    highest = jnp.max(scores, axis=2, keepdims=True)
    log_total = highest + jnp.log(jnp.sum(jnp.exp(scores - highest), axis=2, keepdims=True))
    probs = jnp.exp(scores - log_total)
    probs_b = probs.astype(bf16)
    attended = jnp.einsum("hqk,khd->qhd", probs_b, value_heads, preferred_element_type=jnp.float32)
    attended = attended.reshape(token_count, width).astype(bf16)
    middle = inputs + mm(attended, w_output, NN) + vectors[4]
    normed_second, inverse_second = norm_forward(middle)
    hidden_second = (normed_second * vectors[5] + vectors[6]).astype(bf16)

    (all_second,) = exchange(2, ("zag", hidden_second))
    all_second = all_second.reshape(-1, width)
    own_bias = lax.dynamic_slice_in_dim(vectors[8:].reshape(-1), own_index * quarter, quarter, 0)
    before = mm(all_second, w_expand, NN) + own_bias
    active = jnp.maximum(before, 0.0).astype(bf16)
    out_part = mm(active, w_reduce, NT).astype(bf16)
    grad_before = jnp.where(before > 0.0, mm(all_cotan, w_reduce, NN), 0.0)
    before_grad_b = grad_before.astype(bf16)
    second_part = mm(before_grad_b, w_expand, NT).astype(bf16)

    ffn_terms = jnp.stack(
        [mm(all_second, before_grad_b, TN).astype(bf16), mm(all_cotan, active, TN).astype(bf16)]
    )
    second_parts, ffn_total = exchange(
        3,
        ("za2a", second_part.reshape(group_count, token_count, width)),
        ("dpscatter", ffn_terms),
    )
    total_tokens = float(token_count * dp_count * group_count)
    ffn_grads = ffn_total / total_tokens
    ffn_next = momentum_rate * ffn_momenta + ffn_grads
    ffn_next_b = ffn_next.astype(bf16)
    grad_second = jnp.sum(second_parts.astype(jnp.float32), axis=0)
    grad_middle = cotangent + norm_backward(
        grad_second * vectors[5], normed_second, inverse_second
    )
    middle_b = grad_middle.astype(bf16)
    grad_attended = mm(middle_b, w_output, NT).astype(bf16)
    attended_heads = grad_attended.reshape(token_count, HEADS, head_size)
    grad_probs = jnp.einsum(
        "qhd,khd->hqk", attended_heads, value_heads, preferred_element_type=jnp.float32
    )
    grad_value = jnp.einsum(
        "hqk,qhd->khd", probs_b, attended_heads, preferred_element_type=jnp.float32
    )
    delta = jnp.sum(probs * grad_probs, axis=2, keepdims=True)
    grad_scores = (probs * (grad_probs - delta)).astype(bf16)
    grad_query = (
        jnp.einsum("hqk,khd->qhd", grad_scores, key_heads, preferred_element_type=jnp.float32)
        * scale
    )
    grad_key = jnp.einsum(
        "hqk,qhd->khd", grad_scores, query_heads, preferred_element_type=jnp.float32
    )
    query_grad = grad_query.reshape(token_count, width)
    key_grad = grad_key.reshape(token_count, width)
    value_grad = grad_value.reshape(token_count, width)
    query_grad_b = query_grad.astype(bf16)
    key_grad_b = key_grad.astype(bf16)
    value_grad_b = value_grad.astype(bf16)

    attn_terms = jnp.stack(
        [
            mm(hidden_first, query_grad_b, TN).astype(bf16),
            mm(hidden_first, key_grad_b, TN).astype(bf16),
            mm(hidden_first, value_grad_b, TN).astype(bf16),
            mm(attended, middle_b, TN).astype(bf16),
        ]
    )
    attn_sums, out_parts = exchange(
        4,
        ("dpscatter", attn_terms),
        ("za2a", out_part.reshape(group_count, token_count, width)),
    )
    outputs = middle + jnp.sum(out_parts.astype(jnp.float32), axis=0) + vectors[7]
    grad_first = (
        mm(query_grad_b, w_query, NT) + mm(key_grad_b, w_key, NT) + mm(value_grad_b, w_value, NT)
    )
    input_grad = grad_middle + norm_backward(grad_first * vectors[0], normed_first, inverse_first)
    small_terms = jnp.stack(
        [
            jnp.sum(grad_first * normed_first, axis=0),
            jnp.sum(grad_first, axis=0),
            jnp.sum(query_grad, axis=0),
            jnp.sum(value_grad, axis=0),
            jnp.sum(grad_middle, axis=0),
            jnp.sum(grad_second * normed_second, axis=0),
            jnp.sum(grad_second, axis=0),
            jnp.sum(cotangent, axis=0),
        ]
    )
    owner_mask = jnp.arange(group_count, dtype=jnp.int32) == own_index
    bias_terms = jnp.where(owner_mask[:, None], jnp.sum(grad_before, axis=0)[None], 0.0)
    vector_terms = jnp.concatenate([small_terms, bias_terms.reshape(-1, width)], axis=0)
    def square_sums(own):
        sums = jnp.sum(own * own, axis=(1, 2))
        return jnp.broadcast_to(jnp.pad(sums, (0, 8 - own.shape[0]))[:, None], (8, 128))

    attn_pieces, ffn_full_next, vector_all, ffn_squares = exchange(
        5,
        ("za2a", attn_sums.astype(bf16)),
        ("dprow", ffn_next_b),
        ("dpag", vector_terms),
        ("dpag", square_sums(ffn_next)),
    )
    attn_grads = jnp.sum(attn_pieces.astype(jnp.float32), axis=0, keepdims=True) / total_tokens
    attn_next = momentum_rate * attn_momenta + attn_grads
    gram_part = jnp.concatenate(
        [mm(ffn_next_b[0], ffn_full_next[0], NT), mm(ffn_next_b[1], ffn_full_next[1], NT)]
    )
    piece = 2 * own_count // group_count
    attn_full_next, gram_pieces, attn_squares, ffn_squares, vector_groups = exchange(
        6,
        ("dprow", attn_next.astype(bf16)),
        ("za2a", gram_part.astype(bf16).reshape(group_count, piece, width)),
        ("dpag", square_sums(attn_next)),
        ("zag", jnp.sum(ffn_squares, axis=0)),
        ("zag", jnp.sum(vector_all, axis=0)),
    )
    gram_piece = jnp.sum(gram_pieces.astype(jnp.float32), axis=0).astype(bf16)
    (gram_full,) = exchange(7, (("chain", 2), gram_piece))
    attn_square = jnp.sum(attn_squares, axis=0)[:1, 0]
    ffn_square = jnp.sum(ffn_squares, axis=0)[:2, 0]
    scales = 1.0 / (jnp.sqrt(jnp.concatenate([attn_square, ffn_square])) + 1e-07)
    new_weights = newton_schulz(
        scales,
        dp_index * own_count,
        attn_full_next[0],
        ffn_full_next,
        gram_full,
        jnp.concatenate([attn_next, ffn_next], axis=0),
        jnp.concatenate([attn_weights, ffn_weights], axis=0),
    )
    new_attn_weights = new_weights[:1]
    new_ffn_weights = new_weights[1:]
    vector_grads = jnp.sum(vector_groups, axis=0) / total_tokens
    new_vector_momenta = momentum_rate * vector_momenta + vector_grads
    mean_square = jnp.mean(new_vector_momenta * new_vector_momenta, axis=1, keepdims=True)
    new_vectors = vectors - vector_rate * new_vector_momenta * lax.rsqrt(mean_square + 1e-06)
    return (
        outputs,
        input_grad,
        attn_grads,
        ffn_grads,
        vector_grads,
        new_attn_weights,
        attn_next,
        new_ffn_weights,
        ffn_next,
        new_vectors,
        new_vector_momenta,
    )


def solution(mesh):
    in_specs = (
        P(("dp", "group"), None),
        P(("dp", "group"), None),
        P(("dp", "group"), None),
        P("group", "dp", None),
        P("group", "dp", None),
        P(None, "dp", "group"),
        P(None, "dp", "group"),
        P(),
        P(),
    )
    out_specs = (
        P(("dp", "group"), None),
        P(("dp", "group"), None),
        P("group", "dp", None),
        P(None, "dp", "group"),
        P(),
        P("group", "dp", None),
        P("group", "dp", None),
        P(None, "dp", "group"),
        P(None, "dp", "group"),
        P(),
        P(),
    )
    return jax.shard_map(
        on_device, mesh=mesh, in_specs=in_specs, out_specs=out_specs, check_vma=False
    )
```

```python
import math
import types

import jax
import jax.numpy as jnp
from jax import lax
from jax.experimental import pallas as pl
from jax.experimental.pallas import tpu as pltpu
from jax.sharding import PartitionSpec as P

HEADS = 12
NS_ITERS = 3


coef_first = 3.4445
coef_second = -4.775
coef_third = 2.0315
momentum_rate = 0.9
muon_rate = 0.8
vector_rate = 0.1


def norm_forward(rows):
    centre = jnp.mean(rows, axis=1, keepdims=True)
    centred = rows - centre
    variance = jnp.mean(centred * centred, axis=1, keepdims=True)
    inverse = lax.rsqrt(variance + 1e-05)
    return (centred * inverse, inverse)


def norm_backward(grad_normed, normed, inverse):
    return inverse * (
        grad_normed
        - jnp.mean(grad_normed, axis=1, keepdims=True)
        - normed * jnp.mean(grad_normed * normed, axis=1, keepdims=True)
    )


def masked_scores(query_heads, key_heads, allowed):
    scores = jnp.einsum("qhd,khd->hqk", query_heads, key_heads, preferred_element_type=jnp.float32)
    return jnp.where(allowed[None], scores, -jnp.inf)


MESH = pl.DeviceIdType.MESH


def flip(index, bits):
    result = index
    for bit in (1, 2, 4):
        if bits & bit:
            result = result + bit - 2 * bit * ((index // bit) % 2)
    return result


def exchange(*pairs):
    results = []
    for kind, x in pairs:
        if kind == "zag":
            results.append(lax.all_gather(x, "group", axis=0))
        elif kind == "za2a":
            results.append(lax.all_to_all(x, "group", 0, 0))
        elif kind == "dpag":
            results.append(lax.all_gather(x, "dp", axis=0))
        elif kind == "dprow":
            results.append(lax.all_gather(x, "dp", axis=1, tiled=True))
        elif kind == "dpscatter":
            wide = x.astype(jnp.float32)
            results.append(lax.psum_scatter(wide, "dp", scatter_dimension=1, tiled=True))
        else:
            held = lax.all_gather(x, "group", axis=0).reshape(kind[1], -1, x.shape[1])
            results.append(lax.all_gather(held, "dp", axis=1, tiled=True))
    return results


def mm(left, right, dims):
    return lax.dot_general(left, right, (dims, ((), ())), preferred_element_type=jnp.float32)


NN = ((1,), (0,))
NT = ((1,), (1,))
TN = ((0,), (0,))


def newton_schulz_kernel(
    scale_ref,
    start_ref,
    attn_ref,
    ffn_ref,
    gram_ref,
    own_ref,
    weight_ref,
    out_ref,
    gram,
    gram_b,
    mixed,
    mixed_b,
    half,
    half_b,
):
    rows = own_ref.shape[1]
    mine = pl.ds(pl.multiple_of(start_ref[0], 8), rows)
    bf16 = jnp.bfloat16

    def one(index, whole_b):
        scale = scale_ref[index]
        lead = 1.0
        spread = None
        for iteration in range(NS_ITERS - 1):
            gram_b[...] = gram[...].astype(bf16)
            mixed[...] = coef_second * gram[...] + coef_third * mm(gram_b[...], gram_b[...], NN)
            mixed_b[...] = mixed[...].astype(bf16)
            half[...] = coef_first * gram[...] + mm(mixed_b[...], gram_b[...], NN)
            half_b[...] = half[...].astype(bf16)
            gram[...] = coef_first * half[...] + mm(half_b[...], mixed_b[...], NN)
            if spread is None:
                spread = mixed[mine, :]
            else:
                product = mm(spread.astype(bf16), mixed_b[...], NN)
                spread = coef_first * spread + lead * mixed[mine, :] + product
            lead = lead * coef_first
        gram_b[...] = gram[...].astype(bf16)
        once = lead * gram[mine, :] + mm(spread.astype(bf16), gram_b[...], NN)
        twice = mm(once.astype(bf16), gram_b[...], NN)
        spread = coef_first * spread + coef_second * once + coef_third * twice
        lead = lead * coef_first
        moved = lead * own_ref[index] + mm(spread.astype(bf16), whole_b, NN)
        out_ref[index] = weight_ref[index] - (muon_rate * scale) * moved

    gram[...] = mm(attn_ref[...], attn_ref[...], NT) * (scale_ref[0] * scale_ref[0])
    one(0, attn_ref[...])

    @pl.loop(0, gram_ref.shape[0])
    def _(i):
        gram[...] = gram_ref[i].astype(jnp.float32) * (scale_ref[i + 1] * scale_ref[i + 1])
        one(i + 1, ffn_ref[i])


def newton_schulz(scales, row_start, attn_b, ffn_b, grams, own, weights):
    side = attn_b.shape[0]
    vmem = pl.BlockSpec(memory_space=pltpu.VMEM)
    smem = pl.BlockSpec(memory_space=pltpu.SMEM)
    wide, narrow = pltpu.VMEM((side, side), jnp.float32), pltpu.VMEM((side, side), jnp.bfloat16)
    return pl.pallas_call(
        newton_schulz_kernel,
        out_shape=jax.ShapeDtypeStruct(own.shape, jnp.float32),
        in_specs=[smem, smem, vmem, vmem, vmem, vmem, vmem],
        out_specs=vmem,
        scratch_shapes=[wide, narrow] * 3,
        compiler_params=pltpu.CompilerParams(vmem_limit_bytes=48 * 2**20),
        name="newton_schulz",
    )(scales, jnp.reshape(row_start, (1,)), attn_b, ffn_b, grams, own, weights)


class Net:
    def __init__(self, send_sem, recv_sem, z, d, n):
        self.send_sem, self.recv_sem = send_sem, recv_sem
        self.z, self.d, self.n = z, d, n
        self.slot = 0
        self.copies = []
        self.to_core = {"dp": flip(d, 1)}
        self.to_x = {"dp": flip(d, 2)}
        self.to_y = {"dp": flip(d, 4)}

    def send(self, src, dst, device):
        copy = pltpu.make_async_remote_copy(
            src_ref=src,
            dst_ref=dst,
            send_sem=self.send_sem.at[self.slot],
            recv_sem=self.recv_sem.at[self.slot],
            device_id=device,
            device_id_type=MESH,
        )
        self.slot += 1
        copy.start()
        self.copies.append(copy)
        return copy

    def up(self, k):
        return lax.rem(self.z + k, self.n)

    def down(self, k):
        return lax.rem(self.z + self.n - k, self.n)

    def line(self, src, dst):
        return [self.send(src, dst, {"group": self.up(k)}) for k in range(1, self.n)]

    def plane(self, src, dst):
        return [self.send(src, dst, {"dp": flip(self.d, k)}) for k in range(1, 8)]

    def finish(self):
        for copy in self.copies:
            copy.wait_send()


class Gather:
    def __init__(self, net, src, full, rows):
        self.net, self.full, self.rows = net, full, rows
        place = self.place(net.d)
        self.x = net.send(src, place, net.to_x)
        self.y = net.send(src, place, net.to_y)
        self.core = net.send(src, place, net.to_core)

    def place(self, index, part=None):
        first = self.rows // 32 * 16
        start, size = index * self.rows, self.rows
        if part is not None:
            start = start + part * first
            size = (first, self.rows - first)[part]
        return self.full.at[pl.ds(pl.multiple_of(start, 16), size), :]

    def second(self):
        net = self.net
        from_x, from_y = flip(net.d, 2), flip(net.d, 4)
        self.x.wait_recv()
        self.via_y = net.send(self.place(from_x, 0), self.place(from_x, 0), net.to_y)
        self.share_x = net.send(self.place(from_x), self.place(from_x), net.to_core)
        self.y.wait_recv()
        self.via_x = net.send(self.place(from_y, 1), self.place(from_y, 1), net.to_x)
        self.share_y = net.send(self.place(from_y), self.place(from_y), net.to_core)

    def third(self):
        net = self.net
        far = flip(net.d, 6)
        self.via_y.wait_recv()
        self.via_x.wait_recv()
        self.share_far = net.send(self.place(far), self.place(far), net.to_core)

    def end(self):
        for copy in (self.core, self.share_x, self.share_y, self.share_far):
            copy.wait_recv()


class Scatter:
    def __init__(self, net, x, near, total, recv_b, recv_c, part):
        self.net, self.x, self.rows = net, x, x.shape[0] // 8
        self.near, self.total, self.recv_b, self.recv_c, self.part = near, total, recv_b, recv_c, part
        self.copies = [
            net.send(self.block(2 * r + 1), near.at[r], net.to_core) for r in (3, 1, 2, 0)
        ]

    def block(self, bits):
        start = pl.multiple_of(flip(self.net.d, bits) * self.rows, 16)
        return self.x.at[pl.ds(start, self.rows), :]

    def second(self):
        net, total = self.net, self.total
        wide = jnp.float32
        half = self.rows // 2
        low, high = pl.ds(0, half), pl.ds(half, half)
        for r, copy in zip((3, 1, 2, 0), self.copies):
            copy.wait_recv()
            own = self.block(2 * r)[...].astype(wide)
            total[r] = (own + self.near[r].astype(wide)).astype(total.dtype)
        self.moved = [
            net.send(total.at[3, low], self.recv_b.at[1], net.to_x),
            net.send(total.at[3, high], self.recv_b.at[3], net.to_y),
            net.send(total.at[1, low], self.recv_b.at[0], net.to_x),
            net.send(total.at[2, high], self.recv_b.at[2], net.to_y),
        ]

    def third(self):
        net, total, part = self.net, self.total, self.part
        wide = jnp.float32
        half = self.rows // 2
        low, high = pl.ds(0, half), pl.ds(half, half)
        self.moved[0].wait_recv()
        part[0] = (total[2, low].astype(wide) + self.recv_b[1].astype(wide)).astype(part.dtype)
        self.ends = [net.send(part.at[0], self.recv_c.at[0], net.to_y)]
        self.moved[1].wait_recv()
        part[1] = (total[1, high].astype(wide) + self.recv_b[3].astype(wide)).astype(part.dtype)
        self.ends.append(net.send(part.at[1], self.recv_c.at[1], net.to_x))

    def end(self):
        total = self.total
        wide = jnp.float32
        half = self.rows // 2
        low, high = pl.ds(0, half), pl.ds(half, half)
        self.moved[2].wait_recv()
        self.moved[3].wait_recv()
        self.ends[0].wait_recv()
        self.ends[1].wait_recv()
        first = total[0, low].astype(wide) + self.recv_b[0].astype(wide) + self.recv_c[0].astype(wide)
        second = total[0, high].astype(wide) + self.recv_b[2].astype(wide) + self.recv_c[1].astype(wide)
        return jnp.concatenate([first, second], axis=0)


def muon_steps(gram, gram_b, mixed_b, half_b, mine, own, whole_b, scale, weight, store):
    bf16 = jnp.bfloat16
    lead = 1.0
    spread = None
    for iteration in range(NS_ITERS - 1):
        gram_b[...] = gram[...].astype(bf16)
        own_gram = gram[mine, :]
        mixed_b[...] = (coef_second * gram[...] + coef_third * mm(gram_b[...], gram_b[...], NN)).astype(
            bf16
        )
        yield
        own_mixed = coef_second * own_gram + coef_third * mm(own_gram.astype(bf16), gram_b[...], NN)
        gram[...] = coef_first * gram[...] + mm(mixed_b[...], gram_b[...], NN)
        half_b[...] = gram[...].astype(bf16)
        yield
        gram[...] = coef_first * gram[...] + mm(half_b[...], mixed_b[...], NN)
        if spread is None:
            spread = own_mixed
        else:
            product = mm(spread.astype(bf16), mixed_b[...], NN)
            spread = coef_first * spread + lead * own_mixed + product
        lead = lead * coef_first
        yield
    gram_b[...] = gram[...].astype(bf16)
    once = lead * gram[mine, :] + mm(spread.astype(bf16), gram_b[...], NN)
    twice = mm(once.astype(bf16), gram_b[...], NN)
    spread = coef_first * spread + coef_second * once + coef_third * twice
    lead = lead * coef_first
    moved = lead * own + mm(spread.astype(bf16), whole_b[...], NN)
    store(weight - (muon_rate * scale) * moved)
    yield


def layer_kernel(n, names, *refs):
    ref = types.SimpleNamespace(**dict(zip(names, refs)))
    bf16, wide = jnp.bfloat16, jnp.float32
    z, d = lax.axis_index("group"), lax.axis_index("dp")
    net = Net(ref.send_sem, ref.recv_sem, z, d, n)
    lengths, vectors = ref.lengths, ref.vectors
    tokens, width = ref.inputs.shape
    rows = ref.attn_weights.shape[1]
    head_size = width // HEADS
    pairs = HEADS // 2
    pair_width = 2 * head_size
    scale = 1.0 / math.sqrt(head_size)
    total_tokens = float(tokens * 8 * n)
    ranks = range(1, n)

    def vector(i):
        return vectors[pl.ds(i, 1), :]

    def column_sum(x):
        return jnp.sum(x, axis=0, keepdims=True)

    own_attn, own_ffn = ref.own_attn, ref.own_ffn
    held, attn_full, ffn_full = ref.held, ref.attn_full, ref.ffn_full
    own_attn[...] = ref.attn_weights[0].astype(bf16)
    all_cotan, all_second = ref.all_cotan, ref.all_second
    all_cotan[z] = ref.cotangent[...].astype(bf16)
    own_ffn[...] = ref.ffn_weights[...].astype(bf16)

    barrier = pltpu.get_barrier_semaphore()
    for k in ranks:
        pl.semaphore_signal(barrier, inc=1, device_id={"group": net.up(k)}, device_id_type=MESH)
    for k in range(1, 8):
        pl.semaphore_signal(barrier, inc=1, device_id={"dp": flip(d, k)}, device_id_type=MESH)
    pl.semaphore_wait(barrier, n - 1 + 7)

    chain = net.line(own_attn, held.at[z])
    own_rows = pl.ds(pl.multiple_of(d * rows, 16), rows)

    weights = [Gather(net, own_attn, attn_full.at[z], rows)]
    ffn_weights = [Gather(net, own_ffn.at[i], ffn_full.at[i], rows) for i in range(2)]
    cotan_copies = net.line(all_cotan.at[z], all_cotan.at[z])
    for i in range(2):
        ffn_full[i, own_rows, :] = own_ffn[i]
    attn_full[z, own_rows, :] = own_attn[...]

    centre = jnp.mean(ref.inputs[...], axis=1, keepdims=True)
    centred = ref.inputs[...] - centre
    inverse_first = lax.rsqrt(jnp.mean(centred * centred, axis=1, keepdims=True) + 1e-05)
    ref.normed_first[...] = centred * inverse_first
    hidden_first, attended = ref.hidden_first, ref.attended
    hidden_first[...] = (ref.normed_first[...] * vector(0) + vector(1)).astype(bf16)

    for k in ranks:
        origin = net.down(k)
        chain[k - 1].wait_recv()
        weights.append(Gather(net, held.at[origin], attn_full.at[origin], rows))
        attn_full[origin, own_rows, :] = held[origin]
        if k == 1:
            weights[0].second()
    for gather in weights[1:]:
        gather.second()
    for gather in weights:
        gather.third()
    for gather in ffn_weights:
        gather.second()
    for gather in weights:
        gather.end()
    for gather in ffn_weights:
        gather.third()

    lane = lax.broadcasted_iota(jnp.int32, (tokens, pair_width), 1)
    low_lane = lane < head_size
    ones = lax.broadcasted_iota(jnp.int32, (1, pair_width), 1) < head_size
    low_mask = jnp.where(ones, 1.0, 0.0).astype(bf16)
    high_mask = jnp.where(ones, 0.0, 1.0).astype(bf16)

    def split(x):
        return jnp.concatenate([x * low_mask, x * high_mask], axis=0)

    def join(x):
        return jnp.where(low_lane, x[:tokens], x[tokens:])

    query, keyed, valued = ref.query, ref.keyed, ref.valued
    query[...] = ((mm(hidden_first[...], attn_full[0], NN) + vector(2)) * scale).astype(bf16)
    keyed[...] = mm(hidden_first[...], attn_full[1], NN).astype(bf16)
    valued[...] = (mm(hidden_first[...], attn_full[2], NN) + vector(3)).astype(bf16)

    at_row = lax.broadcasted_iota(jnp.int32, (2 * tokens, tokens), 0)
    at_row = jnp.where(at_row < tokens, at_row, at_row - tokens)
    at_column = lax.broadcasted_iota(jnp.int32, (2 * tokens, tokens), 1)
    row_part = jnp.zeros_like(at_row)
    column_part = jnp.zeros_like(at_column)
    edge = 0
    for i in range(lengths.shape[1]):
        edge = edge + lengths[0, i]
        row_part = row_part + jnp.where(at_row >= edge, 1, 0)
        column_part = column_part + jnp.where(at_column >= edge, 1, 0)
    allowed = (row_part == column_part) & (at_column <= at_row)

    probs = ref.probs
    slices = [pl.ds(p * pair_width, pair_width) for p in range(pairs)]
    for p, lanes in enumerate(slices):
        scores = mm(split(query[:, lanes]), keyed[:, lanes], NT)
        probs[p] = jnp.where(allowed, scores, -jnp.inf)
    for p in range(pairs):
        raised = jnp.exp(probs[p] - jnp.max(probs[p], axis=1, keepdims=True))
        probs[p] = raised * (1.0 / jnp.sum(raised, axis=1, keepdims=True))
    for p, lanes in enumerate(slices):
        attended[:, lanes] = join(mm(probs[p].astype(bf16), valued[:, lanes], NN)).astype(bf16)

    middle = ref.middle
    middle[...] = ref.inputs[...] + mm(attended[...], attn_full[3], NN) + vector(4)
    centre = jnp.mean(middle[...], axis=1, keepdims=True)
    centred = middle[...] - centre
    inverse_second = lax.rsqrt(jnp.mean(centred * centred, axis=1, keepdims=True) + 1e-05)
    normed_second = ref.normed_second
    normed_second[...] = centred * inverse_second
    all_second[z] = (normed_second[...] * vector(5) + vector(6)).astype(bf16)
    second_copies = net.line(all_second.at[z], all_second.at[z])
    for gather in ffn_weights:
        gather.end()

    active, before_grad = ref.active, ref.before_grad
    grad_send, grad_recv, grad_own = ref.grad_send, ref.grad_recv, ref.grad_own
    out_send, out_recv, out_own = ref.out_send, ref.out_recv, ref.out_own
    bias_sum = jnp.zeros((1, width), wide)
    grad_copies = []
    for k in range(n):
        origin = net.down(k)
        if k:
            second_copies[k - 1].wait_recv()
            cotan_copies[k - 1].wait_recv()
        before = mm(all_second[origin], ffn_full[0], NN) + vector(8 + z)
        active[origin] = jnp.maximum(before, 0.0).astype(bf16)
        grad_before = jnp.where(before > 0.0, mm(all_cotan[origin], ffn_full[1], NN), 0.0)
        bias_sum = bias_sum + column_sum(grad_before)
        before_grad[origin] = grad_before.astype(bf16)
        second = mm(before_grad[origin], ffn_full[0], NT)
        if k:
            grad_send[k - 1] = second.astype(bf16)
            grad_copies.append(
                net.send(grad_send.at[k - 1], grad_recv.at[k - 1], {"group": origin})
            )
        else:
            grad_own[...] = second
        out = mm(active[origin], ffn_full[1], NT)
        if k:
            out_send[k - 1] = out.astype(bf16)
        else:
            out_own[...] = out

    def scatter(x, slot):
        pools = (ref.near, ref.total, ref.recv_b, ref.recv_c, ref.part)
        return Scatter(net, x, *[pool.at[slot] for pool in pools])

    ffn_terms, attn_terms = ref.ffn_terms, ref.attn_terms
    many = n * tokens
    ffn_terms[0] = mm(
        all_second[...].reshape(many, width), before_grad[...].reshape(many, width), TN
    ).astype(bf16)
    ffn_sums = [scatter(ffn_terms.at[0], 0)]
    ffn_terms[1] = mm(
        all_cotan[...].reshape(many, width), active[...].reshape(many, width), TN
    ).astype(bf16)
    ffn_sums.append(scatter(ffn_terms.at[1], 1))
    for part in ffn_sums:
        part.second()
    for part in ffn_sums:
        part.third()

    next_own, next_full = ref.next_own, ref.next_full
    ffn_squares, attn_squares = ref.ffn_squares, ref.attn_squares

    def square(x):
        return jnp.broadcast_to(jnp.sum(column_sum(x * x), axis=1, keepdims=True), (8, 128))

    ffn_nexts = []
    for i in range(2):
        grad = ffn_sums[i].end() / total_tokens
        ref.ffn_grads[i] = grad
        moment = momentum_rate * ref.ffn_momenta[i] + grad
        ref.new_ffn_momenta[i] = moment
        next_own[1 + i] = moment.astype(bf16)
        ffn_nexts.append(Gather(net, next_own.at[1 + i], next_full.at[1 + i], rows))
        next_full[1 + i, own_rows, :] = next_own[1 + i]
        ffn_squares[0, i] = square(moment)
    square_copies = net.plane(ffn_squares.at[0], ref.ffn_squares_in.at[d])

    total = grad_own[...]
    for k in ranks:
        grad_copies[k - 1].wait_recv()
        total = total + grad_recv[k - 1].astype(wide)
    out_copies = [
        net.send(out_send.at[k - 1], out_recv.at[k - 1], {"group": net.down(k)}) for k in ranks
    ]
    terms = ref.vector_terms
    terms[...] = jnp.zeros_like(terms)

    def put(i, x):
        terms[pl.ds(i, 1), :] = x

    def norm_back(grad, normed, inverse):
        return inverse * (
            grad
            - jnp.mean(grad, axis=1, keepdims=True)
            - normed * jnp.mean(grad * normed, axis=1, keepdims=True)
        )

    put(8 + z, bias_sum)
    put(5, column_sum(total * normed_second[...]))
    put(6, column_sum(total))
    put(7, column_sum(ref.cotangent[...]))
    grad_middle = ref.grad_middle
    grad_middle[...] = ref.cotangent[...] + norm_back(
        total * vector(5), normed_second[...], inverse_second
    )
    put(4, column_sum(grad_middle[...]))
    middle_b = ref.middle_b
    middle_b[...] = grad_middle[...].astype(bf16)
    attn_terms[3] = mm(attended[...], middle_b[...], TN).astype(bf16)
    attn_sums = [scatter(attn_terms.at[3], 5)]
    grad_attended = ref.grad_attended
    grad_attended[...] = mm(middle_b[...], attn_full[3], NT).astype(bf16)
    grads = [ref.query_grad, ref.key_grad, ref.value_grad]
    pulls, pushes = ref.grad_probs, ref.grad_scores
    for p, lanes in enumerate(slices):
        pulls[p] = mm(split(grad_attended[:, lanes]), valued[:, lanes], NT)
    for p in range(pairs):
        delta = jnp.sum(probs[p] * pulls[p], axis=1, keepdims=True)
        pushes[p] = (probs[p] * (pulls[p] - delta)).astype(bf16)
    for gather in ffn_nexts:
        gather.second()
    attn_sums[0].second()
    for p, lanes in enumerate(slices):
        grad_value = mm(probs[p].astype(bf16), split(grad_attended[:, lanes]), TN)
        grad_query = join(mm(pushes[p], keyed[:, lanes], NN)) * scale
        grad_key = mm(pushes[p], split(query[:, lanes]), TN)
        terms[pl.ds(2, 1), lanes] = column_sum(grad_query)
        terms[pl.ds(3, 1), lanes] = column_sum(grad_value)
        grads[0][:, lanes] = grad_query.astype(bf16)
        grads[1][:, lanes] = grad_key.astype(bf16)
        grads[2][:, lanes] = grad_value.astype(bf16)
    for m in range(3):
        attn_terms[m] = mm(hidden_first[...], grads[m][...], TN).astype(bf16)
        attn_sums.append(scatter(attn_terms.at[m], 2 + m))
    for gather in ffn_nexts:
        gather.third()
    for part in attn_sums[1:]:
        part.second()
    attn_sums[0].third()

    gram_send, gram_recv = ref.gram_send, ref.gram_recv
    piece = 2 * rows // n
    for i in range(2):
        ffn_nexts[i].end()
        gram_send[pl.ds(i * rows, rows), :] = mm(next_own[1 + i], next_full[1 + i], NT).astype(bf16)

    def gram_rows(index):
        return gram_send.at[pl.ds(pl.multiple_of(index * piece, 16), piece), :]

    gram_copies = [
        net.send(gram_rows(net.up(k)), gram_recv.at[k - 1], {"group": net.up(k)}) for k in ranks
    ]

    grad_first = mm(grads[0][...], attn_full[0], NT)
    grad_first = grad_first + mm(grads[1][...], attn_full[1], NT)
    grad_first = grad_first + mm(grads[2][...], attn_full[2], NT)
    put(0, column_sum(grad_first * ref.normed_first[...]))
    put(1, column_sum(grad_first))
    ref.input_grad[...] = grad_middle[...] + norm_back(
        grad_first * vector(0), ref.normed_first[...], inverse_first
    )
    vector_in = ref.vector_in
    vector_copies = net.plane(terms, vector_in.at[d])

    for part in attn_sums[1:]:
        part.third()

    gram_sum = gram_rows(z)[...].astype(wide)
    for k in ranks:
        gram_copies[k - 1].wait_recv()
        gram_sum = gram_sum + gram_recv[k - 1].astype(wide)
    gram_all, gram_full = ref.gram_all, ref.gram_full
    per = n // 2
    own_piece = gram_all.at[z // per, pl.ds(pl.multiple_of(lax.rem(z, per) * piece, 16), piece), :]
    own_piece[...] = gram_sum.astype(bf16)
    gram_line = net.line(own_piece, own_piece)

    piece_send, piece_recv = ref.piece_send, ref.piece_recv
    for m, part in zip((3, 0, 1, 2), attn_sums):
        piece_send[m] = part.end().astype(bf16)
    piece_copies = [
        net.send(piece_send.at[net.up(k)], piece_recv.at[k - 1], {"group": net.up(k)}) for k in ranks
    ]

    plane_sum = ref.plane_sum
    square_in = ref.ffn_squares_in
    square_total = ffn_squares[0]
    for k in range(1, 8):
        square_copies[k - 1].wait_recv()
        square_total = square_total + square_in[flip(d, k)]
    ffn_squares[1] = square_total
    plane_squares = net.line(ffn_squares.at[1], ref.ffn_squares_all.at[z])
    vector_total = terms[...]
    for k in range(1, 8):
        vector_copies[k - 1].wait_recv()
        vector_total = vector_total + vector_in[flip(d, k)]
    plane_sum[...] = vector_total
    vector_all = net.line(plane_sum, ref.vector_all.at[z])

    for copy in gram_line:
        copy.wait_recv()
    grams = []
    for i in range(2):
        grams.append(Gather(net, gram_all.at[i], gram_full.at[i], rows))
        gram_full[i, own_rows, :] = gram_all[i]

    result = out_own[...] + middle[...] + vector(7)
    for k in ranks:
        out_copies[k - 1].wait_recv()
        result = result + out_recv[k - 1].astype(wide)
    ref.outputs[...] = result

    grad = piece_send[z].astype(wide)
    for k in ranks:
        piece_copies[k - 1].wait_recv()
        grad = grad + piece_recv[k - 1].astype(wide)
    grad = grad / total_tokens
    ref.attn_grads[0] = grad
    moment = momentum_rate * ref.attn_momenta[0] + grad
    ref.new_attn_momenta[0] = moment
    next_own[0] = moment.astype(bf16)
    attn_next = Gather(net, next_own.at[0], next_full.at[0], rows)
    next_full[0, own_rows, :] = next_own[0]
    attn_squares[0] = square(moment)
    own_squares = net.plane(attn_squares.at[0], ref.attn_squares_in.at[d])
    for gather in grams:
        gather.second()
    for gather in grams:
        gather.third()

    gram, gram_b, mixed_b, half_b = ref.gram, ref.gram_b, ref.mixed_b, ref.half_b

    def inverse_norm(x):
        return 1.0 / (jnp.sqrt(x[0:1, 0:1]) + 1e-07)

    square_total = ffn_squares[1]
    for k in ranks:
        plane_squares[k - 1].wait_recv()
        square_total = square_total + ref.ffn_squares_all[net.down(k)]

    def descend(i, own_scale, whole, index, new, own, weight):
        def store(x):
            new[index] = x

        return muon_steps(
            gram,
            gram_b,
            mixed_b,
            half_b,
            own_rows,
            own[index],
            whole.at[i],
            own_scale,
            weight[index],
            store,
        )

    for i in range(2):
        grams[i].end()
        own_scale = inverse_norm(square_total[i])
        gram[...] = gram_full[i].astype(wide) * (own_scale * own_scale)
        steps = descend(
            1 + i, own_scale, next_full, i, ref.new_ffn_weights, ref.new_ffn_momenta, ref.ffn_weights
        )
        next(steps)
        if i == 0:
            attn_next.second()
        next(steps)
        next(steps)
        if i == 0:
            attn_next.third()
        for _ in steps:
            pass

    vector_total = plane_sum[...]
    for k in ranks:
        vector_all[k - 1].wait_recv()
        vector_total = vector_total + ref.vector_all[net.down(k)]
    vector_total = vector_total / total_tokens
    ref.vector_grads[...] = vector_total
    moment = momentum_rate * ref.vector_momenta[...] + vector_total
    ref.new_vector_momenta[...] = moment
    mean_square = jnp.mean(moment * moment, axis=1, keepdims=True)
    ref.new_vectors[...] = vectors[...] - vector_rate * moment * lax.rsqrt(mean_square + 1e-06)

    attn_next.end()
    square_total = attn_squares[0]
    for k in range(1, 8):
        own_squares[k - 1].wait_recv()
        square_total = square_total + ref.attn_squares_in[flip(d, k)]
    own_scale = inverse_norm(square_total)
    gram[...] = mm(next_full[0], next_full[0], NT) * (own_scale * own_scale)
    for _ in descend(
        0, own_scale, next_full, 0, ref.new_attn_weights, ref.new_attn_momenta, ref.attn_weights
    ):
        pass
    net.finish()


def settle_kernel(count, *refs):
    for i in range(count):
        refs[count + i][...] = refs[i][...]


def settle(arrays):
    count = len(arrays)
    vmem = pl.BlockSpec(memory_space=pltpu.VMEM)
    return pl.pallas_call(
        lambda *refs: settle_kernel(count, *refs),
        out_shape=[jax.ShapeDtypeStruct(x.shape, x.dtype) for x in arrays],
        in_specs=[vmem] * count,
        out_specs=[vmem] * count,
        name="settle",
    )(*arrays)


def whole_layer(**given):
    inputs, vectors = given["inputs"], given["vectors"]
    attn_weights, ffn_weights = given["attn_weights"], given["ffn_weights"]
    results = dict(
        outputs=inputs,
        input_grad=inputs,
        attn_grads=attn_weights,
        ffn_grads=ffn_weights,
        vector_grads=vectors,
        new_attn_weights=attn_weights,
        new_attn_momenta=attn_weights,
        new_ffn_weights=ffn_weights,
        new_ffn_momenta=ffn_weights,
        new_vectors=vectors,
        new_vector_momenta=vectors,
    )
    n = lax.axis_size("group")
    tokens, width = inputs.shape
    rows = attn_weights.shape[1]
    side = 8 * rows
    piece = 2 * rows // n
    half = rows // 2
    bf16, wide = jnp.bfloat16, jnp.float32
    block = (tokens, width)
    narrow = dict(
        own_attn=(rows, width),
        own_ffn=(2, rows, width),
        held=(n, rows, width),
        attn_full=(n, side, width),
        ffn_full=(2, side, width),
        all_cotan=(n, *block),
        all_second=(n, *block),
        query=block,
        keyed=block,
        valued=block,
        active=(n, *block),
        before_grad=(n, *block),
        grad_send=(n - 1, *block),
        grad_recv=(n - 1, *block),
        out_send=(n - 1, *block),
        out_recv=(n - 1, *block),
        ffn_terms=(2, side, width),
        attn_terms=(n, side, width),
        hidden_first=block,
        attended=block,
        middle_b=block,
        query_grad=block,
        key_grad=block,
        value_grad=block,
        piece_send=(n, rows, width),
        piece_recv=(n - 1, rows, width),
        grad_scores=(HEADS // 2, 2 * tokens, tokens),
        near=(6, 4, rows, width),
        total=(6, 4, rows, width),
        recv_b=(6, 4, half, width),
        recv_c=(6, 2, half, width),
        part=(6, 2, half, width),
        grad_attended=block,
        next_own=(3, rows, width),
        next_full=(3, side, width),
        gram_send=(2 * rows, side),
        gram_recv=(n - 1, piece, side),
        gram_all=(2, rows, side),
        gram_full=(2, side, side),
        gram_b=(side, side),
        mixed_b=(side, side),
        half_b=(side, side),
    )
    full = dict(
        normed_first=block,
        middle=block,
        normed_second=block,
        probs=(HEADS // 2, 2 * tokens, tokens),
        grad_probs=(HEADS // 2, 2 * tokens, tokens),
        grad_own=block,
        out_own=block,
        grad_middle=block,
        vector_terms=vectors.shape,
        vector_in=(8, *vectors.shape),
        plane_sum=vectors.shape,
        vector_all=(n, *vectors.shape),
        ffn_squares=(2, 2, 8, 128),
        ffn_squares_in=(8, 2, 8, 128),
        ffn_squares_all=(n, 2, 8, 128),
        attn_squares=(1, 8, 128),
        attn_squares_in=(8, 8, 128),
        gram=(side, side),
    )
    scratch = {name: pltpu.VMEM(shape, bf16) for name, shape in narrow.items()}
    scratch |= {name: pltpu.VMEM(shape, wide) for name, shape in full.items()}
    copies = 256
    scratch |= dict(
        send_sem=pltpu.SemaphoreType.DMA((copies,)),
        recv_sem=pltpu.SemaphoreType.DMA((copies,)),
    )
    names = (*given, *results, *scratch)
    vmem = pl.BlockSpec(memory_space=pltpu.VMEM)
    smem = pl.BlockSpec(memory_space=pltpu.SMEM)
    arrays = pl.pallas_call(
        lambda *refs: layer_kernel(n, names, *refs),
        out_shape=[jax.ShapeDtypeStruct(like.shape, wide) for like in results.values()],
        in_specs=[smem if name == "lengths" else vmem for name in given],
        out_specs=[vmem] * len(results),
        scratch_shapes=list(scratch.values()),
        compiler_params=pltpu.CompilerParams(
            collective_id=20, has_side_effects=True, vmem_limit_bytes=62 * 2**20
        ),
        name="layer",
    )(*given.values())
    return settle(arrays)


def on_device(
    inputs,
    cotangent,
    lengths,
    attn_weights,
    attn_momenta,
    ffn_weights,
    ffn_momenta,
    vectors,
    vector_momenta,
):
    group_count = lax.axis_size("group")
    dp_count = lax.axis_size("dp")
    if dp_count == 8 and group_count == 4 and ffn_weights.shape[2] == inputs.shape[1]:
        return whole_layer(
            inputs=inputs,
            cotangent=cotangent,
            lengths=lengths,
            attn_weights=attn_weights,
            attn_momenta=attn_momenta,
            ffn_weights=ffn_weights,
            ffn_momenta=ffn_momenta,
            vectors=vectors,
            vector_momenta=vector_momenta,
        )
    own_index = lax.axis_index("group")
    dp_index = lax.axis_index("dp")
    token_count, width = inputs.shape
    own_count = attn_weights.shape[1]
    quarter = ffn_weights.shape[2]
    head_size = width // HEADS
    scale = 1.0 / math.sqrt(head_size)
    bf16 = jnp.bfloat16

    own_attn = attn_weights.astype(bf16)
    own_ffn = ffn_weights.astype(bf16)
    cotan_b = cotangent.astype(bf16)
    attn_full, ffn_full, all_cotan = exchange((("chain", 4), own_attn[0]), ("dprow", own_ffn), ("zag", cotan_b)
    )
    w_query, w_key, w_value, w_output = [attn_full[i] for i in range(4)]
    w_expand, w_reduce = [ffn_full[i] for i in range(2)]
    all_cotan = all_cotan.reshape(-1, width)

    positions = jnp.arange(token_count, dtype=jnp.int32)
    order = jnp.arange(lengths.shape[1], dtype=jnp.int32)
    seq_ends = jnp.sum(jnp.where(order[:, None] <= order[None, :], lengths[0][:, None], 0), axis=0)
    segment = jnp.sum((positions[:, None] >= seq_ends[None, :]).astype(jnp.int32), axis=1)
    allowed = (segment[:, None] == segment[None, :]) & (positions[None, :] <= positions[:, None])
    normed_first, inverse_first = norm_forward(inputs)
    hidden_first = (normed_first * vectors[0] + vectors[1]).astype(bf16)
    query = ((mm(hidden_first, w_query, NN) + vectors[2]) * scale).astype(bf16)
    keyed = mm(hidden_first, w_key, NN).astype(bf16)
    valued = (mm(hidden_first, w_value, NN) + vectors[3]).astype(bf16)
    query_heads = query.reshape(token_count, HEADS, head_size)
    key_heads = keyed.reshape(token_count, HEADS, head_size)
    value_heads = valued.reshape(token_count, HEADS, head_size)
    scores = masked_scores(query_heads, key_heads, allowed)
    highest = jnp.max(scores, axis=2, keepdims=True)
    log_total = highest + jnp.log(jnp.sum(jnp.exp(scores - highest), axis=2, keepdims=True))
    probs = jnp.exp(scores - log_total)
    probs_b = probs.astype(bf16)
    attended = jnp.einsum("hqk,khd->qhd", probs_b, value_heads, preferred_element_type=jnp.float32)
    attended = attended.reshape(token_count, width).astype(bf16)
    middle = inputs + mm(attended, w_output, NN) + vectors[4]
    normed_second, inverse_second = norm_forward(middle)
    hidden_second = (normed_second * vectors[5] + vectors[6]).astype(bf16)

    (all_second,) = exchange(("zag", hidden_second))
    all_second = all_second.reshape(-1, width)
    own_bias = lax.dynamic_slice_in_dim(vectors[8:].reshape(-1), own_index * quarter, quarter, 0)
    before = mm(all_second, w_expand, NN) + own_bias
    active = jnp.maximum(before, 0.0).astype(bf16)
    out_part = mm(active, w_reduce, NT).astype(bf16)
    grad_before = jnp.where(before > 0.0, mm(all_cotan, w_reduce, NN), 0.0)
    before_grad_b = grad_before.astype(bf16)
    second_part = mm(before_grad_b, w_expand, NT).astype(bf16)

    ffn_terms = jnp.stack(
        [mm(all_second, before_grad_b, TN).astype(bf16), mm(all_cotan, active, TN).astype(bf16)]
    )
    second_parts, ffn_total = exchange(
        ("za2a", second_part.reshape(group_count, token_count, width)),
        ("dpscatter", ffn_terms),
    )
    total_tokens = float(token_count * dp_count * group_count)
    ffn_grads = ffn_total / total_tokens
    ffn_next = momentum_rate * ffn_momenta + ffn_grads
    ffn_next_b = ffn_next.astype(bf16)
    grad_second = jnp.sum(second_parts.astype(jnp.float32), axis=0)
    grad_middle = cotangent + norm_backward(
        grad_second * vectors[5], normed_second, inverse_second
    )
    middle_b = grad_middle.astype(bf16)
    grad_attended = mm(middle_b, w_output, NT).astype(bf16)
    attended_heads = grad_attended.reshape(token_count, HEADS, head_size)
    grad_probs = jnp.einsum(
        "qhd,khd->hqk", attended_heads, value_heads, preferred_element_type=jnp.float32
    )
    grad_value = jnp.einsum(
        "hqk,qhd->khd", probs_b, attended_heads, preferred_element_type=jnp.float32
    )
    delta = jnp.sum(probs * grad_probs, axis=2, keepdims=True)
    grad_scores = (probs * (grad_probs - delta)).astype(bf16)
    grad_query = (
        jnp.einsum("hqk,khd->qhd", grad_scores, key_heads, preferred_element_type=jnp.float32)
        * scale
    )
    grad_key = jnp.einsum(
        "hqk,qhd->khd", grad_scores, query_heads, preferred_element_type=jnp.float32
    )
    query_grad = grad_query.reshape(token_count, width)
    key_grad = grad_key.reshape(token_count, width)
    value_grad = grad_value.reshape(token_count, width)
    query_grad_b = query_grad.astype(bf16)
    key_grad_b = key_grad.astype(bf16)
    value_grad_b = value_grad.astype(bf16)

    attn_terms = jnp.stack(
        [
            mm(hidden_first, query_grad_b, TN).astype(bf16),
            mm(hidden_first, key_grad_b, TN).astype(bf16),
            mm(hidden_first, value_grad_b, TN).astype(bf16),
            mm(attended, middle_b, TN).astype(bf16),
        ]
    )
    attn_sums, out_parts = exchange(
        ("dpscatter", attn_terms),
        ("za2a", out_part.reshape(group_count, token_count, width)),
    )
    outputs = middle + jnp.sum(out_parts.astype(jnp.float32), axis=0) + vectors[7]
    grad_first = (
        mm(query_grad_b, w_query, NT) + mm(key_grad_b, w_key, NT) + mm(value_grad_b, w_value, NT)
    )
    input_grad = grad_middle + norm_backward(grad_first * vectors[0], normed_first, inverse_first)
    small_terms = jnp.stack(
        [
            jnp.sum(grad_first * normed_first, axis=0),
            jnp.sum(grad_first, axis=0),
            jnp.sum(query_grad, axis=0),
            jnp.sum(value_grad, axis=0),
            jnp.sum(grad_middle, axis=0),
            jnp.sum(grad_second * normed_second, axis=0),
            jnp.sum(grad_second, axis=0),
            jnp.sum(cotangent, axis=0),
        ]
    )
    owner_mask = jnp.arange(group_count, dtype=jnp.int32) == own_index
    bias_terms = jnp.where(owner_mask[:, None], jnp.sum(grad_before, axis=0)[None], 0.0)
    vector_terms = jnp.concatenate([small_terms, bias_terms.reshape(-1, width)], axis=0)
    def square_sums(own):
        sums = jnp.sum(own * own, axis=(1, 2))
        return jnp.broadcast_to(jnp.pad(sums, (0, 8 - own.shape[0]))[:, None], (8, 128))

    attn_pieces, ffn_full_next, vector_all, ffn_squares = exchange(
        ("za2a", attn_sums.astype(bf16)),
        ("dprow", ffn_next_b),
        ("dpag", vector_terms),
        ("dpag", square_sums(ffn_next)),
    )
    attn_grads = jnp.sum(attn_pieces.astype(jnp.float32), axis=0, keepdims=True) / total_tokens
    attn_next = momentum_rate * attn_momenta + attn_grads
    gram_part = jnp.concatenate(
        [mm(ffn_next_b[0], ffn_full_next[0], NT), mm(ffn_next_b[1], ffn_full_next[1], NT)]
    )
    piece = 2 * own_count // group_count
    attn_full_next, gram_pieces, attn_squares, ffn_squares, vector_groups = exchange(
        ("dprow", attn_next.astype(bf16)),
        ("za2a", gram_part.astype(bf16).reshape(group_count, piece, width)),
        ("dpag", square_sums(attn_next)),
        ("zag", jnp.sum(ffn_squares, axis=0)),
        ("zag", jnp.sum(vector_all, axis=0)),
    )
    gram_piece = jnp.sum(gram_pieces.astype(jnp.float32), axis=0).astype(bf16)
    (gram_full,) = exchange((("chain", 2), gram_piece))
    attn_square = jnp.sum(attn_squares, axis=0)[:1, 0]
    ffn_square = jnp.sum(ffn_squares, axis=0)[:2, 0]
    scales = 1.0 / (jnp.sqrt(jnp.concatenate([attn_square, ffn_square])) + 1e-07)
    new_weights = newton_schulz(
        scales,
        dp_index * own_count,
        attn_full_next[0],
        ffn_full_next,
        gram_full,
        jnp.concatenate([attn_next, ffn_next], axis=0),
        jnp.concatenate([attn_weights, ffn_weights], axis=0),
    )
    new_attn_weights = new_weights[:1]
    new_ffn_weights = new_weights[1:]
    vector_grads = jnp.sum(vector_groups, axis=0) / total_tokens
    new_vector_momenta = momentum_rate * vector_momenta + vector_grads
    mean_square = jnp.mean(new_vector_momenta * new_vector_momenta, axis=1, keepdims=True)
    new_vectors = vectors - vector_rate * new_vector_momenta * lax.rsqrt(mean_square + 1e-06)
    return (
        outputs,
        input_grad,
        attn_grads,
        ffn_grads,
        vector_grads,
        new_attn_weights,
        attn_next,
        new_ffn_weights,
        ffn_next,
        new_vectors,
        new_vector_momenta,
    )


def solution(mesh):
    in_specs = (
        P(("dp", "group"), None),
        P(("dp", "group"), None),
        P(("dp", "group"), None),
        P("group", "dp", None),
        P("group", "dp", None),
        P(None, "dp", "group"),
        P(None, "dp", "group"),
        P(),
        P(),
    )
    out_specs = (
        P(("dp", "group"), None),
        P(("dp", "group"), None),
        P("group", "dp", None),
        P(None, "dp", "group"),
        P(),
        P("group", "dp", None),
        P("group", "dp", None),
        P(None, "dp", "group"),
        P(None, "dp", "group"),
        P(),
        P(),
    )
    return jax.shard_map(
        on_device, mesh=mesh, in_specs=in_specs, out_specs=out_specs, check_vma=False
    )
```

```python
import math
import types

import jax
import jax.numpy as jnp
from jax import lax
from jax.experimental import pallas as pl
from jax.experimental.pallas import tpu as pltpu
from jax.sharding import PartitionSpec as P

HEADS = 12
NS_ITERS = 3


coef_first = 3.4445
coef_second = -4.775
coef_third = 2.0315
momentum_rate = 0.9
muon_rate = 0.8
vector_rate = 0.1


def norm_forward(rows):
    centre = jnp.mean(rows, axis=1, keepdims=True)
    centred = rows - centre
    variance = jnp.mean(centred * centred, axis=1, keepdims=True)
    inverse = lax.rsqrt(variance + 1e-05)
    return (centred * inverse, inverse)


def norm_backward(grad_normed, normed, inverse):
    return inverse * (
        grad_normed
        - jnp.mean(grad_normed, axis=1, keepdims=True)
        - normed * jnp.mean(grad_normed * normed, axis=1, keepdims=True)
    )


def masked_scores(query_heads, key_heads, allowed):
    scores = jnp.einsum("qhd,khd->hqk", query_heads, key_heads, preferred_element_type=jnp.float32)
    return jnp.where(allowed[None], scores, -jnp.inf)


MESH = pl.DeviceIdType.MESH


def flip(index, bits):
    result = index
    for bit in (1, 2, 4):
        if bits & bit:
            result = result + bit - 2 * bit * ((index // bit) % 2)
    return result


def exchange(*pairs):
    results = []
    for kind, x in pairs:
        if kind == "zag":
            results.append(lax.all_gather(x, "group", axis=0))
        elif kind == "za2a":
            results.append(lax.all_to_all(x, "group", 0, 0))
        elif kind == "dpag":
            results.append(lax.all_gather(x, "dp", axis=0))
        elif kind == "dprow":
            results.append(lax.all_gather(x, "dp", axis=1, tiled=True))
        elif kind == "dpscatter":
            wide = x.astype(jnp.float32)
            results.append(lax.psum_scatter(wide, "dp", scatter_dimension=1, tiled=True))
        else:
            held = lax.all_gather(x, "group", axis=0).reshape(kind[1], -1, x.shape[1])
            results.append(lax.all_gather(held, "dp", axis=1, tiled=True))
    return results


def mm(left, right, dims):
    return lax.dot_general(left, right, (dims, ((), ())), preferred_element_type=jnp.float32)


NN = ((1,), (0,))
NT = ((1,), (1,))
TN = ((0,), (0,))


def newton_schulz_kernel(
    scale_ref,
    start_ref,
    attn_ref,
    ffn_ref,
    gram_ref,
    own_ref,
    weight_ref,
    out_ref,
    gram,
    gram_b,
    mixed,
    mixed_b,
    half,
    half_b,
):
    rows = own_ref.shape[1]
    mine = pl.ds(pl.multiple_of(start_ref[0], 8), rows)
    bf16 = jnp.bfloat16

    def one(index, whole_b):
        scale = scale_ref[index]
        lead = 1.0
        spread = None
        for iteration in range(NS_ITERS - 1):
            gram_b[...] = gram[...].astype(bf16)
            mixed[...] = coef_second * gram[...] + coef_third * mm(gram_b[...], gram_b[...], NN)
            mixed_b[...] = mixed[...].astype(bf16)
            half[...] = coef_first * gram[...] + mm(mixed_b[...], gram_b[...], NN)
            half_b[...] = half[...].astype(bf16)
            gram[...] = coef_first * half[...] + mm(half_b[...], mixed_b[...], NN)
            if spread is None:
                spread = mixed[mine, :]
            else:
                product = mm(spread.astype(bf16), mixed_b[...], NN)
                spread = coef_first * spread + lead * mixed[mine, :] + product
            lead = lead * coef_first
        gram_b[...] = gram[...].astype(bf16)
        once = lead * gram[mine, :] + mm(spread.astype(bf16), gram_b[...], NN)
        twice = mm(once.astype(bf16), gram_b[...], NN)
        spread = coef_first * spread + coef_second * once + coef_third * twice
        lead = lead * coef_first
        moved = lead * own_ref[index] + mm(spread.astype(bf16), whole_b, NN)
        out_ref[index] = weight_ref[index] - (muon_rate * scale) * moved

    gram[...] = mm(attn_ref[...], attn_ref[...], NT) * (scale_ref[0] * scale_ref[0])
    one(0, attn_ref[...])

    @pl.loop(0, gram_ref.shape[0])
    def _(i):
        gram[...] = gram_ref[i].astype(jnp.float32) * (scale_ref[i + 1] * scale_ref[i + 1])
        one(i + 1, ffn_ref[i])


def newton_schulz(scales, row_start, attn_b, ffn_b, grams, own, weights):
    side = attn_b.shape[0]
    vmem = pl.BlockSpec(memory_space=pltpu.VMEM)
    smem = pl.BlockSpec(memory_space=pltpu.SMEM)
    wide, narrow = pltpu.VMEM((side, side), jnp.float32), pltpu.VMEM((side, side), jnp.bfloat16)
    return pl.pallas_call(
        newton_schulz_kernel,
        out_shape=jax.ShapeDtypeStruct(own.shape, jnp.float32),
        in_specs=[smem, smem, vmem, vmem, vmem, vmem, vmem],
        out_specs=vmem,
        scratch_shapes=[wide, narrow] * 3,
        compiler_params=pltpu.CompilerParams(vmem_limit_bytes=48 * 2**20),
        name="newton_schulz",
    )(scales, jnp.reshape(row_start, (1,)), attn_b, ffn_b, grams, own, weights)


class Net:
    def __init__(self, send_sem, recv_sem, z, d, n):
        self.send_sem, self.recv_sem = send_sem, recv_sem
        self.z, self.d, self.n = z, d, n
        self.slot = 0
        self.copies = []
        self.to_core = {"dp": flip(d, 1)}
        self.to_x = {"dp": flip(d, 2)}
        self.to_y = {"dp": flip(d, 4)}

    def send(self, src, dst, device):
        copy = pltpu.make_async_remote_copy(
            src_ref=src,
            dst_ref=dst,
            send_sem=self.send_sem.at[self.slot],
            recv_sem=self.recv_sem.at[self.slot],
            device_id=device,
            device_id_type=MESH,
        )
        self.slot += 1
        copy.start()
        self.copies.append(copy)
        return copy

    def up(self, k):
        return lax.rem(self.z + k, self.n)

    def down(self, k):
        return lax.rem(self.z + self.n - k, self.n)

    def line(self, src, dst):
        return [self.send(src, dst, {"group": self.up(k)}) for k in range(1, self.n)]

    def plane(self, src, dst):
        return [self.send(src, dst, {"dp": flip(self.d, k)}) for k in range(1, 8)]

    def finish(self):
        for copy in self.copies:
            copy.wait_send()


class Relay:
    def __init__(self, net, blocks):
        self.net, self.blocks, self.base = net, blocks, net.slot
        net.slot += 2 * (net.n - 1)
        self.each(0, lambda copy: copy.start())

    def copy(self, way, steps, origin):
        net = self.net
        slot = self.base + steps + (net.n - 1) * (way < 0)
        return pltpu.make_async_remote_copy(
            src_ref=self.blocks.at[origin],
            dst_ref=self.blocks.at[origin],
            send_sem=net.send_sem.at[slot],
            recv_sem=net.recv_sem.at[slot],
            device_id={"group": net.z + way},
            device_id_type=MESH,
        )

    def each(self, steps, act):
        net = self.net
        z, last = net.z, net.n - 1
        if steps < last:
            pl.when((z >= steps) & (z < last))(lambda: act(self.copy(1, steps, z - steps)))
            pl.when((z + steps <= last) & (z > 0))(lambda: act(self.copy(-1, steps, z + steps)))

    def step(self, steps):
        net = self.net
        z = net.z
        pl.when(z >= steps)(lambda: self.copy(1, steps - 1, z - steps).wait_recv())
        pl.when(z + steps < net.n)(lambda: self.copy(-1, steps - 1, z + steps).wait_recv())
        self.each(steps, lambda copy: copy.start())

    def finish(self):
        for steps in range(self.net.n - 1):
            self.each(steps, lambda copy: copy.wait_send())


class Gather:
    def __init__(self, net, src, full, rows):
        self.net, self.full, self.rows = net, full, rows
        place = self.place(net.d)
        self.x = net.send(src, place, net.to_x)
        self.y = net.send(src, place, net.to_y)
        self.core = net.send(src, place, net.to_core)

    def place(self, index, part=None):
        first = self.rows // 32 * 16
        start, size = index * self.rows, self.rows
        if part is not None:
            start = start + part * first
            size = (first, self.rows - first)[part]
        return self.full.at[pl.ds(pl.multiple_of(start, 16), size), :]

    def second(self):
        net = self.net
        from_x, from_y = flip(net.d, 2), flip(net.d, 4)
        self.x.wait_recv()
        self.via_y = net.send(self.place(from_x, 0), self.place(from_x, 0), net.to_y)
        self.share_x = net.send(self.place(from_x), self.place(from_x), net.to_core)
        self.y.wait_recv()
        self.via_x = net.send(self.place(from_y, 1), self.place(from_y, 1), net.to_x)
        self.share_y = net.send(self.place(from_y), self.place(from_y), net.to_core)

    def third(self):
        net = self.net
        far = flip(net.d, 6)
        self.via_y.wait_recv()
        self.via_x.wait_recv()
        self.share_far = net.send(self.place(far), self.place(far), net.to_core)

    def end(self):
        for copy in (self.core, self.share_x, self.share_y, self.share_far):
            copy.wait_recv()


class Scatter:
    def __init__(self, net, x, near, total, recv_b, recv_c, part):
        self.net, self.x, self.rows = net, x, x.shape[0] // 8
        self.near, self.total, self.recv_b, self.recv_c, self.part = near, total, recv_b, recv_c, part
        self.copies = [
            net.send(self.block(2 * r + 1), near.at[r], net.to_core) for r in (3, 1, 2, 0)
        ]

    def block(self, bits):
        start = pl.multiple_of(flip(self.net.d, bits) * self.rows, 16)
        return self.x.at[pl.ds(start, self.rows), :]

    def second(self):
        net, total = self.net, self.total
        wide = jnp.float32
        half = self.rows // 2
        low, high = pl.ds(0, half), pl.ds(half, half)
        for r, copy in zip((3, 1, 2, 0), self.copies):
            copy.wait_recv()
            own = self.block(2 * r)[...].astype(wide)
            total[r] = (own + self.near[r].astype(wide)).astype(total.dtype)
        self.moved = [
            net.send(total.at[3, low], self.recv_b.at[1], net.to_x),
            net.send(total.at[3, high], self.recv_b.at[3], net.to_y),
            net.send(total.at[1, low], self.recv_b.at[0], net.to_x),
            net.send(total.at[2, high], self.recv_b.at[2], net.to_y),
        ]

    def third(self):
        net, total, part = self.net, self.total, self.part
        wide = jnp.float32
        half = self.rows // 2
        low, high = pl.ds(0, half), pl.ds(half, half)
        self.moved[0].wait_recv()
        part[0] = (total[2, low].astype(wide) + self.recv_b[1].astype(wide)).astype(part.dtype)
        self.ends = [net.send(part.at[0], self.recv_c.at[0], net.to_y)]
        self.moved[1].wait_recv()
        part[1] = (total[1, high].astype(wide) + self.recv_b[3].astype(wide)).astype(part.dtype)
        self.ends.append(net.send(part.at[1], self.recv_c.at[1], net.to_x))

    def end(self):
        total = self.total
        wide = jnp.float32
        half = self.rows // 2
        low, high = pl.ds(0, half), pl.ds(half, half)
        self.moved[2].wait_recv()
        self.moved[3].wait_recv()
        self.ends[0].wait_recv()
        self.ends[1].wait_recv()
        first = total[0, low].astype(wide) + self.recv_b[0].astype(wide) + self.recv_c[0].astype(wide)
        second = total[0, high].astype(wide) + self.recv_b[2].astype(wide) + self.recv_c[1].astype(wide)
        return jnp.concatenate([first, second], axis=0)


def muon_steps(gram, gram_b, mixed_b, half_b, mine, finish):
    bf16 = jnp.bfloat16
    lead = 1.0
    spread = None
    for iteration in range(NS_ITERS - 1):
        gram_b[...] = gram[...].astype(bf16)
        own_gram = gram[mine, :]
        mixed_b[...] = (coef_second * gram[...] + coef_third * mm(gram_b[...], gram_b[...], NN)).astype(
            bf16
        )
        yield
        own_mixed = coef_second * own_gram + coef_third * mm(own_gram.astype(bf16), gram_b[...], NN)
        gram[...] = coef_first * gram[...] + mm(mixed_b[...], gram_b[...], NN)
        half_b[...] = gram[...].astype(bf16)
        yield
        gram[...] = coef_first * gram[...] + mm(half_b[...], mixed_b[...], NN)
        if spread is None:
            spread = own_mixed
        else:
            product = mm(spread.astype(bf16), mixed_b[...], NN)
            spread = coef_first * spread + lead * own_mixed + product
        lead = lead * coef_first
        yield
    gram_b[...] = gram[...].astype(bf16)
    once = lead * gram[mine, :] + mm(spread.astype(bf16), gram_b[...], NN)
    twice = mm(once.astype(bf16), gram_b[...], NN)
    spread = coef_first * spread + coef_second * once + coef_third * twice
    lead = lead * coef_first
    finish(spread.astype(bf16), lead)
    yield


def layer_kernel(n, names, *refs):
    ref = types.SimpleNamespace(**dict(zip(names, refs)))
    bf16, wide = jnp.bfloat16, jnp.float32
    z, d = lax.axis_index("group"), lax.axis_index("dp")
    net = Net(ref.send_sem, ref.recv_sem, z, d, n)
    lengths, vectors = ref.lengths, ref.vectors
    tokens, width = ref.inputs.shape
    rows = ref.attn_weights.shape[1]
    head_size = width // HEADS
    pairs = HEADS // 2
    pair_width = 2 * head_size
    scale = 1.0 / math.sqrt(head_size)
    total_tokens = float(tokens * 8 * n)
    ranks = range(1, n)

    def vector(i):
        return vectors[pl.ds(i, 1), :]

    def column_sum(x):
        return jnp.sum(x, axis=0, keepdims=True)

    barrier = pltpu.get_barrier_semaphore()
    for k in ranks:
        pl.semaphore_signal(barrier, inc=1, device_id={"group": net.up(k)}, device_id_type=MESH)
    for k in range(1, 8):
        pl.semaphore_signal(barrier, inc=1, device_id={"dp": flip(d, k)}, device_id_type=MESH)

    own_attn, own_ffn = ref.own_attn, ref.own_ffn
    held, attn_full, ffn_full = ref.held, ref.attn_full, ref.ffn_full
    own_attn[...] = ref.attn_weights[0].astype(bf16)
    all_cotan, all_second = ref.all_cotan, ref.all_second
    all_cotan[z] = ref.cotangent[...].astype(bf16)
    own_ffn[...] = ref.ffn_weights[...].astype(bf16)

    pl.semaphore_wait(barrier, n - 1 + 7)

    chain = net.line(own_attn, held.at[z])
    own_rows = pl.ds(pl.multiple_of(d * rows, 16), rows)

    weights = [Gather(net, own_attn, attn_full.at[z], rows)]
    ffn_weights = [Gather(net, own_ffn.at[i], ffn_full.at[i], rows) for i in range(2)]
    for i in range(2):
        ffn_full[i, own_rows, :] = own_ffn[i]
    attn_full[z, own_rows, :] = own_attn[...]

    centre = jnp.mean(ref.inputs[...], axis=1, keepdims=True)
    centred = ref.inputs[...] - centre
    inverse_first = lax.rsqrt(jnp.mean(centred * centred, axis=1, keepdims=True) + 1e-05)
    ref.normed_first[...] = centred * inverse_first
    hidden_first, attended = ref.hidden_first, ref.attended
    hidden_first[...] = (ref.normed_first[...] * vector(0) + vector(1)).astype(bf16)

    for k in ranks:
        origin = net.down(k)
        chain[k - 1].wait_recv()
        weights.append(Gather(net, held.at[origin], attn_full.at[origin], rows))
        attn_full[origin, own_rows, :] = held[origin]
        if k == 1:
            weights[0].second()
    cotan_copies = net.line(all_cotan.at[z], all_cotan.at[z])
    for gather in weights[1:]:
        gather.second()
    for gather in weights:
        gather.third()
    for gather in ffn_weights:
        gather.second()
    for gather in weights:
        gather.end()
    for gather in ffn_weights:
        gather.third()

    lane = lax.broadcasted_iota(jnp.int32, (tokens, pair_width), 1)
    low_lane = lane < head_size
    ones = lax.broadcasted_iota(jnp.int32, (1, pair_width), 1) < head_size
    low_mask = jnp.where(ones, 1.0, 0.0).astype(bf16)
    high_mask = jnp.where(ones, 0.0, 1.0).astype(bf16)

    def split(x):
        return jnp.concatenate([x * low_mask, x * high_mask], axis=0)

    def join(x):
        return jnp.where(low_lane, x[:tokens], x[tokens:])

    query, keyed, valued = ref.query, ref.keyed, ref.valued
    query[...] = ((mm(hidden_first[...], attn_full[0], NN) + vector(2)) * scale).astype(bf16)
    keyed[...] = mm(hidden_first[...], attn_full[1], NN).astype(bf16)
    valued[...] = (mm(hidden_first[...], attn_full[2], NN) + vector(3)).astype(bf16)

    at_row = lax.broadcasted_iota(jnp.int32, (2 * tokens, tokens), 0)
    at_row = jnp.where(at_row < tokens, at_row, at_row - tokens)
    at_column = lax.broadcasted_iota(jnp.int32, (2 * tokens, tokens), 1)
    row_part = jnp.zeros_like(at_row)
    column_part = jnp.zeros_like(at_column)
    edge = 0
    for i in range(lengths.shape[1]):
        edge = edge + lengths[0, i]
        row_part = row_part + jnp.where(at_row >= edge, 1, 0)
        column_part = column_part + jnp.where(at_column >= edge, 1, 0)
    allowed = (row_part == column_part) & (at_column <= at_row)

    probs = ref.probs
    slices = [pl.ds(p * pair_width, pair_width) for p in range(pairs)]
    for p, lanes in enumerate(slices):
        scores = mm(split(query[:, lanes]), keyed[:, lanes], NT)
        probs[p] = jnp.where(allowed, scores, -jnp.inf)
    for p in range(pairs):
        raised = jnp.exp(probs[p] - jnp.max(probs[p], axis=1, keepdims=True))
        probs[p] = raised * (1.0 / jnp.sum(raised, axis=1, keepdims=True))
    for p, lanes in enumerate(slices):
        attended[:, lanes] = join(mm(probs[p].astype(bf16), valued[:, lanes], NN)).astype(bf16)

    middle = ref.middle
    middle[...] = ref.inputs[...] + mm(attended[...], attn_full[3], NN) + vector(4)
    centre = jnp.mean(middle[...], axis=1, keepdims=True)
    centred = middle[...] - centre
    inverse_second = lax.rsqrt(jnp.mean(centred * centred, axis=1, keepdims=True) + 1e-05)
    normed_second = ref.normed_second
    normed_second[...] = centred * inverse_second
    all_second[z] = (normed_second[...] * vector(5) + vector(6)).astype(bf16)
    relay = Relay(net, all_second)
    for gather in ffn_weights:
        gather.end()

    active, before_grad = ref.active, ref.before_grad
    grad_send, grad_recv, grad_own = ref.grad_send, ref.grad_recv, ref.grad_own
    out_send, out_recv, out_own = ref.out_send, ref.out_recv, ref.out_own
    bias_sum = ref.bias_sum
    bias_sum[...] = jnp.zeros_like(bias_sum)
    grad_slot = net.slot
    net.slot += n

    def grad_copy(origin, sender):
        return pltpu.make_async_remote_copy(
            src_ref=grad_send.at[origin],
            dst_ref=grad_recv.at[sender],
            send_sem=net.send_sem.at[grad_slot + origin],
            recv_sem=net.recv_sem.at[grad_slot + sender],
            device_id={"group": origin},
            device_id_type=MESH,
        )

    def feed_forward(origin, own):
        before = mm(all_second[origin], ffn_full[0], NN) + vector(8 + z)
        active[origin] = jnp.maximum(before, 0.0).astype(bf16)
        grad_before = jnp.where(before > 0.0, mm(all_cotan[origin], ffn_full[1], NN), 0.0)
        bias_sum[...] = bias_sum[...] + column_sum(grad_before)
        before_grad[origin] = grad_before.astype(bf16)
        second = mm(before_grad[origin], ffn_full[0], NT)
        if own:
            grad_own[...] = second
        else:
            grad_send[origin] = second.astype(bf16)
            grad_copy(origin, z).start()
        out = mm(active[origin], ffn_full[1], NT)
        if own:
            out_own[...] = out
        else:
            out_send[origin] = out.astype(bf16)

    feed_forward(z, True)
    for copy in cotan_copies:
        copy.wait_recv()
    for steps in ranks:
        relay.step(steps)
        pl.when(z >= steps)(lambda: feed_forward(z - steps, False))
        pl.when(z + steps < n)(lambda: feed_forward(z + steps, False))

    def scatter(x, slot):
        pools = (ref.near, ref.total, ref.recv_b, ref.recv_c, ref.part)
        return Scatter(net, x, *[pool.at[slot] for pool in pools])

    ffn_terms, attn_terms = ref.ffn_terms, ref.attn_terms
    many = n * tokens
    ffn_terms[0] = mm(
        all_second[...].reshape(many, width), before_grad[...].reshape(many, width), TN
    ).astype(bf16)
    ffn_sums = [scatter(ffn_terms.at[0], 0)]
    ffn_terms[1] = mm(
        all_cotan[...].reshape(many, width), active[...].reshape(many, width), TN
    ).astype(bf16)
    ffn_sums.append(scatter(ffn_terms.at[1], 1))
    for part in ffn_sums:
        part.second()
    for part in ffn_sums:
        part.third()

    next_own, next_full = ref.next_own, ref.next_full
    ffn_squares, attn_squares = ref.ffn_squares, ref.attn_squares

    def square(x):
        return jnp.broadcast_to(jnp.sum(column_sum(x * x), axis=1, keepdims=True), (8, 128))

    ffn_nexts = []
    for i in range(2):
        grad = ffn_sums[i].end() / total_tokens
        ref.ffn_grads[i] = grad
        moment = momentum_rate * ref.ffn_momenta[i] + grad
        ref.new_ffn_momenta[i] = moment
        next_own[1 + i] = moment.astype(bf16)
        ffn_nexts.append(Gather(net, next_own.at[1 + i], next_full.at[1 + i], rows))
        next_full[1 + i, own_rows, :] = next_own[1 + i]
        ffn_squares[0, i] = square(moment)
    square_copies = net.plane(ffn_squares.at[0], ref.ffn_squares_in.at[d])

    total = grad_own[...]
    for k in ranks:
        grad_copy(z, net.up(k)).wait_recv()
        total = total + grad_recv[net.up(k)].astype(wide)
    out_copies = [
        net.send(out_send.at[net.down(k)], out_recv.at[k - 1], {"group": net.down(k)}) for k in ranks
    ]
    terms = ref.vector_terms
    terms[...] = jnp.zeros_like(terms)

    def put(i, x):
        terms[pl.ds(i, 1), :] = x

    def norm_back(grad, normed, inverse):
        return inverse * (
            grad
            - jnp.mean(grad, axis=1, keepdims=True)
            - normed * jnp.mean(grad * normed, axis=1, keepdims=True)
        )

    put(8 + z, bias_sum[...])
    put(5, column_sum(total * normed_second[...]))
    put(6, column_sum(total))
    put(7, column_sum(ref.cotangent[...]))
    grad_middle = ref.grad_middle
    grad_middle[...] = ref.cotangent[...] + norm_back(
        total * vector(5), normed_second[...], inverse_second
    )
    put(4, column_sum(grad_middle[...]))
    middle_b = ref.middle_b
    middle_b[...] = grad_middle[...].astype(bf16)
    attn_terms[3] = mm(attended[...], middle_b[...], TN).astype(bf16)
    attn_sums = [scatter(attn_terms.at[3], 5)]
    grad_attended = ref.grad_attended
    grad_attended[...] = mm(middle_b[...], attn_full[3], NT).astype(bf16)
    grads = [ref.query_grad, ref.key_grad, ref.value_grad]
    pulls, pushes = ref.grad_probs, ref.grad_scores
    for p, lanes in enumerate(slices):
        pulls[p] = mm(split(grad_attended[:, lanes]), valued[:, lanes], NT)
    for p in range(pairs):
        delta = jnp.sum(probs[p] * pulls[p], axis=1, keepdims=True)
        pushes[p] = (probs[p] * (pulls[p] - delta)).astype(bf16)
    for gather in ffn_nexts:
        gather.second()
    attn_sums[0].second()
    for p, lanes in enumerate(slices):
        grad_value = mm(probs[p].astype(bf16), split(grad_attended[:, lanes]), TN)
        grad_query = join(mm(pushes[p], keyed[:, lanes], NN)) * scale
        grad_key = mm(pushes[p], split(query[:, lanes]), TN)
        terms[pl.ds(2, 1), lanes] = column_sum(grad_query)
        terms[pl.ds(3, 1), lanes] = column_sum(grad_value)
        grads[0][:, lanes] = grad_query.astype(bf16)
        grads[1][:, lanes] = grad_key.astype(bf16)
        grads[2][:, lanes] = grad_value.astype(bf16)
    for m in range(3):
        attn_terms[m] = mm(hidden_first[...], grads[m][...], TN).astype(bf16)
        attn_sums.append(scatter(attn_terms.at[m], 2 + m))
    for gather in ffn_nexts:
        gather.third()
    for part in attn_sums[1:]:
        part.second()
    attn_sums[0].third()

    gram_send, gram_recv = ref.gram_send, ref.gram_recv
    piece = 2 * rows // n
    for i in range(2):
        ffn_nexts[i].end()
        gram_send[pl.ds(i * rows, rows), :] = mm(next_own[1 + i], next_full[1 + i], NT).astype(bf16)

    def gram_rows(index):
        return gram_send.at[pl.ds(pl.multiple_of(index * piece, 16), piece), :]

    gram_copies = [
        net.send(gram_rows(net.up(k)), gram_recv.at[k - 1], {"group": net.up(k)}) for k in ranks
    ]

    grad_first = mm(grads[0][...], attn_full[0], NT)
    grad_first = grad_first + mm(grads[1][...], attn_full[1], NT)
    grad_first = grad_first + mm(grads[2][...], attn_full[2], NT)
    put(0, column_sum(grad_first * ref.normed_first[...]))
    put(1, column_sum(grad_first))
    ref.input_grad[...] = grad_middle[...] + norm_back(
        grad_first * vector(0), ref.normed_first[...], inverse_first
    )
    vector_in = ref.vector_in
    vector_copies = net.plane(terms, vector_in.at[d])

    for part in attn_sums[1:]:
        part.third()

    gram_sum = gram_rows(z)[...].astype(wide)
    for k in ranks:
        gram_copies[k - 1].wait_recv()
        gram_sum = gram_sum + gram_recv[k - 1].astype(wide)
    gram_all, gram_full = ref.gram_all, ref.gram_full
    per = n // 2
    own_piece = gram_all.at[z // per, pl.ds(pl.multiple_of(lax.rem(z, per) * piece, 16), piece), :]
    own_piece[...] = gram_sum.astype(bf16)
    gram_line = net.line(own_piece, own_piece)

    piece_send, piece_recv = ref.piece_send, ref.piece_recv
    for m, part in zip((3, 0, 1, 2), attn_sums):
        piece_send[m] = part.end().astype(bf16)
    piece_copies = [
        net.send(piece_send.at[net.up(k)], piece_recv.at[k - 1], {"group": net.up(k)}) for k in ranks
    ]

    plane_sum = ref.plane_sum
    square_in = ref.ffn_squares_in
    square_total = ffn_squares[0]
    for k in range(1, 8):
        square_copies[k - 1].wait_recv()
        square_total = square_total + square_in[flip(d, k)]
    ffn_squares[1] = square_total
    plane_squares = net.line(ffn_squares.at[1], ref.ffn_squares_all.at[z])
    vector_total = terms[...]
    for k in range(1, 8):
        vector_copies[k - 1].wait_recv()
        vector_total = vector_total + vector_in[flip(d, k)]
    plane_sum[...] = vector_total
    vector_all = net.line(plane_sum, ref.vector_all.at[z])

    for copy in gram_line:
        copy.wait_recv()
    grams = []
    for i in range(2):
        grams.append(Gather(net, gram_all.at[i], gram_full.at[i], rows))
        gram_full[i, own_rows, :] = gram_all[i]

    result = out_own[...] + middle[...] + vector(7)
    for k in ranks:
        out_copies[k - 1].wait_recv()
        result = result + out_recv[k - 1].astype(wide)
    ref.outputs[...] = result

    grad = piece_send[z].astype(wide)
    for k in ranks:
        piece_copies[k - 1].wait_recv()
        grad = grad + piece_recv[k - 1].astype(wide)
    grad = grad / total_tokens
    ref.attn_grads[0] = grad
    moment = momentum_rate * ref.attn_momenta[0] + grad
    ref.new_attn_momenta[0] = moment
    next_own[0] = moment.astype(bf16)
    attn_next = Gather(net, next_own.at[0], next_full.at[0], rows)
    next_full[0, own_rows, :] = next_own[0]
    attn_squares[0] = square(moment)
    own_squares = net.plane(attn_squares.at[0], ref.attn_squares_in.at[d])
    for gather in grams:
        gather.second()
    for gather in grams:
        gather.third()

    gram, gram_b, mixed_b, half_b = ref.gram, ref.gram_b, ref.mixed_b, ref.half_b

    def inverse_norm(x):
        return 1.0 / (jnp.sqrt(x[0:1, 0:1]) + 1e-07)

    square_total = ffn_squares[1]
    for k in ranks:
        plane_squares[k - 1].wait_recv()
        square_total = square_total + ref.ffn_squares_all[net.down(k)]

    square_sum = ref.square_sum
    square_sum[...] = square_total
    core = lax.rem(d, 2)
    both_rows = pl.ds(pl.multiple_of((d // 2) * 2 * rows, 16), 2 * rows)
    spread_all, spread_in = ref.spread_all, ref.spread_in
    leads = []

    def half_of(index):
        return spread_all.at[pl.ds(pl.multiple_of(index * rows, 16), rows), :]

    def exchange_spread(spread, lead):
        spread_all[...] = spread
        leads.append(lead)

    for gather in grams:
        gather.end()
    own_scale = inverse_norm(square_sum[core])
    gram[...] = gram_full[core].astype(wide) * (own_scale * own_scale)
    steps = muon_steps(gram, gram_b, mixed_b, half_b, both_rows, exchange_spread)
    next(steps)
    attn_next.second()
    next(steps)
    next(steps)
    attn_next.third()
    for _ in steps:
        pass
    spread_copy = net.send(half_of(1 - core), spread_in, net.to_core)

    def ffn_update(index, spread):
        own_scale = inverse_norm(square_sum[index])
        moved = leads[0] * ref.new_ffn_momenta[index] + mm(spread, next_full[1 + index], NN)
        ref.new_ffn_weights[index] = ref.ffn_weights[index] - (muon_rate * own_scale) * moved

    ffn_update(core, half_of(core)[...])

    vector_total = plane_sum[...]
    for k in ranks:
        vector_all[k - 1].wait_recv()
        vector_total = vector_total + ref.vector_all[net.down(k)]
    vector_total = vector_total / total_tokens
    ref.vector_grads[...] = vector_total
    moment = momentum_rate * ref.vector_momenta[...] + vector_total
    ref.new_vector_momenta[...] = moment
    mean_square = jnp.mean(moment * moment, axis=1, keepdims=True)
    ref.new_vectors[...] = vectors[...] - vector_rate * moment * lax.rsqrt(mean_square + 1e-06)

    attn_next.end()
    square_total = attn_squares[0]
    for k in range(1, 8):
        own_squares[k - 1].wait_recv()
        square_total = square_total + ref.attn_squares_in[flip(d, k)]
    own_scale = inverse_norm(square_total)
    gram[...] = mm(next_full[0], next_full[0], NT) * (own_scale * own_scale)
    own_muon = muon_rate * own_scale

    def attn_update(spread, lead):
        moved = lead * ref.new_attn_momenta[0] + mm(spread, next_full[0], NN)
        ref.new_attn_weights[0] = ref.attn_weights[0] - own_muon * moved

    for _ in muon_steps(gram, gram_b, mixed_b, half_b, own_rows, attn_update):
        pass
    spread_copy.wait_recv()
    ffn_update(1 - core, spread_in[...])
    relay.finish()
    for k in ranks:
        grad_copy(net.up(k), z).wait_send()
    net.finish()


def settle_kernel(count, *refs):
    for i in range(count):
        refs[count + i][...] = refs[i][...]


def settle(arrays):
    count = len(arrays)
    vmem = pl.BlockSpec(memory_space=pltpu.VMEM)
    return pl.pallas_call(
        lambda *refs: settle_kernel(count, *refs),
        out_shape=[jax.ShapeDtypeStruct(x.shape, x.dtype) for x in arrays],
        in_specs=[vmem] * count,
        out_specs=[vmem] * count,
        name="settle",
    )(*arrays)


def whole_layer(**given):
    inputs, vectors = given["inputs"], given["vectors"]
    attn_weights, ffn_weights = given["attn_weights"], given["ffn_weights"]
    results = dict(
        outputs=inputs,
        input_grad=inputs,
        attn_grads=attn_weights,
        ffn_grads=ffn_weights,
        vector_grads=vectors,
        new_attn_weights=attn_weights,
        new_attn_momenta=attn_weights,
        new_ffn_weights=ffn_weights,
        new_ffn_momenta=ffn_weights,
        new_vectors=vectors,
        new_vector_momenta=vectors,
    )
    n = lax.axis_size("group")
    tokens, width = inputs.shape
    rows = attn_weights.shape[1]
    side = 8 * rows
    piece = 2 * rows // n
    half = rows // 2
    bf16, wide = jnp.bfloat16, jnp.float32
    block = (tokens, width)
    narrow = dict(
        own_attn=(rows, width),
        own_ffn=(2, rows, width),
        held=(n, rows, width),
        attn_full=(n, side, width),
        ffn_full=(2, side, width),
        all_cotan=(n, *block),
        all_second=(n, *block),
        query=block,
        keyed=block,
        valued=block,
        active=(n, *block),
        before_grad=(n, *block),
        grad_send=(n, *block),
        grad_recv=(n, *block),
        out_send=(n, *block),
        out_recv=(n - 1, *block),
        ffn_terms=(2, side, width),
        attn_terms=(n, side, width),
        hidden_first=block,
        attended=block,
        middle_b=block,
        query_grad=block,
        key_grad=block,
        value_grad=block,
        piece_send=(n, rows, width),
        piece_recv=(n - 1, rows, width),
        grad_scores=(HEADS // 2, 2 * tokens, tokens),
        near=(6, 4, rows, width),
        total=(6, 4, rows, width),
        recv_b=(6, 4, half, width),
        recv_c=(6, 2, half, width),
        part=(6, 2, half, width),
        grad_attended=block,
        next_own=(3, rows, width),
        next_full=(3, side, width),
        gram_send=(2 * rows, side),
        gram_recv=(n - 1, piece, side),
        gram_all=(2, rows, side),
        gram_full=(2, side, side),
        spread_all=(2 * rows, side),
        spread_in=(rows, side),
        gram_b=(side, side),
        mixed_b=(side, side),
        half_b=(side, side),
    )
    full = dict(
        normed_first=block,
        middle=block,
        normed_second=block,
        probs=(HEADS // 2, 2 * tokens, tokens),
        grad_probs=(HEADS // 2, 2 * tokens, tokens),
        grad_own=block,
        out_own=block,
        grad_middle=block,
        vector_terms=vectors.shape,
        vector_in=(8, *vectors.shape),
        plane_sum=vectors.shape,
        vector_all=(n, *vectors.shape),
        ffn_squares=(2, 2, 8, 128),
        ffn_squares_in=(8, 2, 8, 128),
        ffn_squares_all=(n, 2, 8, 128),
        attn_squares=(1, 8, 128),
        square_sum=(2, 8, 128),
        bias_sum=(1, width),
        attn_squares_in=(8, 8, 128),
        gram=(side, side),
    )
    scratch = {name: pltpu.VMEM(shape, bf16) for name, shape in narrow.items()}
    scratch |= {name: pltpu.VMEM(shape, wide) for name, shape in full.items()}
    copies = 256
    scratch |= dict(
        send_sem=pltpu.SemaphoreType.DMA((copies,)),
        recv_sem=pltpu.SemaphoreType.DMA((copies,)),
    )
    names = (*given, *results, *scratch)
    vmem = pl.BlockSpec(memory_space=pltpu.VMEM)
    smem = pl.BlockSpec(memory_space=pltpu.SMEM)
    arrays = pl.pallas_call(
        lambda *refs: layer_kernel(n, names, *refs),
        out_shape=[jax.ShapeDtypeStruct(like.shape, wide) for like in results.values()],
        in_specs=[smem if name == "lengths" else vmem for name in given],
        out_specs=[vmem] * len(results),
        scratch_shapes=list(scratch.values()),
        compiler_params=pltpu.CompilerParams(
            collective_id=20, has_side_effects=True, vmem_limit_bytes=62 * 2**20
        ),
        name="layer",
    )(*given.values())
    return settle(arrays)


def on_device(
    inputs,
    cotangent,
    lengths,
    attn_weights,
    attn_momenta,
    ffn_weights,
    ffn_momenta,
    vectors,
    vector_momenta,
):
    group_count = lax.axis_size("group")
    dp_count = lax.axis_size("dp")
    if dp_count == 8 and group_count == 4 and ffn_weights.shape[2] == inputs.shape[1]:
        return whole_layer(
            inputs=inputs,
            cotangent=cotangent,
            lengths=lengths,
            attn_weights=attn_weights,
            attn_momenta=attn_momenta,
            ffn_weights=ffn_weights,
            ffn_momenta=ffn_momenta,
            vectors=vectors,
            vector_momenta=vector_momenta,
        )
    own_index = lax.axis_index("group")
    dp_index = lax.axis_index("dp")
    token_count, width = inputs.shape
    own_count = attn_weights.shape[1]
    quarter = ffn_weights.shape[2]
    head_size = width // HEADS
    scale = 1.0 / math.sqrt(head_size)
    bf16 = jnp.bfloat16

    own_attn = attn_weights.astype(bf16)
    own_ffn = ffn_weights.astype(bf16)
    cotan_b = cotangent.astype(bf16)
    attn_full, ffn_full, all_cotan = exchange((("chain", 4), own_attn[0]), ("dprow", own_ffn), ("zag", cotan_b)
    )
    w_query, w_key, w_value, w_output = [attn_full[i] for i in range(4)]
    w_expand, w_reduce = [ffn_full[i] for i in range(2)]
    all_cotan = all_cotan.reshape(-1, width)

    positions = jnp.arange(token_count, dtype=jnp.int32)
    order = jnp.arange(lengths.shape[1], dtype=jnp.int32)
    seq_ends = jnp.sum(jnp.where(order[:, None] <= order[None, :], lengths[0][:, None], 0), axis=0)
    segment = jnp.sum((positions[:, None] >= seq_ends[None, :]).astype(jnp.int32), axis=1)
    allowed = (segment[:, None] == segment[None, :]) & (positions[None, :] <= positions[:, None])
    normed_first, inverse_first = norm_forward(inputs)
    hidden_first = (normed_first * vectors[0] + vectors[1]).astype(bf16)
    query = ((mm(hidden_first, w_query, NN) + vectors[2]) * scale).astype(bf16)
    keyed = mm(hidden_first, w_key, NN).astype(bf16)
    valued = (mm(hidden_first, w_value, NN) + vectors[3]).astype(bf16)
    query_heads = query.reshape(token_count, HEADS, head_size)
    key_heads = keyed.reshape(token_count, HEADS, head_size)
    value_heads = valued.reshape(token_count, HEADS, head_size)
    scores = masked_scores(query_heads, key_heads, allowed)
    highest = jnp.max(scores, axis=2, keepdims=True)
    log_total = highest + jnp.log(jnp.sum(jnp.exp(scores - highest), axis=2, keepdims=True))
    probs = jnp.exp(scores - log_total)
    probs_b = probs.astype(bf16)
    attended = jnp.einsum("hqk,khd->qhd", probs_b, value_heads, preferred_element_type=jnp.float32)
    attended = attended.reshape(token_count, width).astype(bf16)
    middle = inputs + mm(attended, w_output, NN) + vectors[4]
    normed_second, inverse_second = norm_forward(middle)
    hidden_second = (normed_second * vectors[5] + vectors[6]).astype(bf16)

    (all_second,) = exchange(("zag", hidden_second))
    all_second = all_second.reshape(-1, width)
    own_bias = lax.dynamic_slice_in_dim(vectors[8:].reshape(-1), own_index * quarter, quarter, 0)
    before = mm(all_second, w_expand, NN) + own_bias
    active = jnp.maximum(before, 0.0).astype(bf16)
    out_part = mm(active, w_reduce, NT).astype(bf16)
    grad_before = jnp.where(before > 0.0, mm(all_cotan, w_reduce, NN), 0.0)
    before_grad_b = grad_before.astype(bf16)
    second_part = mm(before_grad_b, w_expand, NT).astype(bf16)

    ffn_terms = jnp.stack(
        [mm(all_second, before_grad_b, TN).astype(bf16), mm(all_cotan, active, TN).astype(bf16)]
    )
    second_parts, ffn_total = exchange(
        ("za2a", second_part.reshape(group_count, token_count, width)),
        ("dpscatter", ffn_terms),
    )
    total_tokens = float(token_count * dp_count * group_count)
    ffn_grads = ffn_total / total_tokens
    ffn_next = momentum_rate * ffn_momenta + ffn_grads
    ffn_next_b = ffn_next.astype(bf16)
    grad_second = jnp.sum(second_parts.astype(jnp.float32), axis=0)
    grad_middle = cotangent + norm_backward(
        grad_second * vectors[5], normed_second, inverse_second
    )
    middle_b = grad_middle.astype(bf16)
    grad_attended = mm(middle_b, w_output, NT).astype(bf16)
    attended_heads = grad_attended.reshape(token_count, HEADS, head_size)
    grad_probs = jnp.einsum(
        "qhd,khd->hqk", attended_heads, value_heads, preferred_element_type=jnp.float32
    )
    grad_value = jnp.einsum(
        "hqk,qhd->khd", probs_b, attended_heads, preferred_element_type=jnp.float32
    )
    delta = jnp.sum(probs * grad_probs, axis=2, keepdims=True)
    grad_scores = (probs * (grad_probs - delta)).astype(bf16)
    grad_query = (
        jnp.einsum("hqk,khd->qhd", grad_scores, key_heads, preferred_element_type=jnp.float32)
        * scale
    )
    grad_key = jnp.einsum(
        "hqk,qhd->khd", grad_scores, query_heads, preferred_element_type=jnp.float32
    )
    query_grad = grad_query.reshape(token_count, width)
    key_grad = grad_key.reshape(token_count, width)
    value_grad = grad_value.reshape(token_count, width)
    query_grad_b = query_grad.astype(bf16)
    key_grad_b = key_grad.astype(bf16)
    value_grad_b = value_grad.astype(bf16)

    attn_terms = jnp.stack(
        [
            mm(hidden_first, query_grad_b, TN).astype(bf16),
            mm(hidden_first, key_grad_b, TN).astype(bf16),
            mm(hidden_first, value_grad_b, TN).astype(bf16),
            mm(attended, middle_b, TN).astype(bf16),
        ]
    )
    attn_sums, out_parts = exchange(
        ("dpscatter", attn_terms),
        ("za2a", out_part.reshape(group_count, token_count, width)),
    )
    outputs = middle + jnp.sum(out_parts.astype(jnp.float32), axis=0) + vectors[7]
    grad_first = (
        mm(query_grad_b, w_query, NT) + mm(key_grad_b, w_key, NT) + mm(value_grad_b, w_value, NT)
    )
    input_grad = grad_middle + norm_backward(grad_first * vectors[0], normed_first, inverse_first)
    small_terms = jnp.stack(
        [
            jnp.sum(grad_first * normed_first, axis=0),
            jnp.sum(grad_first, axis=0),
            jnp.sum(query_grad, axis=0),
            jnp.sum(value_grad, axis=0),
            jnp.sum(grad_middle, axis=0),
            jnp.sum(grad_second * normed_second, axis=0),
            jnp.sum(grad_second, axis=0),
            jnp.sum(cotangent, axis=0),
        ]
    )
    owner_mask = jnp.arange(group_count, dtype=jnp.int32) == own_index
    bias_terms = jnp.where(owner_mask[:, None], jnp.sum(grad_before, axis=0)[None], 0.0)
    vector_terms = jnp.concatenate([small_terms, bias_terms.reshape(-1, width)], axis=0)
    def square_sums(own):
        sums = jnp.sum(own * own, axis=(1, 2))
        return jnp.broadcast_to(jnp.pad(sums, (0, 8 - own.shape[0]))[:, None], (8, 128))

    attn_pieces, ffn_full_next, vector_all, ffn_squares = exchange(
        ("za2a", attn_sums.astype(bf16)),
        ("dprow", ffn_next_b),
        ("dpag", vector_terms),
        ("dpag", square_sums(ffn_next)),
    )
    attn_grads = jnp.sum(attn_pieces.astype(jnp.float32), axis=0, keepdims=True) / total_tokens
    attn_next = momentum_rate * attn_momenta + attn_grads
    gram_part = jnp.concatenate(
        [mm(ffn_next_b[0], ffn_full_next[0], NT), mm(ffn_next_b[1], ffn_full_next[1], NT)]
    )
    piece = 2 * own_count // group_count
    attn_full_next, gram_pieces, attn_squares, ffn_squares, vector_groups = exchange(
        ("dprow", attn_next.astype(bf16)),
        ("za2a", gram_part.astype(bf16).reshape(group_count, piece, width)),
        ("dpag", square_sums(attn_next)),
        ("zag", jnp.sum(ffn_squares, axis=0)),
        ("zag", jnp.sum(vector_all, axis=0)),
    )
    gram_piece = jnp.sum(gram_pieces.astype(jnp.float32), axis=0).astype(bf16)
    (gram_full,) = exchange((("chain", 2), gram_piece))
    attn_square = jnp.sum(attn_squares, axis=0)[:1, 0]
    ffn_square = jnp.sum(ffn_squares, axis=0)[:2, 0]
    scales = 1.0 / (jnp.sqrt(jnp.concatenate([attn_square, ffn_square])) + 1e-07)
    new_weights = newton_schulz(
        scales,
        dp_index * own_count,
        attn_full_next[0],
        ffn_full_next,
        gram_full,
        jnp.concatenate([attn_next, ffn_next], axis=0),
        jnp.concatenate([attn_weights, ffn_weights], axis=0),
    )
    new_attn_weights = new_weights[:1]
    new_ffn_weights = new_weights[1:]
    vector_grads = jnp.sum(vector_groups, axis=0) / total_tokens
    new_vector_momenta = momentum_rate * vector_momenta + vector_grads
    mean_square = jnp.mean(new_vector_momenta * new_vector_momenta, axis=1, keepdims=True)
    new_vectors = vectors - vector_rate * new_vector_momenta * lax.rsqrt(mean_square + 1e-06)
    return (
        outputs,
        input_grad,
        attn_grads,
        ffn_grads,
        vector_grads,
        new_attn_weights,
        attn_next,
        new_ffn_weights,
        ffn_next,
        new_vectors,
        new_vector_momenta,
    )


def solution(mesh):
    in_specs = (
        P(("dp", "group"), None),
        P(("dp", "group"), None),
        P(("dp", "group"), None),
        P("group", "dp", None),
        P("group", "dp", None),
        P(None, "dp", "group"),
        P(None, "dp", "group"),
        P(),
        P(),
    )
    out_specs = (
        P(("dp", "group"), None),
        P(("dp", "group"), None),
        P("group", "dp", None),
        P(None, "dp", "group"),
        P(),
        P("group", "dp", None),
        P("group", "dp", None),
        P(None, "dp", "group"),
        P(None, "dp", "group"),
        P(),
        P(),
    )
    return jax.shard_map(
        on_device, mesh=mesh, in_specs=in_specs, out_specs=out_specs, check_vma=False
    )
```

```python
import math
import types

import jax
import jax.numpy as jnp
from jax import lax
from jax.experimental import pallas as pl
from jax.experimental.pallas import tpu as pltpu
from jax.sharding import PartitionSpec as P

HEADS = 12
NS_ITERS = 3


coef_first = 3.4445
coef_second = -4.775
coef_third = 2.0315
momentum_rate = 0.9
muon_rate = 0.8
vector_rate = 0.1


def norm_forward(rows):
    centre = jnp.mean(rows, axis=1, keepdims=True)
    centred = rows - centre
    variance = jnp.mean(centred * centred, axis=1, keepdims=True)
    inverse = lax.rsqrt(variance + 1e-05)
    return (centred * inverse, inverse)


def norm_backward(grad_normed, normed, inverse):
    return inverse * (
        grad_normed
        - jnp.mean(grad_normed, axis=1, keepdims=True)
        - normed * jnp.mean(grad_normed * normed, axis=1, keepdims=True)
    )


def masked_scores(query_heads, key_heads, allowed):
    scores = jnp.einsum("qhd,khd->hqk", query_heads, key_heads, preferred_element_type=jnp.float32)
    return jnp.where(allowed[None], scores, -jnp.inf)


MESH = pl.DeviceIdType.MESH


def flip(index, bits):
    result = index
    for bit in (1, 2, 4):
        if bits & bit:
            result = result + bit - 2 * bit * ((index // bit) % 2)
    return result


def exchange(*pairs):
    results = []
    for kind, x in pairs:
        if kind == "zag":
            results.append(lax.all_gather(x, "group", axis=0))
        elif kind == "za2a":
            results.append(lax.all_to_all(x, "group", 0, 0))
        elif kind == "dpag":
            results.append(lax.all_gather(x, "dp", axis=0))
        elif kind == "dprow":
            results.append(lax.all_gather(x, "dp", axis=1, tiled=True))
        elif kind == "dpscatter":
            wide = x.astype(jnp.float32)
            results.append(lax.psum_scatter(wide, "dp", scatter_dimension=1, tiled=True))
        else:
            held = lax.all_gather(x, "group", axis=0).reshape(kind[1], -1, x.shape[1])
            results.append(lax.all_gather(held, "dp", axis=1, tiled=True))
    return results


def mm(left, right, dims):
    return lax.dot_general(left, right, (dims, ((), ())), preferred_element_type=jnp.float32)


NN = ((1,), (0,))
NT = ((1,), (1,))
TN = ((0,), (0,))


def newton_schulz_kernel(
    scale_ref,
    start_ref,
    attn_ref,
    ffn_ref,
    gram_ref,
    own_ref,
    weight_ref,
    out_ref,
    gram,
    gram_b,
    mixed,
    mixed_b,
    half,
    half_b,
):
    rows = own_ref.shape[1]
    mine = pl.ds(pl.multiple_of(start_ref[0], 8), rows)
    bf16 = jnp.bfloat16

    def one(index, whole_b):
        scale = scale_ref[index]
        lead = 1.0
        spread = None
        for iteration in range(NS_ITERS - 1):
            gram_b[...] = gram[...].astype(bf16)
            mixed[...] = coef_second * gram[...] + coef_third * mm(gram_b[...], gram_b[...], NN)
            mixed_b[...] = mixed[...].astype(bf16)
            half[...] = coef_first * gram[...] + mm(mixed_b[...], gram_b[...], NN)
            half_b[...] = half[...].astype(bf16)
            gram[...] = coef_first * half[...] + mm(half_b[...], mixed_b[...], NN)
            if spread is None:
                spread = mixed[mine, :]
            else:
                product = mm(spread.astype(bf16), mixed_b[...], NN)
                spread = coef_first * spread + lead * mixed[mine, :] + product
            lead = lead * coef_first
        gram_b[...] = gram[...].astype(bf16)
        once = lead * gram[mine, :] + mm(spread.astype(bf16), gram_b[...], NN)
        twice = mm(once.astype(bf16), gram_b[...], NN)
        spread = coef_first * spread + coef_second * once + coef_third * twice
        lead = lead * coef_first
        moved = lead * own_ref[index] + mm(spread.astype(bf16), whole_b, NN)
        out_ref[index] = weight_ref[index] - (muon_rate * scale) * moved

    gram[...] = mm(attn_ref[...], attn_ref[...], NT) * (scale_ref[0] * scale_ref[0])
    one(0, attn_ref[...])

    @pl.loop(0, gram_ref.shape[0])
    def _(i):
        gram[...] = gram_ref[i].astype(jnp.float32) * (scale_ref[i + 1] * scale_ref[i + 1])
        one(i + 1, ffn_ref[i])


def newton_schulz(scales, row_start, attn_b, ffn_b, grams, own, weights):
    side = attn_b.shape[0]
    vmem = pl.BlockSpec(memory_space=pltpu.VMEM)
    smem = pl.BlockSpec(memory_space=pltpu.SMEM)
    wide, narrow = pltpu.VMEM((side, side), jnp.float32), pltpu.VMEM((side, side), jnp.bfloat16)
    return pl.pallas_call(
        newton_schulz_kernel,
        out_shape=jax.ShapeDtypeStruct(own.shape, jnp.float32),
        in_specs=[smem, smem, vmem, vmem, vmem, vmem, vmem],
        out_specs=vmem,
        scratch_shapes=[wide, narrow] * 3,
        compiler_params=pltpu.CompilerParams(vmem_limit_bytes=48 * 2**20),
        name="newton_schulz",
    )(scales, jnp.reshape(row_start, (1,)), attn_b, ffn_b, grams, own, weights)


class Net:
    def __init__(self, send_sem, recv_sem, z, d, n):
        self.send_sem, self.recv_sem = send_sem, recv_sem
        self.z, self.d, self.n = z, d, n
        self.slot = 0
        self.copies = []
        self.to_core = {"dp": flip(d, 1)}
        self.to_x = {"dp": flip(d, 2)}
        self.to_y = {"dp": flip(d, 4)}

    def send(self, src, dst, device):
        copy = pltpu.make_async_remote_copy(
            src_ref=src,
            dst_ref=dst,
            send_sem=self.send_sem.at[self.slot],
            recv_sem=self.recv_sem.at[self.slot],
            device_id=device,
            device_id_type=MESH,
        )
        self.slot += 1
        copy.start()
        self.copies.append(copy)
        return copy

    def up(self, k):
        return lax.rem(self.z + k, self.n)

    def down(self, k):
        return lax.rem(self.z + self.n - k, self.n)

    def line(self, src, dst):
        return [self.send(src, dst, {"group": self.up(k)}) for k in range(1, self.n)]

    def plane(self, src, dst):
        return [self.send(src, dst, {"dp": flip(self.d, k)}) for k in range(1, 8)]

    def finish(self):
        for copy in self.copies:
            copy.wait_send()


class Relay:
    def __init__(self, net, blocks):
        self.net, self.blocks, self.base = net, blocks, net.slot
        net.slot += 2 * (net.n - 1)
        self.each(0, lambda copy: copy.start())

    def copy(self, way, steps, origin):
        net = self.net
        slot = self.base + steps + (net.n - 1) * (way < 0)
        return pltpu.make_async_remote_copy(
            src_ref=self.blocks.at[origin],
            dst_ref=self.blocks.at[origin],
            send_sem=net.send_sem.at[slot],
            recv_sem=net.recv_sem.at[slot],
            device_id={"group": net.z + way},
            device_id_type=MESH,
        )

    def each(self, steps, act):
        net = self.net
        z, last = net.z, net.n - 1
        if steps < last:
            pl.when((z >= steps) & (z < last))(lambda: act(self.copy(1, steps, z - steps)))
            pl.when((z + steps <= last) & (z > 0))(lambda: act(self.copy(-1, steps, z + steps)))

    def step(self, steps):
        net = self.net
        z = net.z
        pl.when(z >= steps)(lambda: self.copy(1, steps - 1, z - steps).wait_recv())
        pl.when(z + steps < net.n)(lambda: self.copy(-1, steps - 1, z + steps).wait_recv())
        self.each(steps, lambda copy: copy.start())

    def finish(self):
        for steps in range(self.net.n - 1):
            self.each(steps, lambda copy: copy.wait_send())


class Gather:
    def __init__(self, net, src, full, rows):
        self.net, self.full, self.rows = net, full, rows
        place = self.place(net.d)
        self.x = net.send(src, place, net.to_x)
        self.y = net.send(src, place, net.to_y)
        self.core = net.send(src, place, net.to_core)

    def place(self, index, part=None):
        first = self.rows // 32 * 16
        start, size = index * self.rows, self.rows
        if part is not None:
            start = start + part * first
            size = (first, self.rows - first)[part]
        return self.full.at[pl.ds(pl.multiple_of(start, 16), size), :]

    def second(self):
        net = self.net
        from_x, from_y = flip(net.d, 2), flip(net.d, 4)
        self.x.wait_recv()
        self.via_y = net.send(self.place(from_x, 0), self.place(from_x, 0), net.to_y)
        self.share_x = net.send(self.place(from_x), self.place(from_x), net.to_core)
        self.y.wait_recv()
        self.via_x = net.send(self.place(from_y, 1), self.place(from_y, 1), net.to_x)
        self.share_y = net.send(self.place(from_y), self.place(from_y), net.to_core)

    def third(self):
        net = self.net
        far = flip(net.d, 6)
        self.via_y.wait_recv()
        self.via_x.wait_recv()
        self.share_far = net.send(self.place(far), self.place(far), net.to_core)

    def end(self):
        for copy in (self.core, self.share_x, self.share_y, self.share_far):
            copy.wait_recv()


class Scatter:
    def __init__(self, net, x, near, total, recv_b, recv_c, part):
        self.net, self.x, self.rows = net, x, x.shape[0] // 8
        self.near, self.total, self.recv_b, self.recv_c, self.part = near, total, recv_b, recv_c, part
        self.copies = [
            net.send(self.block(2 * r + 1), near.at[r], net.to_core) for r in (3, 1, 2, 0)
        ]

    def block(self, bits):
        start = pl.multiple_of(flip(self.net.d, bits) * self.rows, 16)
        return self.x.at[pl.ds(start, self.rows), :]

    def second(self):
        net, total = self.net, self.total
        wide = jnp.float32
        half = self.rows // 2
        low, high = pl.ds(0, half), pl.ds(half, half)
        for r, copy in zip((3, 1, 2, 0), self.copies):
            copy.wait_recv()
            own = self.block(2 * r)[...].astype(wide)
            total[r] = (own + self.near[r].astype(wide)).astype(total.dtype)
        self.moved = [
            net.send(total.at[3, low], self.recv_b.at[1], net.to_x),
            net.send(total.at[3, high], self.recv_b.at[3], net.to_y),
            net.send(total.at[1, low], self.recv_b.at[0], net.to_x),
            net.send(total.at[2, high], self.recv_b.at[2], net.to_y),
        ]

    def third(self):
        net, total, part = self.net, self.total, self.part
        wide = jnp.float32
        half = self.rows // 2
        low, high = pl.ds(0, half), pl.ds(half, half)
        self.moved[0].wait_recv()
        part[0] = (total[2, low].astype(wide) + self.recv_b[1].astype(wide)).astype(part.dtype)
        self.ends = [net.send(part.at[0], self.recv_c.at[0], net.to_y)]
        self.moved[1].wait_recv()
        part[1] = (total[1, high].astype(wide) + self.recv_b[3].astype(wide)).astype(part.dtype)
        self.ends.append(net.send(part.at[1], self.recv_c.at[1], net.to_x))

    def end(self):
        total = self.total
        wide = jnp.float32
        half = self.rows // 2
        low, high = pl.ds(0, half), pl.ds(half, half)
        self.moved[2].wait_recv()
        self.moved[3].wait_recv()
        self.ends[0].wait_recv()
        self.ends[1].wait_recv()
        first = total[0, low].astype(wide) + self.recv_b[0].astype(wide) + self.recv_c[0].astype(wide)
        second = total[0, high].astype(wide) + self.recv_b[2].astype(wide) + self.recv_c[1].astype(wide)
        return jnp.concatenate([first, second], axis=0)


def muon_steps(gram, gram_b, mixed_b, half_b, mine, finish):
    bf16 = jnp.bfloat16
    lead = 1.0
    spread = None
    for iteration in range(NS_ITERS - 1):
        gram_b[...] = gram[...].astype(bf16)
        own_gram = gram[mine, :]
        mixed_b[...] = (coef_second * gram[...] + coef_third * mm(gram_b[...], gram_b[...], NN)).astype(
            bf16
        )
        yield
        own_mixed = coef_second * own_gram + coef_third * mm(own_gram.astype(bf16), gram_b[...], NN)
        gram[...] = coef_first * gram[...] + mm(mixed_b[...], gram_b[...], NN)
        half_b[...] = gram[...].astype(bf16)
        yield
        gram[...] = coef_first * gram[...] + mm(half_b[...], mixed_b[...], NN)
        if spread is None:
            spread = own_mixed
        else:
            product = mm(spread.astype(bf16), mixed_b[...], NN)
            spread = coef_first * spread + lead * own_mixed + product
        lead = lead * coef_first
        yield
    gram_b[...] = gram[...].astype(bf16)
    once = lead * gram[mine, :] + mm(spread.astype(bf16), gram_b[...], NN)
    twice = mm(once.astype(bf16), gram_b[...], NN)
    spread = coef_first * spread + coef_second * once + coef_third * twice
    lead = lead * coef_first
    finish(spread.astype(bf16), lead)
    yield


def layer_kernel(n, names, loaded, *refs):
    ref = types.SimpleNamespace(**dict(zip(names, refs)))
    bf16, wide = jnp.bfloat16, jnp.float32
    z, d = lax.axis_index("group"), lax.axis_index("dp")
    net = Net(ref.send_sem, ref.recv_sem, z, d, n)
    lengths, vectors = ref.lengths, ref.vectors
    loads = {
        name: pltpu.make_async_copy(refs[i], vars(ref)[name], ref.load_sem.at[j])
        for j, (i, name) in enumerate(loaded)
    }
    for copy in loads.values():
        copy.start()

    def arrived(*wanted):
        for name in wanted:
            loads.pop(name).wait()

    tokens, width = ref.inputs.shape
    rows = ref.attn_weights.shape[1]
    head_size = width // HEADS
    pairs = HEADS // 2
    pair_width = 2 * head_size
    scale = 1.0 / math.sqrt(head_size)
    total_tokens = float(tokens * 8 * n)
    ranks = range(1, n)

    def vector(i):
        return vectors[pl.ds(i, 1), :]

    def column_sum(x):
        return jnp.sum(x, axis=0, keepdims=True)

    barrier = pltpu.get_barrier_semaphore()
    for k in ranks:
        pl.semaphore_signal(barrier, inc=1, device_id={"group": net.up(k)}, device_id_type=MESH)
    for k in range(1, 8):
        pl.semaphore_signal(barrier, inc=1, device_id={"dp": flip(d, k)}, device_id_type=MESH)

    own_attn, own_ffn = ref.own_attn, ref.own_ffn
    held, attn_full, ffn_full = ref.held, ref.attn_full, ref.ffn_full
    arrived("attn_weights")
    own_attn[...] = ref.attn_weights[0].astype(bf16)
    all_cotan, all_second = ref.all_cotan, ref.all_second

    pl.semaphore_wait(barrier, n - 1 + 7)

    chain = net.line(own_attn, held.at[z])
    own_rows = pl.ds(pl.multiple_of(d * rows, 16), rows)

    weights = [Gather(net, own_attn, attn_full.at[z], rows)]
    arrived("ffn_weights")
    own_ffn[...] = ref.ffn_weights[...].astype(bf16)
    ffn_weights = [Gather(net, own_ffn.at[0], ffn_full.at[0], rows)]
    arrived(*list(loads))
    all_cotan[z] = ref.cotangent[...].astype(bf16)
    for i in range(2):
        ffn_full[i, own_rows, :] = own_ffn[i]
    attn_full[z, own_rows, :] = own_attn[...]

    centre = jnp.mean(ref.inputs[...], axis=1, keepdims=True)
    centred = ref.inputs[...] - centre
    inverse_first = lax.rsqrt(jnp.mean(centred * centred, axis=1, keepdims=True) + 1e-05)
    ref.normed_first[...] = centred * inverse_first
    hidden_first, attended = ref.hidden_first, ref.attended
    hidden_first[...] = (ref.normed_first[...] * vector(0) + vector(1)).astype(bf16)

    for k in ranks:
        origin = net.down(k)
        chain[k - 1].wait_recv()
        weights.append(Gather(net, held.at[origin], attn_full.at[origin], rows))
        attn_full[origin, own_rows, :] = held[origin]
        if k == 1:
            weights[0].second()
    cotan_copies = net.line(all_cotan.at[z], all_cotan.at[z])
    for gather in weights[1:]:
        gather.second()
    ffn_weights.append(Gather(net, own_ffn.at[1], ffn_full.at[1], rows))
    for gather in weights:
        gather.third()
    for gather in ffn_weights:
        gather.second()
    for gather in weights:
        gather.end()
    for gather in ffn_weights:
        gather.third()

    lane = lax.broadcasted_iota(jnp.int32, (tokens, pair_width), 1)
    low_lane = lane < head_size
    ones = lax.broadcasted_iota(jnp.int32, (1, pair_width), 1) < head_size
    low_mask = jnp.where(ones, 1.0, 0.0).astype(bf16)
    high_mask = jnp.where(ones, 0.0, 1.0).astype(bf16)

    def split(x):
        return jnp.concatenate([x * low_mask, x * high_mask], axis=0)

    def join(x):
        return jnp.where(low_lane, x[:tokens], x[tokens:])

    query, keyed, valued = ref.query, ref.keyed, ref.valued
    query[...] = ((mm(hidden_first[...], attn_full[0], NN) + vector(2)) * scale).astype(bf16)
    keyed[...] = mm(hidden_first[...], attn_full[1], NN).astype(bf16)
    valued[...] = (mm(hidden_first[...], attn_full[2], NN) + vector(3)).astype(bf16)

    at_row = lax.broadcasted_iota(jnp.int32, (2 * tokens, tokens), 0)
    at_row = jnp.where(at_row < tokens, at_row, at_row - tokens)
    at_column = lax.broadcasted_iota(jnp.int32, (2 * tokens, tokens), 1)
    row_part = jnp.zeros_like(at_row)
    column_part = jnp.zeros_like(at_column)
    edge = 0
    for i in range(lengths.shape[1]):
        edge = edge + lengths[0, i]
        row_part = row_part + jnp.where(at_row >= edge, 1, 0)
        column_part = column_part + jnp.where(at_column >= edge, 1, 0)
    allowed = (row_part == column_part) & (at_column <= at_row)

    probs = ref.probs
    slices = [pl.ds(p * pair_width, pair_width) for p in range(pairs)]
    for p, lanes in enumerate(slices):
        scores = mm(split(query[:, lanes]), keyed[:, lanes], NT)
        probs[p] = jnp.where(allowed, scores, -jnp.inf)
    for p in range(pairs):
        raised = jnp.exp(probs[p] - jnp.max(probs[p], axis=1, keepdims=True))
        probs[p] = raised * (1.0 / jnp.sum(raised, axis=1, keepdims=True))
    for p, lanes in enumerate(slices):
        attended[:, lanes] = join(mm(probs[p].astype(bf16), valued[:, lanes], NN)).astype(bf16)

    middle = ref.middle
    middle[...] = ref.inputs[...] + mm(attended[...], attn_full[3], NN) + vector(4)
    centre = jnp.mean(middle[...], axis=1, keepdims=True)
    centred = middle[...] - centre
    inverse_second = lax.rsqrt(jnp.mean(centred * centred, axis=1, keepdims=True) + 1e-05)
    normed_second = ref.normed_second
    normed_second[...] = centred * inverse_second
    all_second[z] = (normed_second[...] * vector(5) + vector(6)).astype(bf16)
    relay = Relay(net, all_second)
    for gather in ffn_weights:
        gather.end()

    active, before_grad = ref.active, ref.before_grad
    grad_send, grad_recv, grad_own = ref.grad_send, ref.grad_recv, ref.grad_own
    out_send, out_recv, out_own = ref.out_send, ref.out_recv, ref.out_own
    bias_sum = ref.bias_sum
    bias_sum[...] = jnp.zeros_like(bias_sum)
    grad_slot = net.slot
    net.slot += n

    def grad_copy(origin, sender):
        return pltpu.make_async_remote_copy(
            src_ref=grad_send.at[origin],
            dst_ref=grad_recv.at[sender],
            send_sem=net.send_sem.at[grad_slot + origin],
            recv_sem=net.recv_sem.at[grad_slot + sender],
            device_id={"group": origin},
            device_id_type=MESH,
        )

    def feed_forward(origin, own):
        before = mm(all_second[origin], ffn_full[0], NN) + vector(8 + z)
        active[origin] = jnp.maximum(before, 0.0).astype(bf16)
        grad_before = jnp.where(before > 0.0, mm(all_cotan[origin], ffn_full[1], NN), 0.0)
        bias_sum[...] = bias_sum[...] + column_sum(grad_before)
        before_grad[origin] = grad_before.astype(bf16)
        second = mm(before_grad[origin], ffn_full[0], NT)
        if own:
            grad_own[...] = second
        else:
            grad_send[origin] = second.astype(bf16)
            grad_copy(origin, z).start()
        out = mm(active[origin], ffn_full[1], NT)
        if own:
            out_own[...] = out
        else:
            out_send[origin] = out.astype(bf16)

    feed_forward(z, True)
    for copy in cotan_copies:
        copy.wait_recv()
    for steps in ranks:
        relay.step(steps)
        pl.when(z >= steps)(lambda: feed_forward(z - steps, False))
        pl.when(z + steps < n)(lambda: feed_forward(z + steps, False))

    def scatter(x, slot):
        pools = (ref.near, ref.total, ref.recv_b, ref.recv_c, ref.part)
        return Scatter(net, x, *[pool.at[slot] for pool in pools])

    ffn_terms, attn_terms = ref.ffn_terms, ref.attn_terms
    many = n * tokens
    ffn_terms[0] = mm(
        all_second[...].reshape(many, width), before_grad[...].reshape(many, width), TN
    ).astype(bf16)
    ffn_sums = [scatter(ffn_terms.at[0], 0)]
    ffn_terms[1] = mm(
        all_cotan[...].reshape(many, width), active[...].reshape(many, width), TN
    ).astype(bf16)
    ffn_sums.append(scatter(ffn_terms.at[1], 1))
    for part in ffn_sums:
        part.second()
    for part in ffn_sums:
        part.third()

    next_own, next_full = ref.next_own, ref.next_full
    ffn_squares, attn_squares = ref.ffn_squares, ref.attn_squares

    def square(x):
        return jnp.broadcast_to(jnp.sum(column_sum(x * x), axis=1, keepdims=True), (8, 128))

    ffn_nexts = []
    for i in range(2):
        grad = ffn_sums[i].end() / total_tokens
        ref.ffn_grads[i] = grad
        moment = momentum_rate * ref.ffn_momenta[i] + grad
        ref.new_ffn_momenta[i] = moment
        next_own[1 + i] = moment.astype(bf16)
        ffn_nexts.append(Gather(net, next_own.at[1 + i], next_full.at[1 + i], rows))
        next_full[1 + i, own_rows, :] = next_own[1 + i]
        ffn_squares[0, i] = square(moment)
    square_copies = net.plane(ffn_squares.at[0], ref.ffn_squares_in.at[d])

    total = grad_own[...]
    for k in ranks:
        grad_copy(z, net.up(k)).wait_recv()
        total = total + grad_recv[net.up(k)].astype(wide)
    out_copies = [
        net.send(out_send.at[net.down(k)], out_recv.at[k - 1], {"group": net.down(k)}) for k in ranks
    ]
    terms = ref.vector_terms
    terms[...] = jnp.zeros_like(terms)

    def put(i, x):
        terms[pl.ds(i, 1), :] = x

    def norm_back(grad, normed, inverse):
        return inverse * (
            grad
            - jnp.mean(grad, axis=1, keepdims=True)
            - normed * jnp.mean(grad * normed, axis=1, keepdims=True)
        )

    put(8 + z, bias_sum[...])
    put(5, column_sum(total * normed_second[...]))
    put(6, column_sum(total))
    put(7, column_sum(ref.cotangent[...]))
    grad_middle = ref.grad_middle
    grad_middle[...] = ref.cotangent[...] + norm_back(
        total * vector(5), normed_second[...], inverse_second
    )
    put(4, column_sum(grad_middle[...]))
    middle_b = ref.middle_b
    middle_b[...] = grad_middle[...].astype(bf16)
    attn_terms[3] = mm(attended[...], middle_b[...], TN).astype(bf16)
    attn_sums = [scatter(attn_terms.at[3], 5)]
    grad_attended = ref.grad_attended
    grad_attended[...] = mm(middle_b[...], attn_full[3], NT).astype(bf16)
    grads = [ref.query_grad, ref.key_grad, ref.value_grad]
    pulls, pushes = ref.grad_probs, ref.grad_scores
    for p, lanes in enumerate(slices):
        pulls[p] = mm(split(grad_attended[:, lanes]), valued[:, lanes], NT)
    for p in range(pairs):
        delta = jnp.sum(probs[p] * pulls[p], axis=1, keepdims=True)
        pushes[p] = (probs[p] * (pulls[p] - delta)).astype(bf16)
    for gather in ffn_nexts:
        gather.second()
    attn_sums[0].second()
    for p, lanes in enumerate(slices):
        grad_value = mm(probs[p].astype(bf16), split(grad_attended[:, lanes]), TN)
        grad_query = join(mm(pushes[p], keyed[:, lanes], NN)) * scale
        grad_key = mm(pushes[p], split(query[:, lanes]), TN)
        terms[pl.ds(2, 1), lanes] = column_sum(grad_query)
        terms[pl.ds(3, 1), lanes] = column_sum(grad_value)
        grads[0][:, lanes] = grad_query.astype(bf16)
        grads[1][:, lanes] = grad_key.astype(bf16)
        grads[2][:, lanes] = grad_value.astype(bf16)
    for m in range(3):
        attn_terms[m] = mm(hidden_first[...], grads[m][...], TN).astype(bf16)
        attn_sums.append(scatter(attn_terms.at[m], 2 + m))
    for gather in ffn_nexts:
        gather.third()
    for part in attn_sums[1:]:
        part.second()
    attn_sums[0].third()

    gram_send, gram_recv = ref.gram_send, ref.gram_recv
    piece = 2 * rows // n
    for i in range(2):
        ffn_nexts[i].end()
        gram_send[pl.ds(i * rows, rows), :] = mm(next_own[1 + i], next_full[1 + i], NT).astype(bf16)

    def gram_rows(index):
        return gram_send.at[pl.ds(pl.multiple_of(index * piece, 16), piece), :]

    gram_copies = [
        net.send(gram_rows(net.up(k)), gram_recv.at[k - 1], {"group": net.up(k)}) for k in ranks
    ]

    grad_first = mm(grads[0][...], attn_full[0], NT)
    grad_first = grad_first + mm(grads[1][...], attn_full[1], NT)
    grad_first = grad_first + mm(grads[2][...], attn_full[2], NT)
    put(0, column_sum(grad_first * ref.normed_first[...]))
    put(1, column_sum(grad_first))
    ref.input_grad[...] = grad_middle[...] + norm_back(
        grad_first * vector(0), ref.normed_first[...], inverse_first
    )
    vector_in = ref.vector_in
    vector_copies = net.plane(terms, vector_in.at[d])

    for part in attn_sums[1:]:
        part.third()

    gram_sum = gram_rows(z)[...].astype(wide)
    for k in ranks:
        gram_copies[k - 1].wait_recv()
        gram_sum = gram_sum + gram_recv[k - 1].astype(wide)
    gram_all, gram_full = ref.gram_all, ref.gram_full
    per = n // 2
    own_piece = gram_all.at[z // per, pl.ds(pl.multiple_of(lax.rem(z, per) * piece, 16), piece), :]
    own_piece[...] = gram_sum.astype(bf16)
    gram_line = net.line(own_piece, own_piece)

    piece_send, piece_recv = ref.piece_send, ref.piece_recv
    for m, part in zip((3, 0, 1, 2), attn_sums):
        piece_send[m] = part.end().astype(bf16)
    piece_copies = [
        net.send(piece_send.at[net.up(k)], piece_recv.at[k - 1], {"group": net.up(k)}) for k in ranks
    ]

    for copy in gram_line:
        copy.wait_recv()
    grams = []
    for i in range(2):
        grams.append(Gather(net, gram_all.at[i], gram_full.at[i], rows))
        gram_full[i, own_rows, :] = gram_all[i]

    plane_sum = ref.plane_sum
    square_in = ref.ffn_squares_in
    square_total = ffn_squares[0]
    for k in range(1, 8):
        square_copies[k - 1].wait_recv()
        square_total = square_total + square_in[flip(d, k)]
    ffn_squares[1] = square_total
    plane_squares = net.line(ffn_squares.at[1], ref.ffn_squares_all.at[z])
    vector_total = terms[...]
    for k in range(1, 8):
        vector_copies[k - 1].wait_recv()
        vector_total = vector_total + vector_in[flip(d, k)]
    plane_sum[...] = vector_total
    vector_all = net.line(plane_sum, ref.vector_all.at[z])

    result = out_own[...] + middle[...] + vector(7)
    for k in ranks:
        out_copies[k - 1].wait_recv()
        result = result + out_recv[k - 1].astype(wide)
    ref.outputs[...] = result

    for gather in grams:
        gather.second()
    grad = piece_send[z].astype(wide)
    for k in ranks:
        piece_copies[k - 1].wait_recv()
        grad = grad + piece_recv[k - 1].astype(wide)
    grad = grad / total_tokens
    ref.attn_grads[0] = grad
    moment = momentum_rate * ref.attn_momenta[0] + grad
    ref.new_attn_momenta[0] = moment
    next_own[0] = moment.astype(bf16)
    attn_next = Gather(net, next_own.at[0], next_full.at[0], rows)
    next_full[0, own_rows, :] = next_own[0]
    attn_squares[0] = square(moment)
    own_squares = net.plane(attn_squares.at[0], ref.attn_squares_in.at[d])
    for gather in grams:
        gather.third()

    gram, gram_b, mixed_b, half_b = ref.gram, ref.gram_b, ref.mixed_b, ref.half_b

    def inverse_norm(x):
        return 1.0 / (jnp.sqrt(x[0:1, 0:1]) + 1e-07)

    square_total = ffn_squares[1]
    for k in ranks:
        plane_squares[k - 1].wait_recv()
        square_total = square_total + ref.ffn_squares_all[net.down(k)]

    square_sum = ref.square_sum
    square_sum[...] = square_total
    core = lax.rem(d, 2)
    both_rows = pl.ds(pl.multiple_of((d // 2) * 2 * rows, 16), 2 * rows)
    spread_all, spread_in = ref.spread_all, ref.spread_in
    leads = []

    def half_of(index):
        return spread_all.at[pl.ds(pl.multiple_of(index * rows, 16), rows), :]

    def exchange_spread(spread, lead):
        spread_all[...] = spread
        leads.append(lead)

    for gather in grams:
        gather.end()
    own_scale = inverse_norm(square_sum[core])
    gram[...] = gram_full[core].astype(wide) * (own_scale * own_scale)
    steps = muon_steps(gram, gram_b, mixed_b, half_b, both_rows, exchange_spread)
    next(steps)
    attn_next.second()
    next(steps)
    next(steps)
    attn_next.third()
    for _ in steps:
        pass
    spread_copy = net.send(half_of(1 - core), spread_in, net.to_core)

    def ffn_update(index, spread):
        own_scale = inverse_norm(square_sum[index])
        moved = leads[0] * ref.new_ffn_momenta[index] + mm(spread, next_full[1 + index], NN)
        ref.new_ffn_weights[index] = ref.ffn_weights[index] - (muon_rate * own_scale) * moved

    ffn_update(core, half_of(core)[...])

    vector_total = plane_sum[...]
    for k in ranks:
        vector_all[k - 1].wait_recv()
        vector_total = vector_total + ref.vector_all[net.down(k)]
    vector_total = vector_total / total_tokens
    ref.vector_grads[...] = vector_total
    moment = momentum_rate * ref.vector_momenta[...] + vector_total
    ref.new_vector_momenta[...] = moment
    mean_square = jnp.mean(moment * moment, axis=1, keepdims=True)
    ref.new_vectors[...] = vectors[...] - vector_rate * moment * lax.rsqrt(mean_square + 1e-06)

    attn_next.end()
    square_total = attn_squares[0]
    for k in range(1, 8):
        own_squares[k - 1].wait_recv()
        square_total = square_total + ref.attn_squares_in[flip(d, k)]
    own_scale = inverse_norm(square_total)
    gram[...] = mm(next_full[0], next_full[0], NT) * (own_scale * own_scale)
    own_muon = muon_rate * own_scale

    def attn_update(spread, lead):
        moved = lead * ref.new_attn_momenta[0] + mm(spread, next_full[0], NN)
        ref.new_attn_weights[0] = ref.attn_weights[0] - own_muon * moved

    for _ in muon_steps(gram, gram_b, mixed_b, half_b, own_rows, attn_update):
        pass
    spread_copy.wait_recv()
    ffn_update(1 - core, spread_in[...])
    relay.finish()
    for k in ranks:
        grad_copy(net.up(k), z).wait_send()
    net.finish()


def settle_kernel(count, *refs):
    sources, targets, held = refs[:count], refs[count : 2 * count], refs[2 * count : 3 * count]
    sem_in, sem_out = refs[3 * count :]
    reads = [pltpu.make_async_copy(sources[i], held[i], sem_in.at[i]) for i in range(count)]
    writes = [pltpu.make_async_copy(held[i], targets[i], sem_out.at[i]) for i in range(count)]
    for copy in reads:
        copy.start()
    for read, write in zip(reads, writes):
        read.wait()
        write.start()
    for copy in writes:
        copy.wait()


def settle(arrays):
    count = len(arrays)
    anywhere = pl.BlockSpec(memory_space=pl.ANY)
    return pl.pallas_call(
        lambda *refs: settle_kernel(count, *refs),
        out_shape=[jax.ShapeDtypeStruct(x.shape, x.dtype) for x in arrays],
        in_specs=[anywhere] * count,
        out_specs=[anywhere] * count,
        scratch_shapes=[
            *[pltpu.VMEM(x.shape, x.dtype) for x in arrays],
            pltpu.SemaphoreType.DMA((count,)),
            pltpu.SemaphoreType.DMA((count,)),
        ],
        name="settle",
    )(*arrays)


def whole_layer(**given):
    inputs, vectors = given["inputs"], given["vectors"]
    attn_weights, ffn_weights = given["attn_weights"], given["ffn_weights"]
    results = dict(
        outputs=inputs,
        input_grad=inputs,
        attn_grads=attn_weights,
        ffn_grads=ffn_weights,
        vector_grads=vectors,
        new_attn_weights=attn_weights,
        new_attn_momenta=attn_weights,
        new_ffn_weights=ffn_weights,
        new_ffn_momenta=ffn_weights,
        new_vectors=vectors,
        new_vector_momenta=vectors,
    )
    n = lax.axis_size("group")
    tokens, width = inputs.shape
    rows = attn_weights.shape[1]
    side = 8 * rows
    piece = 2 * rows // n
    half = rows // 2
    bf16, wide = jnp.bfloat16, jnp.float32
    block = (tokens, width)
    narrow = dict(
        own_attn=(rows, width),
        own_ffn=(2, rows, width),
        held=(n, rows, width),
        attn_full=(n, side, width),
        ffn_full=(2, side, width),
        all_cotan=(n, *block),
        all_second=(n, *block),
        query=block,
        keyed=block,
        valued=block,
        active=(n, *block),
        before_grad=(n, *block),
        grad_send=(n, *block),
        grad_recv=(n, *block),
        out_send=(n, *block),
        out_recv=(n - 1, *block),
        ffn_terms=(2, side, width),
        attn_terms=(n, side, width),
        hidden_first=block,
        attended=block,
        middle_b=block,
        query_grad=block,
        key_grad=block,
        value_grad=block,
        piece_send=(n, rows, width),
        piece_recv=(n - 1, rows, width),
        grad_scores=(HEADS // 2, 2 * tokens, tokens),
        near=(6, 4, rows, width),
        total=(6, 4, rows, width),
        recv_b=(6, 4, half, width),
        recv_c=(6, 2, half, width),
        part=(6, 2, half, width),
        grad_attended=block,
        next_own=(3, rows, width),
        next_full=(3, side, width),
        gram_send=(2 * rows, side),
        gram_recv=(n - 1, piece, side),
        gram_all=(2, rows, side),
        gram_full=(2, side, side),
        spread_all=(2 * rows, side),
        spread_in=(rows, side),
        gram_b=(side, side),
        mixed_b=(side, side),
        half_b=(side, side),
    )
    full = dict(
        normed_first=block,
        middle=block,
        normed_second=block,
        probs=(HEADS // 2, 2 * tokens, tokens),
        grad_probs=(HEADS // 2, 2 * tokens, tokens),
        grad_own=block,
        out_own=block,
        grad_middle=block,
        vector_terms=vectors.shape,
        vector_in=(8, *vectors.shape),
        plane_sum=vectors.shape,
        vector_all=(n, *vectors.shape),
        ffn_squares=(2, 2, 8, 128),
        ffn_squares_in=(8, 2, 8, 128),
        ffn_squares_all=(n, 2, 8, 128),
        attn_squares=(1, 8, 128),
        square_sum=(2, 8, 128),
        bias_sum=(1, width),
        attn_squares_in=(8, 8, 128),
        gram=(side, side),
    )
    scratch = {name: pltpu.VMEM(shape, bf16) for name, shape in narrow.items()}
    scratch |= {name: pltpu.VMEM(shape, wide) for name, shape in full.items()}
    copies = 256
    scratch |= dict(
        send_sem=pltpu.SemaphoreType.DMA((copies,)),
        recv_sem=pltpu.SemaphoreType.DMA((copies,)),
    )
    loaded = [(i, name) for i, name in enumerate(given) if name != "lengths"]
    scratch |= {name: pltpu.VMEM(given[name].shape, wide) for _, name in loaded}
    scratch |= dict(load_sem=pltpu.SemaphoreType.DMA((len(loaded),)))
    sources = [name if name == "lengths" else f"from_{name}" for name in given]
    names = (*sources, *results, *scratch)
    anywhere = pl.BlockSpec(memory_space=pl.ANY)
    vmem = pl.BlockSpec(memory_space=pltpu.VMEM)
    smem = pl.BlockSpec(memory_space=pltpu.SMEM)
    arrays = pl.pallas_call(
        lambda *refs: layer_kernel(n, names, loaded, *refs),
        out_shape=[jax.ShapeDtypeStruct(like.shape, wide) for like in results.values()],
        in_specs=[smem if name == "lengths" else anywhere for name in given],
        out_specs=[vmem] * len(results),
        scratch_shapes=list(scratch.values()),
        compiler_params=pltpu.CompilerParams(
            collective_id=20, has_side_effects=True, vmem_limit_bytes=62 * 2**20
        ),
        name="layer",
    )(*given.values())
    return settle(arrays)


def on_device(
    inputs,
    cotangent,
    lengths,
    attn_weights,
    attn_momenta,
    ffn_weights,
    ffn_momenta,
    vectors,
    vector_momenta,
):
    group_count = lax.axis_size("group")
    dp_count = lax.axis_size("dp")
    if dp_count == 8 and group_count == 4 and ffn_weights.shape[2] == inputs.shape[1]:
        return whole_layer(
            inputs=inputs,
            cotangent=cotangent,
            lengths=lengths,
            attn_weights=attn_weights,
            attn_momenta=attn_momenta,
            ffn_weights=ffn_weights,
            ffn_momenta=ffn_momenta,
            vectors=vectors,
            vector_momenta=vector_momenta,
        )
    own_index = lax.axis_index("group")
    dp_index = lax.axis_index("dp")
    token_count, width = inputs.shape
    own_count = attn_weights.shape[1]
    quarter = ffn_weights.shape[2]
    head_size = width // HEADS
    scale = 1.0 / math.sqrt(head_size)
    bf16 = jnp.bfloat16

    own_attn = attn_weights.astype(bf16)
    own_ffn = ffn_weights.astype(bf16)
    cotan_b = cotangent.astype(bf16)
    attn_full, ffn_full, all_cotan = exchange((("chain", 4), own_attn[0]), ("dprow", own_ffn), ("zag", cotan_b)
    )
    w_query, w_key, w_value, w_output = [attn_full[i] for i in range(4)]
    w_expand, w_reduce = [ffn_full[i] for i in range(2)]
    all_cotan = all_cotan.reshape(-1, width)

    positions = jnp.arange(token_count, dtype=jnp.int32)
    order = jnp.arange(lengths.shape[1], dtype=jnp.int32)
    seq_ends = jnp.sum(jnp.where(order[:, None] <= order[None, :], lengths[0][:, None], 0), axis=0)
    segment = jnp.sum((positions[:, None] >= seq_ends[None, :]).astype(jnp.int32), axis=1)
    allowed = (segment[:, None] == segment[None, :]) & (positions[None, :] <= positions[:, None])
    normed_first, inverse_first = norm_forward(inputs)
    hidden_first = (normed_first * vectors[0] + vectors[1]).astype(bf16)
    query = ((mm(hidden_first, w_query, NN) + vectors[2]) * scale).astype(bf16)
    keyed = mm(hidden_first, w_key, NN).astype(bf16)
    valued = (mm(hidden_first, w_value, NN) + vectors[3]).astype(bf16)
    query_heads = query.reshape(token_count, HEADS, head_size)
    key_heads = keyed.reshape(token_count, HEADS, head_size)
    value_heads = valued.reshape(token_count, HEADS, head_size)
    scores = masked_scores(query_heads, key_heads, allowed)
    highest = jnp.max(scores, axis=2, keepdims=True)
    log_total = highest + jnp.log(jnp.sum(jnp.exp(scores - highest), axis=2, keepdims=True))
    probs = jnp.exp(scores - log_total)
    probs_b = probs.astype(bf16)
    attended = jnp.einsum("hqk,khd->qhd", probs_b, value_heads, preferred_element_type=jnp.float32)
    attended = attended.reshape(token_count, width).astype(bf16)
    middle = inputs + mm(attended, w_output, NN) + vectors[4]
    normed_second, inverse_second = norm_forward(middle)
    hidden_second = (normed_second * vectors[5] + vectors[6]).astype(bf16)

    (all_second,) = exchange(("zag", hidden_second))
    all_second = all_second.reshape(-1, width)
    own_bias = lax.dynamic_slice_in_dim(vectors[8:].reshape(-1), own_index * quarter, quarter, 0)
    before = mm(all_second, w_expand, NN) + own_bias
    active = jnp.maximum(before, 0.0).astype(bf16)
    out_part = mm(active, w_reduce, NT).astype(bf16)
    grad_before = jnp.where(before > 0.0, mm(all_cotan, w_reduce, NN), 0.0)
    before_grad_b = grad_before.astype(bf16)
    second_part = mm(before_grad_b, w_expand, NT).astype(bf16)

    ffn_terms = jnp.stack(
        [mm(all_second, before_grad_b, TN).astype(bf16), mm(all_cotan, active, TN).astype(bf16)]
    )
    second_parts, ffn_total = exchange(
        ("za2a", second_part.reshape(group_count, token_count, width)),
        ("dpscatter", ffn_terms),
    )
    total_tokens = float(token_count * dp_count * group_count)
    ffn_grads = ffn_total / total_tokens
    ffn_next = momentum_rate * ffn_momenta + ffn_grads
    ffn_next_b = ffn_next.astype(bf16)
    grad_second = jnp.sum(second_parts.astype(jnp.float32), axis=0)
    grad_middle = cotangent + norm_backward(
        grad_second * vectors[5], normed_second, inverse_second
    )
    middle_b = grad_middle.astype(bf16)
    grad_attended = mm(middle_b, w_output, NT).astype(bf16)
    attended_heads = grad_attended.reshape(token_count, HEADS, head_size)
    grad_probs = jnp.einsum(
        "qhd,khd->hqk", attended_heads, value_heads, preferred_element_type=jnp.float32
    )
    grad_value = jnp.einsum(
        "hqk,qhd->khd", probs_b, attended_heads, preferred_element_type=jnp.float32
    )
    delta = jnp.sum(probs * grad_probs, axis=2, keepdims=True)
    grad_scores = (probs * (grad_probs - delta)).astype(bf16)
    grad_query = (
        jnp.einsum("hqk,khd->qhd", grad_scores, key_heads, preferred_element_type=jnp.float32)
        * scale
    )
    grad_key = jnp.einsum(
        "hqk,qhd->khd", grad_scores, query_heads, preferred_element_type=jnp.float32
    )
    query_grad = grad_query.reshape(token_count, width)
    key_grad = grad_key.reshape(token_count, width)
    value_grad = grad_value.reshape(token_count, width)
    query_grad_b = query_grad.astype(bf16)
    key_grad_b = key_grad.astype(bf16)
    value_grad_b = value_grad.astype(bf16)

    attn_terms = jnp.stack(
        [
            mm(hidden_first, query_grad_b, TN).astype(bf16),
            mm(hidden_first, key_grad_b, TN).astype(bf16),
            mm(hidden_first, value_grad_b, TN).astype(bf16),
            mm(attended, middle_b, TN).astype(bf16),
        ]
    )
    attn_sums, out_parts = exchange(
        ("dpscatter", attn_terms),
        ("za2a", out_part.reshape(group_count, token_count, width)),
    )
    outputs = middle + jnp.sum(out_parts.astype(jnp.float32), axis=0) + vectors[7]
    grad_first = (
        mm(query_grad_b, w_query, NT) + mm(key_grad_b, w_key, NT) + mm(value_grad_b, w_value, NT)
    )
    input_grad = grad_middle + norm_backward(grad_first * vectors[0], normed_first, inverse_first)
    small_terms = jnp.stack(
        [
            jnp.sum(grad_first * normed_first, axis=0),
            jnp.sum(grad_first, axis=0),
            jnp.sum(query_grad, axis=0),
            jnp.sum(value_grad, axis=0),
            jnp.sum(grad_middle, axis=0),
            jnp.sum(grad_second * normed_second, axis=0),
            jnp.sum(grad_second, axis=0),
            jnp.sum(cotangent, axis=0),
        ]
    )
    owner_mask = jnp.arange(group_count, dtype=jnp.int32) == own_index
    bias_terms = jnp.where(owner_mask[:, None], jnp.sum(grad_before, axis=0)[None], 0.0)
    vector_terms = jnp.concatenate([small_terms, bias_terms.reshape(-1, width)], axis=0)
    def square_sums(own):
        sums = jnp.sum(own * own, axis=(1, 2))
        return jnp.broadcast_to(jnp.pad(sums, (0, 8 - own.shape[0]))[:, None], (8, 128))

    attn_pieces, ffn_full_next, vector_all, ffn_squares = exchange(
        ("za2a", attn_sums.astype(bf16)),
        ("dprow", ffn_next_b),
        ("dpag", vector_terms),
        ("dpag", square_sums(ffn_next)),
    )
    attn_grads = jnp.sum(attn_pieces.astype(jnp.float32), axis=0, keepdims=True) / total_tokens
    attn_next = momentum_rate * attn_momenta + attn_grads
    gram_part = jnp.concatenate(
        [mm(ffn_next_b[0], ffn_full_next[0], NT), mm(ffn_next_b[1], ffn_full_next[1], NT)]
    )
    piece = 2 * own_count // group_count
    attn_full_next, gram_pieces, attn_squares, ffn_squares, vector_groups = exchange(
        ("dprow", attn_next.astype(bf16)),
        ("za2a", gram_part.astype(bf16).reshape(group_count, piece, width)),
        ("dpag", square_sums(attn_next)),
        ("zag", jnp.sum(ffn_squares, axis=0)),
        ("zag", jnp.sum(vector_all, axis=0)),
    )
    gram_piece = jnp.sum(gram_pieces.astype(jnp.float32), axis=0).astype(bf16)
    (gram_full,) = exchange((("chain", 2), gram_piece))
    attn_square = jnp.sum(attn_squares, axis=0)[:1, 0]
    ffn_square = jnp.sum(ffn_squares, axis=0)[:2, 0]
    scales = 1.0 / (jnp.sqrt(jnp.concatenate([attn_square, ffn_square])) + 1e-07)
    new_weights = newton_schulz(
        scales,
        dp_index * own_count,
        attn_full_next[0],
        ffn_full_next,
        gram_full,
        jnp.concatenate([attn_next, ffn_next], axis=0),
        jnp.concatenate([attn_weights, ffn_weights], axis=0),
    )
    new_attn_weights = new_weights[:1]
    new_ffn_weights = new_weights[1:]
    vector_grads = jnp.sum(vector_groups, axis=0) / total_tokens
    new_vector_momenta = momentum_rate * vector_momenta + vector_grads
    mean_square = jnp.mean(new_vector_momenta * new_vector_momenta, axis=1, keepdims=True)
    new_vectors = vectors - vector_rate * new_vector_momenta * lax.rsqrt(mean_square + 1e-06)
    return (
        outputs,
        input_grad,
        attn_grads,
        ffn_grads,
        vector_grads,
        new_attn_weights,
        attn_next,
        new_ffn_weights,
        ffn_next,
        new_vectors,
        new_vector_momenta,
    )


def solution(mesh):
    in_specs = (
        P(("dp", "group"), None),
        P(("dp", "group"), None),
        P(("dp", "group"), None),
        P("group", "dp", None),
        P("group", "dp", None),
        P(None, "dp", "group"),
        P(None, "dp", "group"),
        P(),
        P(),
    )
    out_specs = (
        P(("dp", "group"), None),
        P(("dp", "group"), None),
        P("group", "dp", None),
        P(None, "dp", "group"),
        P(),
        P("group", "dp", None),
        P("group", "dp", None),
        P(None, "dp", "group"),
        P(None, "dp", "group"),
        P(),
        P(),
    )
    return jax.shard_map(
        on_device, mesh=mesh, in_specs=in_specs, out_specs=out_specs, check_vma=False
    )
```

```python
import math
import types

import jax
import jax.numpy as jnp
from jax import lax
from jax.experimental import pallas as pl
from jax.experimental.pallas import tpu as pltpu
from jax.sharding import PartitionSpec as P

HEADS = 12
NS_ITERS = 3


coef_first = 3.4445
coef_second = -4.775
coef_third = 2.0315
momentum_rate = 0.9
muon_rate = 0.8
vector_rate = 0.1


def norm_forward(rows):
    centre = jnp.mean(rows, axis=1, keepdims=True)
    centred = rows - centre
    variance = jnp.mean(centred * centred, axis=1, keepdims=True)
    inverse = lax.rsqrt(variance + 1e-05)
    return (centred * inverse, inverse)


def norm_backward(grad_normed, normed, inverse):
    return inverse * (
        grad_normed
        - jnp.mean(grad_normed, axis=1, keepdims=True)
        - normed * jnp.mean(grad_normed * normed, axis=1, keepdims=True)
    )


def masked_scores(query_heads, key_heads, allowed):
    scores = jnp.einsum("qhd,khd->hqk", query_heads, key_heads, preferred_element_type=jnp.float32)
    return jnp.where(allowed[None], scores, -jnp.inf)


MESH = pl.DeviceIdType.MESH


def flip(index, bits):
    result = index
    for bit in (1, 2, 4):
        if bits & bit:
            result = result + bit - 2 * bit * ((index // bit) % 2)
    return result


def exchange(*pairs):
    results = []
    for kind, x in pairs:
        if kind == "zag":
            results.append(lax.all_gather(x, "group", axis=0))
        elif kind == "za2a":
            results.append(lax.all_to_all(x, "group", 0, 0))
        elif kind == "dpag":
            results.append(lax.all_gather(x, "dp", axis=0))
        elif kind == "dprow":
            results.append(lax.all_gather(x, "dp", axis=1, tiled=True))
        elif kind == "dpscatter":
            wide = x.astype(jnp.float32)
            results.append(lax.psum_scatter(wide, "dp", scatter_dimension=1, tiled=True))
        else:
            held = lax.all_gather(x, "group", axis=0).reshape(kind[1], -1, x.shape[1])
            results.append(lax.all_gather(held, "dp", axis=1, tiled=True))
    return results


def mm(left, right, dims):
    return lax.dot_general(left, right, (dims, ((), ())), preferred_element_type=jnp.float32)


NN = ((1,), (0,))
NT = ((1,), (1,))
TN = ((0,), (0,))


def newton_schulz_kernel(
    scale_ref,
    start_ref,
    attn_ref,
    ffn_ref,
    gram_ref,
    own_ref,
    weight_ref,
    out_ref,
    gram,
    gram_b,
    mixed,
    mixed_b,
    half,
    half_b,
):
    rows = own_ref.shape[1]
    mine = pl.ds(pl.multiple_of(start_ref[0], 8), rows)
    bf16 = jnp.bfloat16

    def one(index, whole_b):
        scale = scale_ref[index]
        lead = 1.0
        spread = None
        for iteration in range(NS_ITERS - 1):
            gram_b[...] = gram[...].astype(bf16)
            mixed[...] = coef_second * gram[...] + coef_third * mm(gram_b[...], gram_b[...], NN)
            mixed_b[...] = mixed[...].astype(bf16)
            half[...] = coef_first * gram[...] + mm(mixed_b[...], gram_b[...], NN)
            half_b[...] = half[...].astype(bf16)
            gram[...] = coef_first * half[...] + mm(half_b[...], mixed_b[...], NN)
            if spread is None:
                spread = mixed[mine, :]
            else:
                product = mm(spread.astype(bf16), mixed_b[...], NN)
                spread = coef_first * spread + lead * mixed[mine, :] + product
            lead = lead * coef_first
        gram_b[...] = gram[...].astype(bf16)
        once = lead * gram[mine, :] + mm(spread.astype(bf16), gram_b[...], NN)
        twice = mm(once.astype(bf16), gram_b[...], NN)
        spread = coef_first * spread + coef_second * once + coef_third * twice
        lead = lead * coef_first
        moved = lead * own_ref[index] + mm(spread.astype(bf16), whole_b, NN)
        out_ref[index] = weight_ref[index] - (muon_rate * scale) * moved

    gram[...] = mm(attn_ref[...], attn_ref[...], NT) * (scale_ref[0] * scale_ref[0])
    one(0, attn_ref[...])

    @pl.loop(0, gram_ref.shape[0])
    def _(i):
        gram[...] = gram_ref[i].astype(jnp.float32) * (scale_ref[i + 1] * scale_ref[i + 1])
        one(i + 1, ffn_ref[i])


def newton_schulz(scales, row_start, attn_b, ffn_b, grams, own, weights):
    side = attn_b.shape[0]
    vmem = pl.BlockSpec(memory_space=pltpu.VMEM)
    smem = pl.BlockSpec(memory_space=pltpu.SMEM)
    wide, narrow = pltpu.VMEM((side, side), jnp.float32), pltpu.VMEM((side, side), jnp.bfloat16)
    return pl.pallas_call(
        newton_schulz_kernel,
        out_shape=jax.ShapeDtypeStruct(own.shape, jnp.float32),
        in_specs=[smem, smem, vmem, vmem, vmem, vmem, vmem],
        out_specs=vmem,
        scratch_shapes=[wide, narrow] * 3,
        compiler_params=pltpu.CompilerParams(vmem_limit_bytes=48 * 2**20),
        name="newton_schulz",
    )(scales, jnp.reshape(row_start, (1,)), attn_b, ffn_b, grams, own, weights)


class Net:
    def __init__(self, send_sem, recv_sem, z, d, n):
        self.send_sem, self.recv_sem = send_sem, recv_sem
        self.z, self.d, self.n = z, d, n
        self.slot = 0
        self.copies = []
        self.to_core = {"dp": flip(d, 1)}
        self.to_x = {"dp": flip(d, 2)}
        self.to_y = {"dp": flip(d, 4)}

    def send(self, src, dst, device):
        copy = pltpu.make_async_remote_copy(
            src_ref=src,
            dst_ref=dst,
            send_sem=self.send_sem.at[self.slot],
            recv_sem=self.recv_sem.at[self.slot],
            device_id=device,
            device_id_type=MESH,
        )
        self.slot += 1
        copy.start()
        self.copies.append(copy)
        return copy

    def up(self, k):
        return lax.rem(self.z + k, self.n)

    def down(self, k):
        return lax.rem(self.z + self.n - k, self.n)

    def line(self, src, dst):
        return [self.send(src, dst, {"group": self.up(k)}) for k in range(1, self.n)]

    def plane(self, src, dst):
        return [self.send(src, dst, {"dp": flip(self.d, k)}) for k in range(1, 8)]

    def finish(self):
        for copy in self.copies:
            copy.wait_send()


class Relay:
    def __init__(self, net, blocks):
        self.net, self.blocks, self.base = net, blocks, net.slot
        net.slot += 2 * (net.n - 1)
        self.each(0, lambda copy: copy.start())

    def copy(self, way, steps, origin):
        net = self.net
        slot = self.base + steps + (net.n - 1) * (way < 0)
        return pltpu.make_async_remote_copy(
            src_ref=self.blocks.at[origin],
            dst_ref=self.blocks.at[origin],
            send_sem=net.send_sem.at[slot],
            recv_sem=net.recv_sem.at[slot],
            device_id={"group": net.z + way},
            device_id_type=MESH,
        )

    def each(self, steps, act):
        net = self.net
        z, last = net.z, net.n - 1
        if steps < last:
            pl.when((z >= steps) & (z < last))(lambda: act(self.copy(1, steps, z - steps)))
            pl.when((z + steps <= last) & (z > 0))(lambda: act(self.copy(-1, steps, z + steps)))

    def step(self, steps):
        net = self.net
        z = net.z
        pl.when(z >= steps)(lambda: self.copy(1, steps - 1, z - steps).wait_recv())
        pl.when(z + steps < net.n)(lambda: self.copy(-1, steps - 1, z + steps).wait_recv())
        self.each(steps, lambda copy: copy.start())

    def finish(self):
        for steps in range(self.net.n - 1):
            self.each(steps, lambda copy: copy.wait_send())


class Gather:
    def __init__(self, net, src, full, rows):
        self.net, self.full, self.rows = net, full, rows
        place = self.place(net.d)
        self.x = net.send(src, place, net.to_x)
        self.y = net.send(src, place, net.to_y)
        self.core = net.send(src, place, net.to_core)

    def place(self, index, part=None):
        first = self.rows // 32 * 16
        start, size = index * self.rows, self.rows
        if part is not None:
            start = start + part * first
            size = (first, self.rows - first)[part]
        return self.full.at[pl.ds(pl.multiple_of(start, 16), size), :]

    def second(self):
        net = self.net
        from_x, from_y = flip(net.d, 2), flip(net.d, 4)
        self.x.wait_recv()
        self.via_y = net.send(self.place(from_x, 0), self.place(from_x, 0), net.to_y)
        self.share_x = net.send(self.place(from_x), self.place(from_x), net.to_core)
        self.y.wait_recv()
        self.via_x = net.send(self.place(from_y, 1), self.place(from_y, 1), net.to_x)
        self.share_y = net.send(self.place(from_y), self.place(from_y), net.to_core)

    def third(self):
        net = self.net
        far = flip(net.d, 6)
        self.via_y.wait_recv()
        self.via_x.wait_recv()
        self.share_far = net.send(self.place(far), self.place(far), net.to_core)

    def end(self):
        for copy in (self.core, self.share_x, self.share_y, self.share_far):
            copy.wait_recv()


class Scatter:
    def __init__(self, net, x, near, total, recv_b, recv_c, part):
        self.net, self.x, self.rows = net, x, x.shape[0] // 8
        self.near, self.total, self.recv_b, self.recv_c, self.part = near, total, recv_b, recv_c, part
        self.copies = [
            net.send(self.block(2 * r + 1), near.at[r], net.to_core) for r in (3, 1, 2, 0)
        ]

    def block(self, bits):
        start = pl.multiple_of(flip(self.net.d, bits) * self.rows, 16)
        return self.x.at[pl.ds(start, self.rows), :]

    def second(self):
        net, total = self.net, self.total
        wide = jnp.float32
        half = self.rows // 2
        low, high = pl.ds(0, half), pl.ds(half, half)
        for r, copy in zip((3, 1, 2, 0), self.copies):
            copy.wait_recv()
            own = self.block(2 * r)[...].astype(wide)
            total[r] = (own + self.near[r].astype(wide)).astype(total.dtype)
        self.moved = [
            net.send(total.at[3, low], self.recv_b.at[1], net.to_x),
            net.send(total.at[3, high], self.recv_b.at[3], net.to_y),
            net.send(total.at[1, low], self.recv_b.at[0], net.to_x),
            net.send(total.at[2, high], self.recv_b.at[2], net.to_y),
        ]

    def third(self):
        net, total, part = self.net, self.total, self.part
        wide = jnp.float32
        half = self.rows // 2
        low, high = pl.ds(0, half), pl.ds(half, half)
        self.moved[0].wait_recv()
        part[0] = (total[2, low].astype(wide) + self.recv_b[1].astype(wide)).astype(part.dtype)
        self.ends = [net.send(part.at[0], self.recv_c.at[0], net.to_y)]
        self.moved[1].wait_recv()
        part[1] = (total[1, high].astype(wide) + self.recv_b[3].astype(wide)).astype(part.dtype)
        self.ends.append(net.send(part.at[1], self.recv_c.at[1], net.to_x))

    def end(self):
        total = self.total
        wide = jnp.float32
        half = self.rows // 2
        low, high = pl.ds(0, half), pl.ds(half, half)
        self.moved[2].wait_recv()
        self.moved[3].wait_recv()
        self.ends[0].wait_recv()
        self.ends[1].wait_recv()
        first = total[0, low].astype(wide) + self.recv_b[0].astype(wide) + self.recv_c[0].astype(wide)
        second = total[0, high].astype(wide) + self.recv_b[2].astype(wide) + self.recv_c[1].astype(wide)
        return jnp.concatenate([first, second], axis=0)


def muon_steps(gram, gram_b, mixed_b, half_b, mine, finish):
    bf16 = jnp.bfloat16
    lead = 1.0
    spread = None
    for iteration in range(NS_ITERS - 1):
        gram_b[...] = gram[...].astype(bf16)
        own_gram = gram[mine, :]
        mixed_b[...] = (coef_second * gram[...] + coef_third * mm(gram_b[...], gram_b[...], NN)).astype(
            bf16
        )
        yield
        own_mixed = coef_second * own_gram + coef_third * mm(own_gram.astype(bf16), gram_b[...], NN)
        gram[...] = coef_first * gram[...] + mm(mixed_b[...], gram_b[...], NN)
        half_b[...] = gram[...].astype(bf16)
        yield
        gram[...] = coef_first * gram[...] + mm(half_b[...], mixed_b[...], NN)
        if spread is None:
            spread = own_mixed
        else:
            product = mm(spread.astype(bf16), mixed_b[...], NN)
            spread = coef_first * spread + lead * own_mixed + product
        lead = lead * coef_first
        yield
    gram_b[...] = gram[...].astype(bf16)
    once = lead * gram[mine, :] + mm(spread.astype(bf16), gram_b[...], NN)
    twice = mm(once.astype(bf16), gram_b[...], NN)
    spread = coef_first * spread + coef_second * once + coef_third * twice
    lead = lead * coef_first
    finish(spread.astype(bf16), lead)
    yield


def layer_kernel(n, names, loaded, *refs):
    ref = types.SimpleNamespace(**dict(zip(names, refs)))
    bf16, wide = jnp.bfloat16, jnp.float32
    z, d = lax.axis_index("group"), lax.axis_index("dp")
    net = Net(ref.send_sem, ref.recv_sem, z, d, n)
    lengths, vectors = ref.lengths, ref.vectors
    loads = {
        name: pltpu.make_async_copy(refs[i], vars(ref)[name], ref.load_sem.at[j])
        for j, (i, name) in enumerate(loaded)
    }
    for copy in loads.values():
        copy.start()

    def arrived(*wanted):
        for name in wanted:
            loads.pop(name).wait()

    tokens, width = ref.inputs.shape
    rows = ref.attn_weights.shape[1]
    head_size = width // HEADS
    pairs = HEADS // 2
    pair_width = 2 * head_size
    scale = 1.0 / math.sqrt(head_size)
    total_tokens = float(tokens * 8 * n)
    ranks = range(1, n)

    def vector(i):
        return vectors[pl.ds(i, 1), :]

    def column_sum(x):
        return jnp.sum(x, axis=0, keepdims=True)

    barrier = pltpu.get_barrier_semaphore()
    for k in ranks:
        pl.semaphore_signal(barrier, inc=1, device_id={"group": net.up(k)}, device_id_type=MESH)
    for k in range(1, 8):
        pl.semaphore_signal(barrier, inc=1, device_id={"dp": flip(d, k)}, device_id_type=MESH)

    own_attn, own_ffn = ref.own_attn, ref.own_ffn
    held, attn_full, ffn_full = ref.held, ref.attn_full, ref.ffn_full
    arrived("attn_weights")
    own_attn[...] = ref.attn_weights[0].astype(bf16)
    all_cotan, all_second = ref.all_cotan, ref.all_second

    pl.semaphore_wait(barrier, n - 1 + 7)

    chain = net.line(own_attn, held.at[z])
    own_rows = pl.ds(pl.multiple_of(d * rows, 16), rows)

    weights = [Gather(net, own_attn, attn_full.at[z], rows)]
    arrived("ffn_weights")
    own_ffn[...] = ref.ffn_weights[...].astype(bf16)
    ffn_weights = [Gather(net, own_ffn.at[0], ffn_full.at[0], rows)]
    arrived(*list(loads))
    all_cotan[z] = ref.cotangent[...].astype(bf16)
    for i in range(2):
        ffn_full[i, own_rows, :] = own_ffn[i]
    attn_full[z, own_rows, :] = own_attn[...]

    centre = jnp.mean(ref.inputs[...], axis=1, keepdims=True)
    centred = ref.inputs[...] - centre
    inverse_first = lax.rsqrt(jnp.mean(centred * centred, axis=1, keepdims=True) + 1e-05)
    ref.normed_first[...] = centred * inverse_first
    hidden_first, attended = ref.hidden_first, ref.attended
    hidden_first[...] = (ref.normed_first[...] * vector(0) + vector(1)).astype(bf16)

    for k in ranks:
        origin = net.down(k)
        chain[k - 1].wait_recv()
        weights.append(Gather(net, held.at[origin], attn_full.at[origin], rows))
        attn_full[origin, own_rows, :] = held[origin]
        if k == 1:
            weights[0].second()
    cotan_copies = net.line(all_cotan.at[z], all_cotan.at[z])
    for gather in weights[1:]:
        gather.second()
    ffn_weights.append(Gather(net, own_ffn.at[1], ffn_full.at[1], rows))
    for gather in weights:
        gather.third()
    for gather in ffn_weights:
        gather.second()
    for gather in weights:
        gather.end()
    for gather in ffn_weights:
        gather.third()

    lane = lax.broadcasted_iota(jnp.int32, (tokens, pair_width), 1)
    low_lane = lane < head_size
    ones = lax.broadcasted_iota(jnp.int32, (1, pair_width), 1) < head_size
    low_mask = jnp.where(ones, 1.0, 0.0).astype(bf16)
    high_mask = jnp.where(ones, 0.0, 1.0).astype(bf16)

    def split(x):
        return jnp.concatenate([x * low_mask, x * high_mask], axis=0)

    def join(x):
        return jnp.where(low_lane, x[:tokens], x[tokens:])

    query, keyed, valued = ref.query, ref.keyed, ref.valued
    query[...] = ((mm(hidden_first[...], attn_full[0], NN) + vector(2)) * scale).astype(bf16)
    keyed[...] = mm(hidden_first[...], attn_full[1], NN).astype(bf16)
    valued[...] = (mm(hidden_first[...], attn_full[2], NN) + vector(3)).astype(bf16)

    at_row = lax.broadcasted_iota(jnp.int32, (2 * tokens, tokens), 0)
    at_row = jnp.where(at_row < tokens, at_row, at_row - tokens)
    at_column = lax.broadcasted_iota(jnp.int32, (2 * tokens, tokens), 1)
    row_part = jnp.zeros_like(at_row)
    column_part = jnp.zeros_like(at_column)
    edge = 0
    for i in range(lengths.shape[1]):
        edge = edge + lengths[0, i]
        row_part = row_part + jnp.where(at_row >= edge, 1, 0)
        column_part = column_part + jnp.where(at_column >= edge, 1, 0)
    allowed = (row_part == column_part) & (at_column <= at_row)

    probs = ref.probs
    slices = [pl.ds(p * pair_width, pair_width) for p in range(pairs)]
    for p, lanes in enumerate(slices):
        scores = mm(split(query[:, lanes]), keyed[:, lanes], NT)
        probs[p] = jnp.where(allowed, scores, -jnp.inf)
    for p in range(pairs):
        raised = jnp.exp(probs[p] - jnp.max(probs[p], axis=1, keepdims=True))
        probs[p] = raised * (1.0 / jnp.sum(raised, axis=1, keepdims=True))
    for p, lanes in enumerate(slices):
        attended[:, lanes] = join(mm(probs[p].astype(bf16), valued[:, lanes], NN)).astype(bf16)

    middle = ref.middle
    middle[...] = ref.inputs[...] + mm(attended[...], attn_full[3], NN) + vector(4)
    centre = jnp.mean(middle[...], axis=1, keepdims=True)
    centred = middle[...] - centre
    inverse_second = lax.rsqrt(jnp.mean(centred * centred, axis=1, keepdims=True) + 1e-05)
    normed_second = ref.normed_second
    normed_second[...] = centred * inverse_second
    all_second[z] = (normed_second[...] * vector(5) + vector(6)).astype(bf16)
    relay = Relay(net, all_second)
    for gather in ffn_weights:
        gather.end()

    active, before_grad = ref.active, ref.before_grad
    grad_send, grad_recv, grad_own = ref.grad_send, ref.grad_recv, ref.grad_own
    out_send, out_recv, out_own = ref.out_send, ref.out_recv, ref.out_own
    bias_sum = ref.bias_sum
    bias_sum[...] = jnp.zeros_like(bias_sum)
    grad_slot = net.slot
    net.slot += n

    def grad_copy(origin, sender):
        return pltpu.make_async_remote_copy(
            src_ref=grad_send.at[origin],
            dst_ref=grad_recv.at[sender],
            send_sem=net.send_sem.at[grad_slot + origin],
            recv_sem=net.recv_sem.at[grad_slot + sender],
            device_id={"group": origin},
            device_id_type=MESH,
        )

    def feed_forward(origin, own):
        before = mm(all_second[origin], ffn_full[0], NN) + vector(8 + z)
        active[origin] = jnp.maximum(before, 0.0).astype(bf16)
        grad_before = jnp.where(before > 0.0, mm(all_cotan[origin], ffn_full[1], NN), 0.0)
        bias_sum[...] = bias_sum[...] + column_sum(grad_before)
        before_grad[origin] = grad_before.astype(bf16)
        second = mm(before_grad[origin], ffn_full[0], NT)
        if own:
            grad_own[...] = second
        else:
            grad_send[origin] = second.astype(bf16)
            grad_copy(origin, z).start()
        out = mm(active[origin], ffn_full[1], NT)
        if own:
            out_own[...] = out
        else:
            out_send[origin] = out.astype(bf16)

    feed_forward(z, True)
    for copy in cotan_copies:
        copy.wait_recv()
    for steps in ranks:
        relay.step(steps)
        pl.when(z >= steps)(lambda: feed_forward(z - steps, False))
        pl.when(z + steps < n)(lambda: feed_forward(z + steps, False))

    def scatter(x, slot):
        pools = (ref.near, ref.total, ref.recv_b, ref.recv_c, ref.part)
        return Scatter(net, x, *[pool.at[slot] for pool in pools])

    ffn_terms, attn_terms = ref.ffn_terms, ref.attn_terms
    many = n * tokens
    ffn_terms[0] = mm(
        all_second[...].reshape(many, width), before_grad[...].reshape(many, width), TN
    ).astype(bf16)
    ffn_sums = [scatter(ffn_terms.at[0], 0)]
    ffn_terms[1] = mm(
        all_cotan[...].reshape(many, width), active[...].reshape(many, width), TN
    ).astype(bf16)
    ffn_sums.append(scatter(ffn_terms.at[1], 1))
    for part in ffn_sums:
        part.second()
    for part in ffn_sums:
        part.third()

    next_own, next_full = ref.next_own, ref.next_full
    ffn_squares, attn_squares = ref.ffn_squares, ref.attn_squares

    def square(x):
        return jnp.broadcast_to(jnp.sum(column_sum(x * x), axis=1, keepdims=True), (8, 128))

    ffn_nexts = []
    for i in range(2):
        grad = ffn_sums[i].end() / total_tokens
        ref.ffn_grads[i] = grad
        moment = momentum_rate * ref.ffn_momenta[i] + grad
        ref.new_ffn_momenta[i] = moment
        next_own[1 + i] = moment.astype(bf16)
        ffn_nexts.append(Gather(net, next_own.at[1 + i], next_full.at[1 + i], rows))
        next_full[1 + i, own_rows, :] = next_own[1 + i]
        ffn_squares[0, i] = square(moment)
    square_copies = net.plane(ffn_squares.at[0], ref.ffn_squares_in.at[d])

    total = grad_own[...]
    for k in ranks:
        grad_copy(z, net.up(k)).wait_recv()
        total = total + grad_recv[net.up(k)].astype(wide)
    out_copies = [
        net.send(out_send.at[net.down(k)], out_recv.at[k - 1], {"group": net.down(k)}) for k in ranks
    ]
    terms = ref.vector_terms
    terms[...] = jnp.zeros_like(terms)

    def put(i, x):
        terms[pl.ds(i, 1), :] = x

    def norm_back(grad, normed, inverse):
        return inverse * (
            grad
            - jnp.mean(grad, axis=1, keepdims=True)
            - normed * jnp.mean(grad * normed, axis=1, keepdims=True)
        )

    put(8 + z, bias_sum[...])
    put(5, column_sum(total * normed_second[...]))
    put(6, column_sum(total))
    put(7, column_sum(ref.cotangent[...]))
    grad_middle = ref.grad_middle
    grad_middle[...] = ref.cotangent[...] + norm_back(
        total * vector(5), normed_second[...], inverse_second
    )
    put(4, column_sum(grad_middle[...]))
    middle_b = ref.middle_b
    middle_b[...] = grad_middle[...].astype(bf16)
    attn_terms[3] = mm(attended[...], middle_b[...], TN).astype(bf16)
    attn_sums = [scatter(attn_terms.at[3], 5)]
    grad_attended = ref.grad_attended
    grad_attended[...] = mm(middle_b[...], attn_full[3], NT).astype(bf16)
    grads = [ref.query_grad, ref.key_grad, ref.value_grad]
    pulls, pushes = ref.grad_probs, ref.grad_scores
    for p, lanes in enumerate(slices):
        pulls[p] = mm(split(grad_attended[:, lanes]), valued[:, lanes], NT)
    for p in range(pairs):
        delta = jnp.sum(probs[p] * pulls[p], axis=1, keepdims=True)
        pushes[p] = (probs[p] * (pulls[p] - delta)).astype(bf16)
    for gather in ffn_nexts:
        gather.second()
    attn_sums[0].second()
    for p, lanes in enumerate(slices):
        grad_value = mm(probs[p].astype(bf16), split(grad_attended[:, lanes]), TN)
        grad_query = join(mm(pushes[p], keyed[:, lanes], NN)) * scale
        grad_key = mm(pushes[p], split(query[:, lanes]), TN)
        terms[pl.ds(2, 1), lanes] = column_sum(grad_query)
        terms[pl.ds(3, 1), lanes] = column_sum(grad_value)
        grads[0][:, lanes] = grad_query.astype(bf16)
        grads[1][:, lanes] = grad_key.astype(bf16)
        grads[2][:, lanes] = grad_value.astype(bf16)
    for m in range(3):
        attn_terms[m] = mm(hidden_first[...], grads[m][...], TN).astype(bf16)
        attn_sums.append(scatter(attn_terms.at[m], 2 + m))
    for gather in ffn_nexts:
        gather.third()
    for part in attn_sums[1:]:
        part.second()
    attn_sums[0].third()

    gram_send, gram_recv = ref.gram_send, ref.gram_recv
    piece = 2 * rows // n
    for i in range(2):
        ffn_nexts[i].end()
        gram_send[pl.ds(i * rows, rows), :] = mm(next_own[1 + i], next_full[1 + i], NT).astype(bf16)

    def gram_rows(index):
        return gram_send.at[pl.ds(pl.multiple_of(index * piece, 16), piece), :]

    gram_copies = [
        net.send(gram_rows(net.up(k)), gram_recv.at[k - 1], {"group": net.up(k)}) for k in ranks
    ]

    grad_first = mm(grads[0][...], attn_full[0], NT)
    grad_first = grad_first + mm(grads[1][...], attn_full[1], NT)
    grad_first = grad_first + mm(grads[2][...], attn_full[2], NT)
    put(0, column_sum(grad_first * ref.normed_first[...]))
    put(1, column_sum(grad_first))
    ref.input_grad[...] = grad_middle[...] + norm_back(
        grad_first * vector(0), ref.normed_first[...], inverse_first
    )
    vector_in = ref.vector_in
    vector_copies = net.plane(terms, vector_in.at[d])

    gram_sum = gram_rows(z)[...].astype(wide)
    for k in ranks:
        gram_copies[k - 1].wait_recv()
        gram_sum = gram_sum + gram_recv[k - 1].astype(wide)
    gram_all, gram_full = ref.gram_all, ref.gram_full
    per = n // 2
    own_piece = gram_all.at[z // per, pl.ds(pl.multiple_of(lax.rem(z, per) * piece, 16), piece), :]
    own_piece[...] = gram_sum.astype(bf16)
    gram_line = net.line(own_piece, own_piece)

    for part in attn_sums[1:]:
        part.third()

    piece_send, piece_recv = ref.piece_send, ref.piece_recv
    for m, part in zip((3, 0, 1, 2), attn_sums):
        piece_send[m] = part.end().astype(bf16)
    piece_copies = [
        net.send(piece_send.at[net.up(k)], piece_recv.at[k - 1], {"group": net.up(k)}) for k in ranks
    ]

    for copy in gram_line:
        copy.wait_recv()
    grams = []
    for i in range(2):
        grams.append(Gather(net, gram_all.at[i], gram_full.at[i], rows))
        gram_full[i, own_rows, :] = gram_all[i]

    plane_sum = ref.plane_sum
    square_in = ref.ffn_squares_in
    square_total = ffn_squares[0]
    for k in range(1, 8):
        square_copies[k - 1].wait_recv()
        square_total = square_total + square_in[flip(d, k)]
    ffn_squares[1] = square_total
    plane_squares = net.line(ffn_squares.at[1], ref.ffn_squares_all.at[z])
    vector_total = terms[...]
    for k in range(1, 8):
        vector_copies[k - 1].wait_recv()
        vector_total = vector_total + vector_in[flip(d, k)]
    plane_sum[...] = vector_total
    vector_all = net.line(plane_sum, ref.vector_all.at[z])

    result = out_own[...] + middle[...] + vector(7)
    for k in ranks:
        out_copies[k - 1].wait_recv()
        result = result + out_recv[k - 1].astype(wide)
    ref.outputs[...] = result

    for gather in grams:
        gather.second()
    grad = piece_send[z].astype(wide)
    for k in ranks:
        piece_copies[k - 1].wait_recv()
        grad = grad + piece_recv[k - 1].astype(wide)
    grad = grad / total_tokens
    ref.attn_grads[0] = grad
    moment = momentum_rate * ref.attn_momenta[0] + grad
    ref.new_attn_momenta[0] = moment
    next_own[0] = moment.astype(bf16)
    attn_next = Gather(net, next_own.at[0], next_full.at[0], rows)
    next_full[0, own_rows, :] = next_own[0]
    attn_squares[0] = square(moment)
    own_squares = net.plane(attn_squares.at[0], ref.attn_squares_in.at[d])
    for gather in grams:
        gather.third()

    gram, gram_b, mixed_b, half_b = ref.gram, ref.gram_b, ref.mixed_b, ref.half_b

    def inverse_norm(x):
        return 1.0 / (jnp.sqrt(x[0:1, 0:1]) + 1e-07)

    square_total = ffn_squares[1]
    for k in ranks:
        plane_squares[k - 1].wait_recv()
        square_total = square_total + ref.ffn_squares_all[net.down(k)]

    square_sum = ref.square_sum
    square_sum[...] = square_total
    core = lax.rem(d, 2)
    both_rows = pl.ds(pl.multiple_of((d // 2) * 2 * rows, 16), 2 * rows)
    spread_all, spread_in = ref.spread_all, ref.spread_in
    leads = []

    def half_of(index):
        return spread_all.at[pl.ds(pl.multiple_of(index * rows, 16), rows), :]

    def exchange_spread(spread, lead):
        spread_all[...] = spread
        leads.append(lead)

    for gather in grams:
        gather.end()
    own_scale = inverse_norm(square_sum[core])
    gram[...] = gram_full[core].astype(wide) * (own_scale * own_scale)
    steps = muon_steps(gram, gram_b, mixed_b, half_b, both_rows, exchange_spread)
    next(steps)
    attn_next.second()
    next(steps)
    next(steps)
    attn_next.third()
    for _ in steps:
        pass
    spread_copy = net.send(half_of(1 - core), spread_in, net.to_core)

    def ffn_update(index, spread):
        own_scale = inverse_norm(square_sum[index])
        moved = leads[0] * ref.new_ffn_momenta[index] + mm(spread, next_full[1 + index], NN)
        ref.new_ffn_weights[index] = ref.ffn_weights[index] - (muon_rate * own_scale) * moved

    ffn_update(core, half_of(core)[...])

    vector_total = plane_sum[...]
    for k in ranks:
        vector_all[k - 1].wait_recv()
        vector_total = vector_total + ref.vector_all[net.down(k)]
    vector_total = vector_total / total_tokens
    ref.vector_grads[...] = vector_total
    moment = momentum_rate * ref.vector_momenta[...] + vector_total
    ref.new_vector_momenta[...] = moment
    mean_square = jnp.mean(moment * moment, axis=1, keepdims=True)
    ref.new_vectors[...] = vectors[...] - vector_rate * moment * lax.rsqrt(mean_square + 1e-06)

    attn_next.end()
    square_total = attn_squares[0]
    for k in range(1, 8):
        own_squares[k - 1].wait_recv()
        square_total = square_total + ref.attn_squares_in[flip(d, k)]
    own_scale = inverse_norm(square_total)
    gram[...] = mm(next_full[0], next_full[0], NT) * (own_scale * own_scale)
    own_muon = muon_rate * own_scale

    def attn_update(spread, lead):
        moved = lead * ref.new_attn_momenta[0] + mm(spread, next_full[0], NN)
        ref.new_attn_weights[0] = ref.attn_weights[0] - own_muon * moved

    for _ in muon_steps(gram, gram_b, mixed_b, half_b, own_rows, attn_update):
        pass
    spread_copy.wait_recv()
    ffn_update(1 - core, spread_in[...])
    relay.finish()
    for k in ranks:
        grad_copy(net.up(k), z).wait_send()
    net.finish()


def settle_kernel(count, *refs):
    sources, targets, held = refs[:count], refs[count : 2 * count], refs[2 * count : 3 * count]
    sem_in, sem_out = refs[3 * count :]
    reads = [pltpu.make_async_copy(sources[i], held[i], sem_in.at[i]) for i in range(count)]
    writes = [pltpu.make_async_copy(held[i], targets[i], sem_out.at[i]) for i in range(count)]
    for copy in reads:
        copy.start()
    for read, write in zip(reads, writes):
        read.wait()
        write.start()
    for copy in writes:
        copy.wait()


def settle(arrays):
    count = len(arrays)
    anywhere = pl.BlockSpec(memory_space=pl.ANY)
    return pl.pallas_call(
        lambda *refs: settle_kernel(count, *refs),
        out_shape=[jax.ShapeDtypeStruct(x.shape, x.dtype) for x in arrays],
        in_specs=[anywhere] * count,
        out_specs=[anywhere] * count,
        scratch_shapes=[
            *[pltpu.VMEM(x.shape, x.dtype) for x in arrays],
            pltpu.SemaphoreType.DMA((count,)),
            pltpu.SemaphoreType.DMA((count,)),
        ],
        name="settle",
    )(*arrays)


def whole_layer(**given):
    inputs, vectors = given["inputs"], given["vectors"]
    attn_weights, ffn_weights = given["attn_weights"], given["ffn_weights"]
    results = dict(
        outputs=inputs,
        input_grad=inputs,
        attn_grads=attn_weights,
        ffn_grads=ffn_weights,
        vector_grads=vectors,
        new_attn_weights=attn_weights,
        new_attn_momenta=attn_weights,
        new_ffn_weights=ffn_weights,
        new_ffn_momenta=ffn_weights,
        new_vectors=vectors,
        new_vector_momenta=vectors,
    )
    n = lax.axis_size("group")
    tokens, width = inputs.shape
    rows = attn_weights.shape[1]
    side = 8 * rows
    piece = 2 * rows // n
    half = rows // 2
    bf16, wide = jnp.bfloat16, jnp.float32
    block = (tokens, width)
    narrow = dict(
        own_attn=(rows, width),
        own_ffn=(2, rows, width),
        held=(n, rows, width),
        attn_full=(n, side, width),
        ffn_full=(2, side, width),
        all_cotan=(n, *block),
        all_second=(n, *block),
        query=block,
        keyed=block,
        valued=block,
        active=(n, *block),
        before_grad=(n, *block),
        grad_send=(n, *block),
        grad_recv=(n, *block),
        out_send=(n, *block),
        out_recv=(n - 1, *block),
        ffn_terms=(2, side, width),
        attn_terms=(n, side, width),
        hidden_first=block,
        attended=block,
        middle_b=block,
        query_grad=block,
        key_grad=block,
        value_grad=block,
        piece_send=(n, rows, width),
        piece_recv=(n - 1, rows, width),
        grad_scores=(HEADS // 2, 2 * tokens, tokens),
        near=(6, 4, rows, width),
        total=(6, 4, rows, width),
        recv_b=(6, 4, half, width),
        recv_c=(6, 2, half, width),
        part=(6, 2, half, width),
        grad_attended=block,
        next_own=(3, rows, width),
        next_full=(3, side, width),
        gram_send=(2 * rows, side),
        gram_recv=(n - 1, piece, side),
        gram_all=(2, rows, side),
        gram_full=(2, side, side),
        spread_all=(2 * rows, side),
        spread_in=(rows, side),
        gram_b=(side, side),
        mixed_b=(side, side),
        half_b=(side, side),
    )
    full = dict(
        normed_first=block,
        middle=block,
        normed_second=block,
        probs=(HEADS // 2, 2 * tokens, tokens),
        grad_probs=(HEADS // 2, 2 * tokens, tokens),
        grad_own=block,
        out_own=block,
        grad_middle=block,
        vector_terms=vectors.shape,
        vector_in=(8, *vectors.shape),
        plane_sum=vectors.shape,
        vector_all=(n, *vectors.shape),
        ffn_squares=(2, 2, 8, 128),
        ffn_squares_in=(8, 2, 8, 128),
        ffn_squares_all=(n, 2, 8, 128),
        attn_squares=(1, 8, 128),
        square_sum=(2, 8, 128),
        bias_sum=(1, width),
        attn_squares_in=(8, 8, 128),
        gram=(side, side),
    )
    scratch = {name: pltpu.VMEM(shape, bf16) for name, shape in narrow.items()}
    scratch |= {name: pltpu.VMEM(shape, wide) for name, shape in full.items()}
    copies = 256
    scratch |= dict(
        send_sem=pltpu.SemaphoreType.DMA((copies,)),
        recv_sem=pltpu.SemaphoreType.DMA((copies,)),
    )
    loaded = [(i, name) for i, name in enumerate(given) if name != "lengths"]
    scratch |= {name: pltpu.VMEM(given[name].shape, wide) for _, name in loaded}
    scratch |= dict(load_sem=pltpu.SemaphoreType.DMA((len(loaded),)))
    sources = [name if name == "lengths" else f"from_{name}" for name in given]
    names = (*sources, *results, *scratch)
    anywhere = pl.BlockSpec(memory_space=pl.ANY)
    vmem = pl.BlockSpec(memory_space=pltpu.VMEM)
    smem = pl.BlockSpec(memory_space=pltpu.SMEM)
    arrays = pl.pallas_call(
        lambda *refs: layer_kernel(n, names, loaded, *refs),
        out_shape=[jax.ShapeDtypeStruct(like.shape, wide) for like in results.values()],
        in_specs=[smem if name == "lengths" else anywhere for name in given],
        out_specs=[vmem] * len(results),
        scratch_shapes=list(scratch.values()),
        compiler_params=pltpu.CompilerParams(
            collective_id=20, has_side_effects=True, vmem_limit_bytes=62 * 2**20
        ),
        name="layer",
    )(*given.values())
    return settle(arrays)


def on_device(
    inputs,
    cotangent,
    lengths,
    attn_weights,
    attn_momenta,
    ffn_weights,
    ffn_momenta,
    vectors,
    vector_momenta,
):
    group_count = lax.axis_size("group")
    dp_count = lax.axis_size("dp")
    if dp_count == 8 and group_count == 4 and ffn_weights.shape[2] == inputs.shape[1]:
        return whole_layer(
            inputs=inputs,
            cotangent=cotangent,
            lengths=lengths,
            attn_weights=attn_weights,
            attn_momenta=attn_momenta,
            ffn_weights=ffn_weights,
            ffn_momenta=ffn_momenta,
            vectors=vectors,
            vector_momenta=vector_momenta,
        )
    own_index = lax.axis_index("group")
    dp_index = lax.axis_index("dp")
    token_count, width = inputs.shape
    own_count = attn_weights.shape[1]
    quarter = ffn_weights.shape[2]
    head_size = width // HEADS
    scale = 1.0 / math.sqrt(head_size)
    bf16 = jnp.bfloat16

    own_attn = attn_weights.astype(bf16)
    own_ffn = ffn_weights.astype(bf16)
    cotan_b = cotangent.astype(bf16)
    attn_full, ffn_full, all_cotan = exchange((("chain", 4), own_attn[0]), ("dprow", own_ffn), ("zag", cotan_b)
    )
    w_query, w_key, w_value, w_output = [attn_full[i] for i in range(4)]
    w_expand, w_reduce = [ffn_full[i] for i in range(2)]
    all_cotan = all_cotan.reshape(-1, width)

    positions = jnp.arange(token_count, dtype=jnp.int32)
    order = jnp.arange(lengths.shape[1], dtype=jnp.int32)
    seq_ends = jnp.sum(jnp.where(order[:, None] <= order[None, :], lengths[0][:, None], 0), axis=0)
    segment = jnp.sum((positions[:, None] >= seq_ends[None, :]).astype(jnp.int32), axis=1)
    allowed = (segment[:, None] == segment[None, :]) & (positions[None, :] <= positions[:, None])
    normed_first, inverse_first = norm_forward(inputs)
    hidden_first = (normed_first * vectors[0] + vectors[1]).astype(bf16)
    query = ((mm(hidden_first, w_query, NN) + vectors[2]) * scale).astype(bf16)
    keyed = mm(hidden_first, w_key, NN).astype(bf16)
    valued = (mm(hidden_first, w_value, NN) + vectors[3]).astype(bf16)
    query_heads = query.reshape(token_count, HEADS, head_size)
    key_heads = keyed.reshape(token_count, HEADS, head_size)
    value_heads = valued.reshape(token_count, HEADS, head_size)
    scores = masked_scores(query_heads, key_heads, allowed)
    highest = jnp.max(scores, axis=2, keepdims=True)
    log_total = highest + jnp.log(jnp.sum(jnp.exp(scores - highest), axis=2, keepdims=True))
    probs = jnp.exp(scores - log_total)
    probs_b = probs.astype(bf16)
    attended = jnp.einsum("hqk,khd->qhd", probs_b, value_heads, preferred_element_type=jnp.float32)
    attended = attended.reshape(token_count, width).astype(bf16)
    middle = inputs + mm(attended, w_output, NN) + vectors[4]
    normed_second, inverse_second = norm_forward(middle)
    hidden_second = (normed_second * vectors[5] + vectors[6]).astype(bf16)

    (all_second,) = exchange(("zag", hidden_second))
    all_second = all_second.reshape(-1, width)
    own_bias = lax.dynamic_slice_in_dim(vectors[8:].reshape(-1), own_index * quarter, quarter, 0)
    before = mm(all_second, w_expand, NN) + own_bias
    active = jnp.maximum(before, 0.0).astype(bf16)
    out_part = mm(active, w_reduce, NT).astype(bf16)
    grad_before = jnp.where(before > 0.0, mm(all_cotan, w_reduce, NN), 0.0)
    before_grad_b = grad_before.astype(bf16)
    second_part = mm(before_grad_b, w_expand, NT).astype(bf16)

    ffn_terms = jnp.stack(
        [mm(all_second, before_grad_b, TN).astype(bf16), mm(all_cotan, active, TN).astype(bf16)]
    )
    second_parts, ffn_total = exchange(
        ("za2a", second_part.reshape(group_count, token_count, width)),
        ("dpscatter", ffn_terms),
    )
    total_tokens = float(token_count * dp_count * group_count)
    ffn_grads = ffn_total / total_tokens
    ffn_next = momentum_rate * ffn_momenta + ffn_grads
    ffn_next_b = ffn_next.astype(bf16)
    grad_second = jnp.sum(second_parts.astype(jnp.float32), axis=0)
    grad_middle = cotangent + norm_backward(
        grad_second * vectors[5], normed_second, inverse_second
    )
    middle_b = grad_middle.astype(bf16)
    grad_attended = mm(middle_b, w_output, NT).astype(bf16)
    attended_heads = grad_attended.reshape(token_count, HEADS, head_size)
    grad_probs = jnp.einsum(
        "qhd,khd->hqk", attended_heads, value_heads, preferred_element_type=jnp.float32
    )
    grad_value = jnp.einsum(
        "hqk,qhd->khd", probs_b, attended_heads, preferred_element_type=jnp.float32
    )
    delta = jnp.sum(probs * grad_probs, axis=2, keepdims=True)
    grad_scores = (probs * (grad_probs - delta)).astype(bf16)
    grad_query = (
        jnp.einsum("hqk,khd->qhd", grad_scores, key_heads, preferred_element_type=jnp.float32)
        * scale
    )
    grad_key = jnp.einsum(
        "hqk,qhd->khd", grad_scores, query_heads, preferred_element_type=jnp.float32
    )
    query_grad = grad_query.reshape(token_count, width)
    key_grad = grad_key.reshape(token_count, width)
    value_grad = grad_value.reshape(token_count, width)
    query_grad_b = query_grad.astype(bf16)
    key_grad_b = key_grad.astype(bf16)
    value_grad_b = value_grad.astype(bf16)

    attn_terms = jnp.stack(
        [
            mm(hidden_first, query_grad_b, TN).astype(bf16),
            mm(hidden_first, key_grad_b, TN).astype(bf16),
            mm(hidden_first, value_grad_b, TN).astype(bf16),
            mm(attended, middle_b, TN).astype(bf16),
        ]
    )
    attn_sums, out_parts = exchange(
        ("dpscatter", attn_terms),
        ("za2a", out_part.reshape(group_count, token_count, width)),
    )
    outputs = middle + jnp.sum(out_parts.astype(jnp.float32), axis=0) + vectors[7]
    grad_first = (
        mm(query_grad_b, w_query, NT) + mm(key_grad_b, w_key, NT) + mm(value_grad_b, w_value, NT)
    )
    input_grad = grad_middle + norm_backward(grad_first * vectors[0], normed_first, inverse_first)
    small_terms = jnp.stack(
        [
            jnp.sum(grad_first * normed_first, axis=0),
            jnp.sum(grad_first, axis=0),
            jnp.sum(query_grad, axis=0),
            jnp.sum(value_grad, axis=0),
            jnp.sum(grad_middle, axis=0),
            jnp.sum(grad_second * normed_second, axis=0),
            jnp.sum(grad_second, axis=0),
            jnp.sum(cotangent, axis=0),
        ]
    )
    owner_mask = jnp.arange(group_count, dtype=jnp.int32) == own_index
    bias_terms = jnp.where(owner_mask[:, None], jnp.sum(grad_before, axis=0)[None], 0.0)
    vector_terms = jnp.concatenate([small_terms, bias_terms.reshape(-1, width)], axis=0)
    def square_sums(own):
        sums = jnp.sum(own * own, axis=(1, 2))
        return jnp.broadcast_to(jnp.pad(sums, (0, 8 - own.shape[0]))[:, None], (8, 128))

    attn_pieces, ffn_full_next, vector_all, ffn_squares = exchange(
        ("za2a", attn_sums.astype(bf16)),
        ("dprow", ffn_next_b),
        ("dpag", vector_terms),
        ("dpag", square_sums(ffn_next)),
    )
    attn_grads = jnp.sum(attn_pieces.astype(jnp.float32), axis=0, keepdims=True) / total_tokens
    attn_next = momentum_rate * attn_momenta + attn_grads
    gram_part = jnp.concatenate(
        [mm(ffn_next_b[0], ffn_full_next[0], NT), mm(ffn_next_b[1], ffn_full_next[1], NT)]
    )
    piece = 2 * own_count // group_count
    attn_full_next, gram_pieces, attn_squares, ffn_squares, vector_groups = exchange(
        ("dprow", attn_next.astype(bf16)),
        ("za2a", gram_part.astype(bf16).reshape(group_count, piece, width)),
        ("dpag", square_sums(attn_next)),
        ("zag", jnp.sum(ffn_squares, axis=0)),
        ("zag", jnp.sum(vector_all, axis=0)),
    )
    gram_piece = jnp.sum(gram_pieces.astype(jnp.float32), axis=0).astype(bf16)
    (gram_full,) = exchange((("chain", 2), gram_piece))
    attn_square = jnp.sum(attn_squares, axis=0)[:1, 0]
    ffn_square = jnp.sum(ffn_squares, axis=0)[:2, 0]
    scales = 1.0 / (jnp.sqrt(jnp.concatenate([attn_square, ffn_square])) + 1e-07)
    new_weights = newton_schulz(
        scales,
        dp_index * own_count,
        attn_full_next[0],
        ffn_full_next,
        gram_full,
        jnp.concatenate([attn_next, ffn_next], axis=0),
        jnp.concatenate([attn_weights, ffn_weights], axis=0),
    )
    new_attn_weights = new_weights[:1]
    new_ffn_weights = new_weights[1:]
    vector_grads = jnp.sum(vector_groups, axis=0) / total_tokens
    new_vector_momenta = momentum_rate * vector_momenta + vector_grads
    mean_square = jnp.mean(new_vector_momenta * new_vector_momenta, axis=1, keepdims=True)
    new_vectors = vectors - vector_rate * new_vector_momenta * lax.rsqrt(mean_square + 1e-06)
    return (
        outputs,
        input_grad,
        attn_grads,
        ffn_grads,
        vector_grads,
        new_attn_weights,
        attn_next,
        new_ffn_weights,
        ffn_next,
        new_vectors,
        new_vector_momenta,
    )


def solution(mesh):
    in_specs = (
        P(("dp", "group"), None),
        P(("dp", "group"), None),
        P(("dp", "group"), None),
        P("group", "dp", None),
        P("group", "dp", None),
        P(None, "dp", "group"),
        P(None, "dp", "group"),
        P(),
        P(),
    )
    out_specs = (
        P(("dp", "group"), None),
        P(("dp", "group"), None),
        P("group", "dp", None),
        P(None, "dp", "group"),
        P(),
        P("group", "dp", None),
        P("group", "dp", None),
        P(None, "dp", "group"),
        P(None, "dp", "group"),
        P(),
        P(),
    )
    return jax.shard_map(
        on_device, mesh=mesh, in_specs=in_specs, out_specs=out_specs, check_vma=False
    )
```
